32 devices in a mesh: tensor: 4 (over y, x), expert: 8 (over z, core).
Axes of the slice: x: 2, y: 2, z: 4, core: 2. Of those that a mesh axis runs over, the one named last changes fastest.
Arguments:
- tokens: bfloat16 [16, 1024, 768], P('expert', 'tensor'), may hold values from -6 to 6
- out_grad: bfloat16 [16, 1024, 768], P('expert', 'tensor'), may hold values from -6 to 6
- masked: int32 [16, 1024], P('expert', 'tensor'), may hold values from 0 to 1, as said below
- route: int32 [16, 1024, 1], P('expert', 'tensor'), may hold values from 0 to 3
- norm1_gain: float32 [768], replicated, may hold values from 0.5 to 1.5
- query_key_value_weight: bfloat16 [3, 768, 768], P(None, None, 'tensor'), may hold values from -0.625 to 0.625
- output_weight: bfloat16 [768, 768], P('tensor'), may hold values from -5 to 5
- norm2_gain: float32 [768], replicated, may hold values from 0.5 to 1.5
- route_weight: float32 [768, 16], replicated, may hold values from -0.21875 to 0.21875
- expert_embed: float32 [4, 16], replicated, may hold values from -6 to 6
- up_weight: bfloat16 [8, 768, 1536], P('expert'), may hold values from -0.21875 to 0.21875
- down_weight: bfloat16 [8, 768, 1536], P('expert'), may hold values from -1 to 1
Outputs:
- out: float32 [16, 1024, 768], P('expert', 'tensor')
- input_grad: float32 [16, 1024, 768], P('expert', 'tensor')
- loads: float32 [4], replicated
- norm1_grad: float32 [768], replicated
- query_key_value_gradient: float32 [3, 768, 768], P(None, None, 'tensor')
- out_proj_grad: float32 [768, 768], P('tensor')
- norm2_grad: float32 [768], replicated
- route_weight_grad: float32 [768, 16], replicated
- embed_grad: float32 [4, 16], replicated
- up_weight_grad: float32 [8, 768, 1536], P('expert', None, 'tensor')
- down_weight_grad: float32 [8, 768, 1536], P('expert', None, 'tensor')
The draws below stay inside these ranges and needn't reach their ends.
Inputs may be any that keep to these rules, and one draw needn't show every extreme that they name: 1 marks a masked position; only these carry a gradient. Every expert is the route of some token.
All inputs are finite; a program needn't handle non-finite values.
Results may differ from the reference program's by a relative error of at most 0.015.
The reference program's roundings to bfloat16 on the way count: a program that leaves them out, or rounds other values in their place, can miss the bound.
Values may be sent and summed in bfloat16 or wider, within the bound.
No kernel may reach another device: no remote copies, remote signals or barrier semaphores. Data moves between devices by JAX's collectives and lax.ppermute only.
A program may use at most 192 MiB of HBM per device.

```python
from functools import partial
import jax
import jax.numpy as jnp
from jax import lax

D = 768
HEADS = 12
HEAD = 64
FF = 3072
RDIM = 16
LEN = 1024
SEQ_DEV = 2
EXPERTS = 4
SEQS = 16
CAP = 128
N_TENSOR = 4
N_EXPERT = 8


def draw_masked(key, part):
    rate_key, coin_key = jax.random.split(key)
    rates = jax.random.randint(rate_key, (SEQS, 1), 51, 257)
    coins = jax.random.randint(coin_key, (SEQS, LEN), 0, 1024)
    return (coins < rates).astype(jnp.int32)


def level_of(own_key, shape, pieces, smallest, top_value):
    level, own = 1.0, jax.random.fold_in(own_key, 6)
    for dim, parts in pieces:
        draws = jnp.exp(jax.random.uniform(jax.random.fold_in(own, dim), (parts,), jnp.float32, smallest / len(pieces), top_value / len(pieces)))
        level = level * jnp.repeat(draws, shape[dim] // parts).reshape([-1 if axis == dim else 1 for axis in range(len(shape))])
    return level


def distinct(key, rows, number_of, top, lift):
    sequence = jax.random.permutation(jax.random.fold_in(key, 1), number_of)
    pull = sequence
    for power in range(3):
        pull = pull * pull // number_of
    pull = pull * lift // number_of
    lots = jax.random.randint(jax.random.fold_in(key, 2), (rows, number_of), 0, 4096) + pull
    sure = jax.random.permutation(jax.random.fold_in(key, 3), rows)[jnp.arange(number_of) % rows]
    lots = jnp.where(jnp.arange(rows)[:, None] == sure[None, :], 1 << 14, lots)
    score = lots * number_of + jnp.arange(number_of)
    return lax.top_k(score.astype(jnp.int32), top)[1].astype(jnp.int32)


def centred(key, dims, scale, reach, pieces=(), held_as=jnp.bfloat16):
    array = jax.random.normal(key, dims, jnp.float32) * scale
    if len(pieces) > 0:
        array = level_of(key, dims, pieces, -0.22, 0.18) * array
    return jnp.clip(array, min=-reach, max=reach).astype(held_as)


def setup_inputs(seed: int = 0) -> dict:
    streams_of = jax.random.split(jax.random.key(seed), 13)
    tokens = centred(streams_of[0], (SEQS, LEN, D), 1.0, 6.0, ((0, 8), (1, 4)))
    out_grad = centred(streams_of[1], (SEQS, LEN, D), 1.0, 6.0, ((0, 8), (1, 4)))
    masked = draw_masked(jax.random.fold_in(streams_of[12], 71), 0)
    route = distinct(streams_of[3], SEQS * LEN, EXPERTS, 1, 2048).reshape((SEQS, LEN, 1))
    norm1_gain = jnp.clip(1.0 + 0.1 * jax.random.normal(streams_of[4], (D,), jnp.float32), 0.5, 1.5)
    query_key_value_weight = centred(streams_of[5], (3, D, HEADS * HEAD), (1.2 / D ** 0.5), 0.625, ((2, 4),))
    output_weight = centred(streams_of[6], (HEADS * HEAD, D), (10 / D ** 0.5), 5.0, ((0, 4),))
    norm2_gain = jnp.clip(1.0 + 0.1 * jax.random.normal(streams_of[7], (D,), jnp.float32), 0.5, 1.5)
    route_weight = centred(streams_of[8], (D, RDIM), D ** -0.5, 0.21875, (), jnp.float32)
    expert_embed = centred(streams_of[9], (EXPERTS, RDIM), 1.0, 6.0, (), jnp.float32)
    up_weight = centred(streams_of[10], (2 * EXPERTS, D, FF // 2), D ** -0.5, 0.21875, ((0, 8),))
    down_weight = centred(streams_of[11], (2 * EXPERTS, D, FF // 2), (EXPERTS / FF ** 0.5), 1.0, ((0, 8),))
    return {"tokens": tokens, "out_grad": out_grad, "masked": masked, "route": route, "norm1_gain": norm1_gain, "query_key_value_weight": query_key_value_weight, "output_weight": output_weight, "norm2_gain": norm2_gain, "route_weight": route_weight, "expert_embed": expert_embed, "up_weight": up_weight, "down_weight": down_weight}


@jax.custom_vjp
def low(v):
    return lax.optimization_barrier(v.astype(jnp.bfloat16)).astype(jnp.float32)

@jax.custom_vjp
def low_back(v):
    return v

def low_keep(v):
    return (low(v), None)

def low_pass(kept, grad):
    return (grad,)

def back_keep(v):
    return (v, None)

def back_low(kept, grad):
    return (low(grad),)
low.defvjp(low_keep, low_pass)
low_back.defvjp(back_keep, back_low)

def layer_norm(values, gain):
    center = values - lax.optimization_barrier(jnp.mean(values, axis=-1, keepdims=True))
    spread = lax.optimization_barrier(jnp.mean(center * center, axis=-1, keepdims=True))
    return center * lax.rsqrt(spread + 1e-05) * gain

def unit_rows(values):
    return values * lax.rsqrt(lax.optimization_barrier(jnp.sum(values * values, axis=-1, keepdims=True)) + 1e-06)

def join_halves(values):
    return values.reshape(EXPERTS, 2, D, FF // 2).transpose(0, 2, 1, 3).reshape(EXPERTS, D, FF)

def attend_sequence(normed, qkv_w, out_w):
    projected = jnp.einsum('ld,kdh->klh', normed, qkv_w, precision=lax.Precision.HIGHEST)
    projected = low_back(low(projected))
    heads_view = projected.reshape(3, LEN, HEADS, HEAD)
    scores = jnp.einsum('qhe,khe->hqk', heads_view[0], heads_view[1], precision=lax.Precision.HIGHEST) * HEAD ** (-0.5)
    scores = low_back(scores)
    probs = jax.nn.softmax(scores, axis=-1)
    mixed = jnp.einsum('hqk,khe->qhe', low(probs), heads_view[2], precision=lax.Precision.HIGHEST)
    mixed = low_back(low(mixed)).reshape(LEN, HEADS * HEAD)
    return jnp.dot(mixed, out_w, precision=lax.Precision.HIGHEST)

def expert_ffn(operands):
    rows, up_w, down_w = operands
    up = low_back(jnp.dot(rows, up_w, precision=lax.Precision.HIGHEST))
    active = low(jax.nn.gelu(up, approximate=False))
    returned = jnp.dot(active, down_w.T, precision=lax.Precision.HIGHEST)
    return low_back(low(returned))

def reference(tokens, out_grad, masked, route, norm1_gain, query_key_value_weight, output_weight, norm2_gain, route_weight, expert_embed, up_weight, down_weight):
    shard_len = LEN // N_TENSOR
    groups = N_EXPERT * N_TENSOR
    group_rows = SEQ_DEV * shard_len
    picks = route[..., 0]
    expert_ids = jnp.arange(EXPERTS, dtype=jnp.int32)
    grouped_picks = picks.reshape(N_EXPERT, SEQ_DEV, N_TENSOR, shard_len).transpose(0, 2, 1, 3).reshape(groups, group_rows)
    member = (grouped_picks[..., None] == expert_ids).astype(jnp.int32)
    earlier = jnp.cumsum(member, axis=1) - member
    slot_ids = lax.optimization_barrier(jnp.sum(earlier * member, axis=-1))
    target = jnp.where(slot_ids < CAP, grouped_picks * CAP + slot_ids, EXPERTS * CAP).astype(jnp.int32)
    group_index = jnp.arange(groups, dtype=jnp.int32)[:, None]
    picked = (picks[..., None] == expert_ids).astype(jnp.float32)
    loads = lax.optimization_barrier(jnp.sum(picked, axis=(0, 1)))

    def forward(inputs, gain_one, qkv_w, out_w, gain_two, route_w, embed, up_w, down_w):
        normed = low(layer_norm(inputs, gain_one))
        attn = lax.map(jax.checkpoint(partial(attend_sequence, qkv_w=qkv_w, out_w=out_w)), normed)
        hidden = inputs + low_back(attn)
        normed_two = layer_norm(hidden, gain_two)
        rows = unit_rows(jnp.dot(normed_two, route_w, precision=lax.Precision.HIGHEST))
        centers = unit_rows(embed)
        logits = 3.0 * jnp.dot(rows, centers.T, precision=lax.Precision.HIGHEST)
        gate = lax.optimization_barrier(jnp.sum(jax.nn.softmax(logits, axis=-1) * picked, axis=-1))
        sent = low_back(low(normed_two))
        sent_groups = sent.reshape(N_EXPERT, SEQ_DEV, N_TENSOR, shard_len, D).transpose(0, 2, 1, 3, 4).reshape(groups, group_rows, D)
        buffer = jnp.zeros((groups, EXPERTS * CAP + 1, D), jnp.float32).at[group_index, target].add(sent_groups)
        slots = buffer[:, :EXPERTS * CAP].reshape(groups, EXPERTS, CAP, D).transpose(1, 0, 2, 3).reshape(EXPERTS, groups * CAP, D)
        returned = lax.map(jax.checkpoint(expert_ffn), (slots, join_halves(up_w), join_halves(down_w)))
        back = returned.reshape(EXPERTS, groups, CAP, D).transpose(1, 0, 2, 3).reshape(groups, EXPERTS * CAP, D)
        back = jnp.concatenate([back, jnp.zeros((groups, 1, D), jnp.float32)], axis=1)
        taken = back[group_index, target]
        mixture = taken.reshape(N_EXPERT, N_TENSOR, SEQ_DEV, shard_len, D).transpose(0, 2, 1, 3, 4).reshape(SEQS, LEN, D)
        return hidden + gate[..., None] * mixture
    params = (tokens.astype(jnp.float32), norm1_gain, query_key_value_weight.astype(jnp.float32), output_weight.astype(jnp.float32), norm2_gain, route_weight, expert_embed, up_weight.astype(jnp.float32), down_weight.astype(jnp.float32))
    result, pullback = jax.vjp(forward, *params)
    cotangent = out_grad.astype(jnp.float32) * masked.astype(jnp.float32)[..., None]
    grads = pullback(cotangent)
    return (result, grads[0], loads, grads[1], grads[2], grads[3], grads[4], grads[5], grads[6], grads[7], grads[8])
```

```python
from functools import partial

import jax
import jax.numpy as jnp
from jax import lax
from jax.sharding import PartitionSpec as P

HEAD = 64
F32 = jnp.float32
BF16 = jnp.bfloat16


def layer_norm(values, gain):
    center = values - jnp.mean(values, axis=-1, keepdims=True)
    spread = jnp.mean(center * center, axis=-1, keepdims=True)
    return center * lax.rsqrt(spread + 1e-05) * gain


def unit_rows(values):
    return values * lax.rsqrt(jnp.sum(values * values, axis=-1, keepdims=True) + 1e-06)


def gelu_exact(values):
    return jax.nn.gelu(values, approximate=False)


def route_gate(normed, route_weight, expert_embed, picked):
    rows = unit_rows(jnp.dot(normed, route_weight, precision=lax.Precision.HIGHEST))
    centers = unit_rows(expert_embed)
    logits = 3.0 * jnp.dot(rows, centers.T, precision=lax.Precision.HIGHEST)
    probs = jax.nn.softmax(logits, axis=-1)
    return jnp.sum(probs * picked, axis=-1)


def three_parts(values):
    first = lax.reduce_precision(values, 8, 7)
    rest = values - first
    second = lax.reduce_precision(rest, 8, 7)
    third = rest - second
    return jnp.stack([first, second, third], axis=-2).astype(BF16)


def attach(rows, scalars):
    groups, cap, features = rows.shape
    extra = jnp.pad(three_parts(scalars), ((0, 0), (0, 5), (0, features - cap)))
    return jnp.concatenate([rows, extra], axis=1)


def detach(packed):
    cap = packed.shape[1] - 8
    return packed[:, :cap], jnp.sum(packed[:, cap : cap + 3, :cap].astype(F32), axis=1)


def attend_forward(query, key_all, value_all, score_scale):
    scores = (
        jnp.einsum("bhe,khe->hbk", query, key_all, preferred_element_type=jnp.float32) * score_scale
    )
    top = jnp.max(scores, axis=-1, keepdims=True)
    expos = jnp.exp(scores - top)
    total = jnp.sum(expos, axis=-1, keepdims=True)
    probs = (expos / total).astype(jnp.bfloat16)
    mixed = jnp.einsum("hbk,khe->bhe", probs, value_all, preferred_element_type=jnp.float32)
    return (mixed.astype(jnp.bfloat16), (top + jnp.log(total))[..., 0])


def attend_backward(query, key_all, value_all, grad_mixed, log_total, score_scale):
    scores = (
        jnp.einsum("bhe,khe->hbk", query, key_all, preferred_element_type=jnp.float32) * score_scale
    )
    probs = jnp.exp(scores - log_total[..., None])
    probs_low = probs.astype(jnp.bfloat16)
    grad_probs = jnp.einsum(
        "bhe,khe->hbk", grad_mixed, value_all, preferred_element_type=jnp.float32
    )
    inner = jnp.sum(probs * grad_probs, axis=-1, keepdims=True)
    grad_scores = (probs * (grad_probs - inner)).astype(jnp.bfloat16)
    query_part = (
        jnp.einsum("hbk,khe->bhe", grad_scores, key_all, preferred_element_type=jnp.float32)
        * score_scale
    )
    key_part = (
        jnp.einsum("hbk,bhe->khe", grad_scores, query, preferred_element_type=jnp.float32)
        * score_scale
    )
    value_part = jnp.einsum(
        "hbk,bhe->khe", probs_low, grad_mixed, preferred_element_type=jnp.float32
    )
    return (query_part, key_part, value_part)


def dot_nt(left, right):
    return lax.dot_general(left, right, (((1,), (1,)), ((), ())), preferred_element_type=F32)


def dot_tn(left, right):
    return lax.dot_general(left, right, (((0,), (0,)), ((), ())), preferred_element_type=F32)


def dot_nn(left, right):
    return jnp.dot(left, right, preferred_element_type=F32)


def program(tensor_size, expert_size):
    chips = expert_size // 2
    bits = chips.bit_length() - 1

    def over_tensor(values, mask):
        return lax.ppermute(values, "tensor", [(i, i ^ mask) for i in range(tensor_size)])

    def over_core(values):
        return lax.ppermute(values, "expert", [(i, i ^ 1) for i in range(expert_size)])

    def over_chip(values, mask):
        return lax.ppermute(values, "expert", [(i, i ^ (2 * mask)) for i in range(expert_size)])

    def swap_chips(blocks):
        if chips <= 4:
            return jnp.concatenate(
                [blocks[:1]] + [over_chip(blocks[m : m + 1], m) for m in range(1, chips)], axis=0
            )
        chip = lax.axis_index("expert") // 2
        order = chip ^ jnp.arange(chips)
        groups = [[2 * i + core for i in range(chips)] for core in range(2)]
        moved = lax.all_to_all(
            blocks[order], "expert", split_axis=0, concat_axis=0, tiled=True, axis_index_groups=groups
        )
        return moved[order]

    if chips == 4:
        masks = (1, 3)
    else:
        masks = tuple(1 << bit for bit in range(bits))

    def chip_bit(level):
        chip = lax.axis_index("expert") // 2
        if chips == 4:
            return ((chip ^ (chip >> 1)) & 1) if level == 0 else (chip >> 1) & 1
        return (chip >> level) & 1

    def halves(values, bit):
        half = values.shape[0] // 2
        low, high = values[:half], values[half:]
        return jnp.where(bit == 0, low, high), jnp.where(bit == 0, high, low)

    def joined(mine, theirs, bit):
        return jnp.concatenate(
            [jnp.where(bit == 0, mine, theirs), jnp.where(bit == 0, theirs, mine)], axis=0
        )

    def total_everywhere(values):
        for mask in (1, 2):
            values = values + over_tensor(values, mask)
        values = values + over_core(values)
        for mask in masks:
            values = values + over_chip(values, mask)
        return values

    def total_over_chips(values):
        for level, mask in enumerate(masks):
            keep, send = halves(values, chip_bit(level))
            values = keep + over_chip(send.astype(BF16), mask).astype(F32)
        low = values.astype(BF16)
        for level in reversed(range(bits)):
            low = joined(low, over_chip(low, masks[level]), chip_bit(level))
        return low

    def body(
        tokens,
        out_grad,
        masked,
        route,
        norm1_gain,
        query_key_value_weight,
        output_weight,
        norm2_gain,
        route_weight,
        expert_embed,
        up_weight,
        down_weight,
    ):
        seq_count, shard_len, features = tokens.shape
        rows_here = seq_count * shard_len
        experts = expert_embed.shape[0]
        capacity = rows_here // experts
        channels = query_key_value_weight.shape[2]
        head_count = channels // HEAD
        score_scale = HEAD ** (-0.5)
        me = lax.axis_index("tensor")
        place = lax.axis_index("expert")
        chip, core = place // 2, place % 2

        gathered = [
            jnp.concatenate(
                [tokens[s]] + [over_tensor(tokens[s], m) for m in range(1, tensor_size)], axis=0
            )
            for s in range(seq_count)
        ]
        seq_len = gathered[0].shape[0]
        block = min(512, seq_len)

        picks = route.reshape(rows_here)
        expert_ids = jnp.arange(experts, dtype=jnp.int32)
        member = (picks[:, None] == expert_ids[None, :]).astype(jnp.int32)
        earlier = jnp.cumsum(member, axis=0) - member
        slot_ids = jnp.sum(earlier * member, axis=1)
        target = (picks ^ chip) * capacity + slot_ids
        slot_range = jnp.arange(experts * capacity, dtype=jnp.int32)
        placing = ((slot_range[:, None] == target[None, :]) & (slot_ids < capacity)[None, :]).astype(
            BF16
        )
        cotangent = out_grad.reshape(rows_here, features) * masked.reshape(rows_here, 1).astype(BF16)
        sent_cotangent = dot_nn(placing, cotangent).astype(BF16)
        slot_cotangent = swap_chips(sent_cotangent.reshape(experts, capacity, features)).reshape(
            rows_here, features
        )

        out_weight_all = jnp.concatenate(
            [output_weight] + [over_tensor(output_weight, m) for m in range(1, tensor_size)], axis=0
        )
        qkv_rows = query_key_value_weight.transpose(0, 2, 1).reshape(3 * channels, features)
        qkv_rows_all = jnp.concatenate(
            [qkv_rows] + [over_tensor(qkv_rows, m) for m in range(1, tensor_size)], axis=0
        )
        up_all = jnp.concatenate([up_weight[0], over_core(up_weight[0])], axis=1)
        down_all = jnp.concatenate([down_weight[0], over_core(down_weight[0])], axis=1)
        hidden_units = up_weight.shape[2]

        inputs = tokens.astype(F32).reshape(rows_here, features)
        normed_own, norm_one_pull = jax.vjp(layer_norm, inputs, norm1_gain)
        normed_rows = []
        views = []
        mixed_parts = []
        totals = []
        for s in range(seq_count):
            normed_low = layer_norm(gathered[s].astype(F32), norm1_gain).astype(BF16)
            normed_rows.append(normed_low)
            projected = (
                jnp.einsum("xa,cam->cxm", normed_low, query_key_value_weight, preferred_element_type=F32)
                .astype(BF16)
                .reshape(3, seq_len, head_count, HEAD)
            )
            views.append(projected)
            mixed_blocks = []
            total_blocks = []
            for start_row in range(0, seq_len, block):
                mixed_blk, total_blk = attend_forward(
                    projected[0, start_row : start_row + block], projected[1], projected[2], score_scale
                )
                mixed_blocks.append(mixed_blk)
                total_blocks.append(total_blk)
            totals.append(jnp.concatenate(total_blocks, axis=1))
            mixed = jnp.concatenate(mixed_blocks, axis=0).reshape(tensor_size, shard_len, channels)
            mixed_parts.append(
                jnp.concatenate(
                    [mixed[0]] + [over_tensor(mixed[m], m) for m in range(1, tensor_size)], axis=1
                )
            )
        mixed_own = jnp.concatenate(mixed_parts, axis=0)
        hidden = inputs + dot_nn(mixed_own, out_weight_all)
        normed_two, norm_two_pull = jax.vjp(layer_norm, hidden, norm2_gain)
        gate, gate_pull = jax.vjp(
            partial(route_gate, picked=member.astype(F32)), normed_two, route_weight, expert_embed
        )
        sent = dot_nn(placing, normed_two.astype(BF16)).astype(BF16)
        sent_gate = jnp.sum(placing.astype(F32) * gate[None, :], axis=1)
        slot_rows, slot_gate = detach(
            swap_chips(
                attach(
                    sent.reshape(experts, capacity, features), sent_gate.reshape(experts, capacity)
                )
            )
        )
        slot_rows = slot_rows.reshape(rows_here, features)

        up = dot_nn(slot_rows, up_all)
        active, act_pull = jax.vjp(gelu_exact, up)
        active_low = active.astype(BF16)
        returned = dot_nt(active_low, down_all).astype(BF16)
        grad_returned = (slot_gate.reshape(rows_here, 1) * slot_cotangent.astype(F32)).astype(BF16)
        slot_grad_gate = jnp.sum(slot_cotangent.astype(F32) * returned.astype(F32), axis=1)
        grad_up = act_pull(dot_nn(grad_returned, down_all))[0].astype(BF16)
        grad_slots = dot_nt(grad_up, up_all).astype(BF16)
        back_grad, back_grad_gate = detach(
            swap_chips(
                attach(
                    grad_slots.reshape(experts, capacity, features),
                    slot_grad_gate.reshape(experts, capacity),
                )
            )
        )
        back = swap_chips(returned.reshape(experts, capacity, features))

        def weight_grad(left, right):
            full = dot_tn(left, right)
            kept = full[:, :hidden_units] + over_core(full[:, hidden_units:].astype(BF16)).astype(F32)
            width = hidden_units // tensor_size
            total = lax.dynamic_slice_in_dim(kept, me * width, width, axis=1)
            for m in range(1, tensor_size):
                part = lax.dynamic_slice_in_dim(kept, (me ^ m) * width, width, axis=1)
                total = total + over_tensor(part.astype(BF16), m).astype(F32)
            return total[None]

        up_weight_grad = weight_grad(slot_rows, grad_up)
        down_weight_grad = weight_grad(grad_returned, active_low)

        mixture = dot_tn(placing, back.reshape(rows_here, features))
        result = hidden + gate[:, None] * mixture

        grad_gate = jnp.sum(placing.astype(F32) * back_grad_gate.reshape(rows_here, 1), axis=0)
        grad_normed = dot_tn(placing, back_grad.reshape(rows_here, features))
        grad_from_gate, route_weight_grad, embed_grad = gate_pull(grad_gate)
        grad_hidden_norm, norm2_grad = norm_two_pull(grad_normed + grad_from_gate)
        grad_hidden = cotangent.astype(F32) + grad_hidden_norm
        grad_attn = grad_hidden.astype(BF16)
        grad_mixed_own = dot_nt(grad_attn, out_weight_all).astype(BF16)
        grad_mixed_own = grad_mixed_own.reshape(seq_count, shard_len, tensor_size, channels)

        out_local = dot_tn(mixed_own, grad_attn).reshape(tensor_size, 2, channels // 2, features)
        out_keep = jnp.where(core == 0, out_local[:, 0], out_local[:, 1])
        out_send = jnp.where(core == 0, out_local[:, 1], out_local[:, 0])
        out_keep = out_keep + over_core(out_send.astype(BF16)).astype(F32)
        out_part = out_keep[0]
        for m in range(1, tensor_size):
            out_part = out_part + over_tensor(out_keep[m].astype(BF16), m).astype(F32)

        grad_inputs_parts = []
        weight_part = jnp.zeros((3 * channels, features), F32)
        for s in range(seq_count):
            grad_mixed = jnp.concatenate(
                [grad_mixed_own[s, :, 0]]
                + [over_tensor(grad_mixed_own[s, :, m], m) for m in range(1, tensor_size)],
                axis=0,
            ).reshape(seq_len, head_count, HEAD)
            key_all = views[s][1]
            value_all = views[s][2]
            grad_key = jnp.zeros((seq_len, head_count, HEAD), F32)
            grad_value = jnp.zeros((seq_len, head_count, HEAD), F32)
            query_grads = []
            for start_row in range(0, seq_len, block):
                query_part, key_part, value_part = attend_backward(
                    views[s][0, start_row : start_row + block],
                    key_all,
                    value_all,
                    grad_mixed[start_row : start_row + block],
                    totals[s][:, start_row : start_row + block],
                    score_scale,
                )
                query_grads.append(query_part)
                grad_key = grad_key + key_part
                grad_value = grad_value + value_part
            grad_qkv = jnp.concatenate(
                [
                    g.astype(BF16).reshape(seq_len, channels)
                    for g in (jnp.concatenate(query_grads, axis=0), grad_key, grad_value)
                ],
                axis=1,
            )
            weight_part = weight_part + dot_tn(grad_qkv, normed_rows[s])
            blocks = grad_qkv.reshape(tensor_size, shard_len, 3 * channels)
            grad_inputs_parts.append(
                jnp.concatenate(
                    [blocks[0]] + [over_tensor(blocks[m], m) for m in range(1, tensor_size)], axis=1
                )
            )
        grad_normed_one = dot_nn(jnp.concatenate(grad_inputs_parts, axis=0), qkv_rows_all)
        grad_inputs_norm, norm1_grad = norm_one_pull(grad_normed_one)
        input_grad = grad_hidden + grad_inputs_norm

        qkv_keep, qkv_send = halves(weight_part, core)
        qkv_keep = qkv_keep + over_core(qkv_send.astype(BF16)).astype(F32)
        summed = total_over_chips(jnp.concatenate([qkv_keep, out_part], axis=0))
        other = over_core(summed)
        split = 3 * channels // 2
        query_key_value_gradient = (
            joined(summed[:split], other[:split], core)
            .reshape(3, channels, features)
            .transpose(0, 2, 1)
            .astype(F32)
        )
        out_proj_grad = joined(summed[split:], other[split:], core).astype(F32)

        loads_local = jnp.sum(member, axis=0).astype(F32)
        small = (loads_local, norm2_grad, route_weight_grad, embed_grad, norm1_grad)
        flat = jnp.concatenate([part.reshape(-1) for part in small])
        width = flat.shape[0]
        flat = jnp.pad(flat, (0, -width % 1024)).reshape(-1, 128)
        flat = total_everywhere(flat).reshape(-1)
        found = []
        start = 0
        for part in small:
            found.append(flat[start : start + part.size].reshape(part.shape))
            start += part.size
        loads, norm2_grad, route_weight_grad, embed_grad, norm1_grad = found
        return (
            result.reshape(seq_count, shard_len, features),
            input_grad.reshape(seq_count, shard_len, features),
            loads,
            norm1_grad,
            query_key_value_gradient,
            out_proj_grad,
            norm2_grad,
            route_weight_grad,
            embed_grad,
            up_weight_grad,
            down_weight_grad,
        )

    return body


def solution(mesh):
    return jax.shard_map(
        program(mesh.shape["tensor"], mesh.shape["expert"]),
        mesh=mesh,
        in_specs=(
            P("expert", "tensor", None),
            P("expert", "tensor", None),
            P("expert", "tensor"),
            P("expert", "tensor", None),
            P(),
            P(None, None, "tensor"),
            P("tensor", None),
            P(),
            P(),
            P(),
            P("expert", None, None),
            P("expert", None, None),
        ),
        out_specs=(
            P("expert", "tensor", None),
            P("expert", "tensor", None),
            P(),
            P(),
            P(None, None, "tensor"),
            P("tensor", None),
            P(),
            P(),
            P(),
            P("expert", None, "tensor"),
            P("expert", None, "tensor"),
        ),
        check_vma=False,
    )
```

```python
import functools

import jax
import jax.numpy as jnp
from jax import lax
from jax.experimental import pallas as pl
from jax.experimental.pallas import tpu as pltpu
from jax.sharding import PartitionSpec as P

HEAD = 64
F32 = jnp.float32
BF16 = jnp.bfloat16
LOG2E = 1.4426950408889634
SCALE = HEAD**-0.5
EXACT = lax.Precision.HIGHEST
SDS = jax.ShapeDtypeStruct
VMEM = pltpu.VMEM
COVER = 4

ERFC_SLOPE = 0.44
ERFC = (
    0.248227568,
    0.248777028,
    0.217859919,
    0.214130365,
    -0.0172025688,
    0.293641958,
    -0.276276279,
    0.0708421859,
)


def dot_nn(left, right, precision=None):
    return jnp.dot(left, right, preferred_element_type=F32, precision=precision)


def dot_nt(left, right, precision=None):
    return lax.dot_general(
        left, right, (((1,), (1,)), ((), ())), preferred_element_type=F32, precision=precision
    )


def dot_tn(left, right, precision=None):
    return lax.dot_general(
        left, right, (((0,), (0,)), ((), ())), preferred_element_type=F32, precision=precision
    )


class Far:
    def __init__(self, value, block=None, at=0):
        self.value = value
        self.block = value.shape if block is None else block
        self.at = at


def plain(value):
    return value.value if isinstance(value, Far) else value


def in_hbm(value):
    return pltpu.with_memory_space_constraint(value, pltpu.HBM)


def cost(flops, size, transcendentals=0, cover=COVER):
    return pl.CostEstimate(
        flops=flops * cover, bytes_accessed=size * cover, transcendentals=transcendentals * cover
    )


def call(kernel, outs, args, flops, scratch=(), limit=24, transcendentals=0, scalar=None):
    whole = pl.BlockSpec(memory_space=VMEM)

    def spec(arg):
        if not isinstance(arg, Far):
            return whole
        where = (arg.at,) + (0,) * (arg.value.ndim - 1)
        return pl.BlockSpec(
            arg.block, lambda i: where, pipeline_mode=pl.Buffered(buffer_count=1)
        )

    specs = [spec(a) for a in args]
    out_specs = [spec(o) for o in outs]
    size = sum(a.size * a.dtype.itemsize for a in map(plain, args))
    size += sum(o.size * o.dtype.itemsize for o in map(plain, outs))
    args = [in_hbm(a.value) if isinstance(a, Far) else a for a in args]
    outs = [pltpu.HBM(o.value.shape, o.value.dtype) if isinstance(o, Far) else o for o in outs]
    if scalar is not None:
        specs = [pl.BlockSpec(memory_space=pltpu.SMEM)] + specs
        args = [scalar.reshape(1)] + args
    return pl.pallas_call(
        kernel,
        grid=(1,),
        out_shape=list(outs),
        in_specs=specs,
        out_specs=out_specs,
        scratch_shapes=list(scratch),
        compiler_params=pltpu.CompilerParams(vmem_limit_bytes=limit << 20),
        cost_estimate=cost(flops, size, transcendentals),
    )(*args)


def centred(x):
    cen = x - jnp.mean(x, axis=1, keepdims=True)
    return cen, lax.rsqrt(jnp.mean(cen * cen, axis=1, keepdims=True) + 1e-05)


def tie(values, *after):
    return lax.optimization_barrier((values, after))[0]


def attend_kernel(parts, channels, riding, *refs):
    tok = refs[:parts]
    gain_ref, w_ref = refs[parts : parts + 2]
    rider = refs[parts + 2 : parts + 2 + riding]
    refs = refs[parts + 2 + riding :]
    normed_ref, qkv_ref, lse_ref = refs[:3]
    mixed = refs[3:]
    shard = tok[0].shape[0]
    for ref in rider:
        for b in range(parts):
            mixed[b][:, pl.ds(shard, ref.shape[1])] = ref[...]
    for b in range(parts):
        cen, inv = centred(tok[b][...].astype(F32))
        rows = (cen * inv * gain_ref[...]).astype(BF16)
        normed_ref[pl.ds(b * shard, shard), :] = rows
        qkv_ref[:, pl.ds(b * shard, shard)] = dot_nt(w_ref[...], rows).astype(BF16)

    def head(h, carry):
        off = pl.multiple_of(h * HEAD, HEAD)
        key = qkv_ref[pl.ds(channels + off, HEAD), :].T
        value_t = qkv_ref[pl.ds(2 * channels + off, HEAD), :]
        for b in range(parts):
            query_t = qkv_ref[pl.ds(off, HEAD), pl.ds(b * shard, shard)]
            scores = dot_nn(key, query_t)
            top = jnp.max(scores, axis=0, keepdims=True)
            expos = jnp.exp2((scores - top) * (SCALE * LOG2E))
            total = jnp.sum(expos, axis=0, keepdims=True)
            probs = (expos * (1.0 / total)).astype(BF16)
            mixed[b][pl.ds(off, HEAD), pl.ds(0, shard)] = dot_nn(value_t, probs).astype(BF16)
            lse_ref[pl.ds(h, 1), pl.ds(b * shard, shard)] = top * (SCALE * LOG2E) + jnp.log2(total)
        return carry

    lax.fori_loop(0, channels // HEAD, head, 0)


def attend(tok, gain, w_rows, *rider):
    parts = len(tok)
    shard, feat = tok[0].shape
    length = parts * shard
    channels = w_rows.shape[0] // 3
    outs = call(
        functools.partial(attend_kernel, parts, channels, len(rider)),
        [
            Far(SDS((length, feat), BF16)),
            Far(SDS((3 * channels, length), BF16)),
            Far(SDS((8, length), F32)),
        ]
        + [SDS((channels, shard + sum(r.shape[1] for r in rider)), BF16)] * parts,
        [*tok, gain, Far(w_rows), *[Far(r) for r in rider]],
        2 * length * feat * 3 * channels + 4 * length * length * channels,
        transcendentals=length * length * channels // HEAD,
    )
    return outs[0], outs[1], outs[2], outs[3:]


def attend_back_kernel(parts, channels, at, *refs):
    qkv_ref, lse_ref = refs[:2]
    shard = qkv_ref.shape[1] // parts
    grad = [ref.at[:, pl.ds(at * shard, shard)] for ref in refs[2 : 2 + parts]]
    refs = refs[2 + parts :]
    outs = refs[:parts]
    key_acc, value_acc = refs[parts:]

    def head(h, carry):
        off = pl.multiple_of(h * HEAD, HEAD)
        key_t = qkv_ref[pl.ds(channels + off, HEAD), :]
        key = key_t.T
        value = qkv_ref[pl.ds(2 * channels + off, HEAD), :].T
        for b in range(parts):
            query_t = qkv_ref[pl.ds(off, HEAD), pl.ds(b * shard, shard)]
            grad_t = grad[b][pl.ds(off, HEAD), :]
            scores = dot_nn(key, query_t)
            probs = jnp.exp2(
                scores * (SCALE * LOG2E) - lse_ref[pl.ds(h, 1), pl.ds(b * shard, shard)]
            )
            grad_probs = dot_nn(value, grad_t)
            inner = jnp.sum(probs * grad_probs, axis=0, keepdims=True)
            grad_scores = (probs * (grad_probs - inner)).astype(BF16)
            value_part = dot_nt(grad_t, probs.astype(BF16))
            key_part = dot_nt(query_t, grad_scores)
            outs[b][pl.ds(off, HEAD), :] = (dot_nn(key_t, grad_scores) * SCALE).astype(BF16)
            if b == 0:
                key_acc[...] = key_part
                value_acc[...] = value_part
            else:
                key_acc[...] += key_part
                value_acc[...] += value_part
        for b in range(parts):
            cols = pl.ds(b * shard, shard)
            outs[b][pl.ds(channels + off, HEAD), :] = (key_acc[:, cols] * SCALE).astype(BF16)
            outs[b][pl.ds(2 * channels + off, HEAD), :] = value_acc[:, cols].astype(BF16)
        return carry

    lax.fori_loop(0, channels // HEAD, head, 0)


def attend_back(qkv, lse, grad, at):
    parts = len(grad)
    channels = grad[0].shape[0]
    length = qkv.shape[1]
    shard = length // parts
    return call(
        functools.partial(attend_back_kernel, parts, channels, at),
        [SDS((3 * channels, shard), BF16)] * parts,
        [Far(qkv), Far(lse), *[Far(g) for g in grad]],
        10 * length * length * channels,
        scratch=[VMEM((HEAD, length), F32)] * 2,
        transcendentals=length * length * channels // HEAD,
    )


def gate_parts(normed, route_t, embed, member):
    raw = dot_nt(route_t, normed, EXACT)
    inv = lax.rsqrt(jnp.sum(raw * raw, axis=0, keepdims=True) + 1e-06)
    rows = raw * inv
    embed_inv = lax.rsqrt(jnp.sum(embed * embed, axis=1, keepdims=True) + 1e-06)
    centers = embed * embed_inv
    logits = 3.0 * dot_nn(centers, rows, EXACT)
    expos = jnp.exp(logits - jnp.max(logits, axis=0, keepdims=True))
    probs = expos / jnp.sum(expos, axis=0, keepdims=True)
    gate = jnp.sum(probs * member, axis=0, keepdims=True)
    return raw, inv, rows, embed_inv, centers, probs, gate


def split_rows(row):
    first = row.astype(BF16).astype(F32)
    second = (row - first).astype(BF16).astype(F32)
    third = (row - first) - second
    shape = (8, row.shape[1])
    at = lax.broadcasted_iota(jnp.int32, shape, 0)
    parts = jnp.where(at == 0, first, jnp.where(at == 1, second, jnp.where(at == 2, third, 0.0)))
    return parts.astype(BF16)


def middle_kernel(seqs, parts, groups, *refs):
    refs = list(refs)
    take = lambda n: [refs.pop(0) for _ in range(n)]
    (tok_ref,) = take(1)
    mixed = [take(parts) for _ in range(seqs)]
    gain_ref, route_ref, embed_ref, member_ref, place_ref = take(5)
    hidden_ref, gate_ref = take(2)
    cap = place_ref.shape[0] // groups
    packed = []
    while refs:
        (ref,) = take(1)
        packed += [ref.at[pl.ds(g, cap + 8), :] for g in range(0, ref.shape[0], cap + 8)]
    shard = tok_ref.shape[0] // seqs
    weight = [ref.at[:, pl.ds(shard, tok_ref.shape[1])] for ref in mixed[0]]
    mixed[0] = [ref.at[:, pl.ds(0, shard)] for ref in mixed[0]]
    for s in range(seqs):
        total = tok_ref[pl.ds(s * shard, shard), :].astype(F32)
        attn = dot_tn(mixed[s][0][...], weight[0][...])
        for m in range(1, parts):
            attn += dot_tn(mixed[s][m][...], weight[m][...])
        hidden_ref[pl.ds(s * shard, shard), :] = total + attn
    cen, inv = centred(hidden_ref[...])
    normed = cen * inv * gain_ref[...]
    gate = gate_parts(normed, route_ref[...], embed_ref[...], member_ref[...])[-1]
    gate_ref[...] = jnp.broadcast_to(gate, gate_ref.shape)
    low = normed.astype(BF16)
    scalars = split_rows(gate)
    for g in range(groups):
        place = place_ref[pl.ds(g * cap, cap), :]
        packed[g][pl.ds(0, cap), :] = dot_nn(place, low).astype(BF16)
        packed[g][pl.ds(cap, 8), :] = jnp.zeros((8, packed[g].shape[1]), BF16)
        packed[g][pl.ds(cap, 8), pl.ds(0, cap)] = dot_nt(scalars, place).astype(BF16)


def back_kernel(seqs, parts, groups, *refs):
    refs = list(refs)
    take = lambda n: [refs.pop(0) for _ in range(n)]
    packed = take(groups)
    cot_ref, hidden_ref = take(2)
    weight = take(parts)
    gain_ref, route_ref, embed_ref, member_ref, place_ref = take(5)
    grad_ref, low_ref, stats_ref = take(3)
    mixed_grad = take(parts)
    rows = hidden_ref.shape[0]
    shard = rows // seqs
    cap = place_ref.shape[0] // groups
    weight = [ref.at[:, pl.ds(shard, hidden_ref.shape[1])] for ref in weight]
    grad_normed = None
    scalars = None
    for g in range(groups):
        place = place_ref[pl.ds(g * cap, cap), :]
        part = dot_tn(place, packed[g][pl.ds(0, cap), :])
        scalar = dot_nn(packed[g][pl.ds(cap, 8), pl.ds(0, cap)], place)
        grad_normed = part if g == 0 else grad_normed + part
        scalars = scalar if g == 0 else scalars + scalar
    at = lax.broadcasted_iota(jnp.int32, scalars.shape, 0)
    grad_gate = jnp.sum(jnp.where(at < 3, scalars, 0.0), axis=0, keepdims=True)
    cen, inv = centred(hidden_ref[...])
    unit = cen * inv
    gain = gain_ref[...]
    normed = unit * gain
    raw, raw_inv, dirs, embed_inv, centers, probs, gate = gate_parts(
        normed, route_ref[...], embed_ref[...], member_ref[...]
    )
    grad_logits = (3.0 * grad_gate * gate) * (member_ref[...] - probs)
    grad_dirs = dot_tn(centers, grad_logits, EXACT)
    grad_centers = dot_nt(grad_logits, dirs, EXACT)
    grad_raw = raw_inv * (
        grad_dirs - dirs * jnp.sum(dirs * grad_dirs, axis=0, keepdims=True)
    )
    router = route_ref.shape[0]
    experts = embed_ref.shape[0]
    stats_ref[...] = jnp.zeros(stats_ref.shape, F32)
    stats_ref[pl.ds(router + 16, experts), pl.ds(0, router)] = embed_inv * (
        grad_centers - centers * jnp.sum(centers * grad_centers, axis=1, keepdims=True)
    )
    stats_ref[pl.ds(0, router), :] = dot_nn(grad_raw, normed, EXACT)
    stats_ref[pl.ds(router + 8, 8), pl.ds(0, experts)] = dot_nt(
        jnp.ones((8, rows), F32), member_ref[...], EXACT
    )
    grad_normed = grad_normed + dot_tn(grad_raw, route_ref[...], EXACT)
    stats_ref[pl.ds(router, 1), :] = jnp.sum(grad_normed * unit, axis=0, keepdims=True)
    grad_unit = grad_normed * gain
    grad_hidden = inv * (
        grad_unit
        - jnp.mean(grad_unit, axis=1, keepdims=True)
        - unit * jnp.mean(grad_unit * unit, axis=1, keepdims=True)
    )
    grad_hidden = cot_ref[...].astype(F32) + grad_hidden
    grad_ref[...] = grad_hidden
    low_ref[...] = grad_hidden.astype(BF16)
    for s in range(seqs):
        low = low_ref[pl.ds(s * shard, shard), :]
        for m in range(parts):
            mixed_grad[m][:, pl.ds(s * shard, shard)] = dot_nt(weight[m][...], low).astype(BF16)


def out_kernel(groups, cap, *refs):
    back = refs[:groups]
    hidden_ref, gate_ref, place_ref, out_ref = refs[groups:]
    mixture = None
    for g in range(groups):
        rows = back[g][pl.ds(back[g].shape[0] - cap, cap), :]
        part = dot_tn(place_ref[pl.ds(g * cap, cap), :], rows)
        mixture = part if g == 0 else mixture + part
    out_ref[...] = hidden_ref[...] + gate_ref[...] * mixture


def tail_kernel(parts, core_ref, *refs):
    refs = list(refs)
    take = lambda n: [refs.pop(0) for _ in range(n)]
    grads = take(parts)
    (weight,) = take(1)
    mine = take(parts - 1)
    theirs, tok_ref, gain_ref, hidden_grad_ref, out_ref = take(5)
    core = core_ref[0]
    rows = weight.shape[0]
    half = rows // 2
    near = pl.ds(pl.multiple_of(core * half, 16), half)
    away = pl.ds(pl.multiple_of((1 - core) * half, 16), half)
    grad_normed = dot_tn(grads[0][...], weight[...])
    for m in range(1, parts):
        grad_normed += dot_tn(grads[m][near, :], mine[m - 1][...])
        grad_normed += dot_tn(grads[m][away, :], theirs[pl.ds((m - 1) * half, half), :])
    cen, inv = centred(tok_ref[...].astype(F32))
    unit = cen * inv
    grad_unit = grad_normed * gain_ref[...]
    out_ref[...] = hidden_grad_ref[...] + inv * (
        grad_unit
        - jnp.mean(grad_unit, axis=1, keepdims=True)
        - unit * jnp.mean(grad_unit * unit, axis=1, keepdims=True)
    )


def gelu_pair(x):
    z = jnp.abs(x) * (0.5**0.5)
    t = 1.0 / (1.0 + ERFC_SLOPE * z)
    poly = jnp.full_like(t, ERFC[-1])
    for value in ERFC[-2::-1]:
        poly = poly * t + value
    bell = jnp.exp2(x * x * (-0.5 * LOG2E))
    tail = (0.5 * bell) * (t * poly)
    cdf = jnp.where(x < 0.0, tail, 1.0 - tail)
    return x * cdf, cdf + x * (bell * 0.3989422804014327)


def expert_kernel(count, steps, *refs):
    refs = list(refs)
    take = lambda n: [refs.pop(0) for _ in range(n)]
    packed, cot = take(count), take(count)
    ups, downs = take(2), take(2)
    cap = cot[0].shape[0]
    returned, grads = [], []
    for i in range(count):
        (ref,) = take(1)
        if ref.shape[0] == cap:
            returned.append(ref)
            grads += take(1)
        else:
            grads.append(ref.at[pl.ds(0, cap + 8), :])
            returned.append(ref.at[pl.ds(cap + 8, cap), :])
    rows_ref, gr_ref = take(2)
    acts, gups = take(2), take(2)
    ret_acc, grad_acc = take(2)
    step = pl.program_id(0)

    def eye():
        shape = (cap, cap)
        return lax.broadcasted_iota(jnp.int32, shape, 0) == lax.broadcasted_iota(jnp.int32, shape, 1)

    @pl.when(step == 0)
    def _():
        for i in range(count):
            part = pl.ds(i * cap, cap)
            rows_ref[part, :] = packed[i][pl.ds(0, cap), :]
            scalars = packed[i][pl.ds(cap, 8), pl.ds(0, cap)].astype(F32)
            at = lax.broadcasted_iota(jnp.int32, scalars.shape, 0)
            row = jnp.sum(jnp.where(at < 3, scalars, 0.0), axis=0, keepdims=True)
            gate = jnp.sum(jnp.where(eye(), row, 0.0), axis=1, keepdims=True)
            gr_ref[part, :] = (gate * cot[i][...].astype(F32)).astype(BF16)

    rows, grad_rows = rows_ref[...], gr_ref[...]
    ret = None
    for h in range(2):
        up_w, down_w = ups[h][...], downs[h][...]
        act, slope = gelu_pair(dot_nn(rows, up_w))
        act = act.astype(BF16)
        gup = (dot_nn(grad_rows, down_w) * slope).astype(BF16)
        acts[h][...] = act
        gups[h][...] = gup
        ret_part = dot_nt(act, down_w)
        grad_part = dot_nt(gup, up_w)
        ret = ret_part if h == 0 else ret + ret_part
        grad = grad_part if h == 0 else grad + grad_part

    @pl.when(step == 0)
    def _():
        ret_acc[...] = ret
        grad_acc[...] = grad

    @pl.when(step > 0)
    def _():
        ret_acc[...] += ret
        grad_acc[...] += grad

    @pl.when(step == steps - 1)
    def _():
        for i in range(count):
            part = pl.ds(i * cap, cap)
            low = ret_acc[part, :].astype(BF16)
            returned[i][...] = low
            product = jnp.sum(low.astype(F32) * cot[i][...].astype(F32), axis=1, keepdims=True)
            row = jnp.sum(jnp.where(eye(), product, 0.0), axis=0, keepdims=True)
            grads[i][pl.ds(0, cap), :] = grad_acc[part, :].astype(BF16)
            grads[i][pl.ds(cap, 8), :] = jnp.zeros((8, grads[i].shape[1]), BF16)
            grads[i][pl.ds(cap, 8), pl.ds(0, cap)] = split_rows(row)


def expert(packed, cot, cap, up_own, up_other, down_own, down_other, joined=()):
    count = len(cot)
    feat, units = up_own.shape
    width = 512 if units % 512 == 0 else units
    steps = units // width
    rows = count * cap

    def same(size, at=0):
        return pl.BlockSpec((size, feat), lambda j: (at, 0))

    weight = pl.BlockSpec((feat, width), lambda j: (0, j))
    wide = pl.BlockSpec((rows, width), lambda j: (0, j))
    sizes = []
    for i in range(count):
        sizes += [2 * cap + 8] if i in joined else [cap, cap + 8]
    outs = pl.pallas_call(
        functools.partial(expert_kernel, count, steps),
        grid=(steps,),
        in_specs=[same(cap + 8, at) for _, at in packed]
        + [same(cap, at) for _, at in cot]
        + [weight] * 4,
        out_specs=[same(size) for size in sizes] + [same(rows)] * 2 + [wide] * 4,
        out_shape=[SDS((size, feat), BF16) for size in sizes]
        + [pltpu.HBM((rows, feat), BF16)] * 2
        + [pltpu.HBM((rows, units), BF16)] * 4,
        scratch_shapes=[VMEM((rows, feat), F32)] * 2,
        compiler_params=pltpu.CompilerParams(
            vmem_limit_bytes=24 << 20, dimension_semantics=("arbitrary",)
        ),
        cost_estimate=cost(
            16 * rows * feat * units, 8 * feat * units + 16 * rows * units, 4 * rows * units
        ),
    )(
        *[a for a, _ in packed],
        *[in_hbm(a) for a, _ in cot],
        *[in_hbm(w) for w in (up_own, up_other, down_own, down_other)],
    )
    back, grads = [], []
    at = 0
    for i in range(count):
        back.append(outs[at])
        if i not in joined:
            at += 1
        grads.append(outs[at])
        at += 1
    return back, grads, outs[at], outs[at + 1], outs[at + 2 : at + 4], outs[at + 4 :]


def expert_grad_kernel(halves, me_ref, *refs):
    refs = list(refs)
    take = lambda n: [refs.pop(0) for _ in range(n)]
    rows = take(halves)
    wide = [take(2) for _ in range(halves)]
    own_ref, other_ref = take(2)
    (row_t,) = take(1)
    size = rows[0].shape[0]

    @pl.when(pl.program_id(0) == 0)
    def _():
        for i in range(halves):
            row_t[:, pl.ds(i * size, size)] = rows[i][...].T

    for h, ref in enumerate((own_ref, other_ref)):
        full = jnp.concatenate([wide[i][h][...] for i in range(halves)], axis=0)
        ref[0] = dot_nn(row_t[...], full).astype(ref.dtype)


def expert_grad(me, rows, wide, tensor_size, cover=COVER):
    halves = len(rows)
    size, feat = rows[0].shape
    units = wide[0][0].shape[1]
    width = units // tensor_size
    same = pl.BlockSpec((size, feat), lambda j, me: (0, 0))
    part = pl.BlockSpec((size, width), lambda j, me: (0, me[0] ^ j))
    block = pl.BlockSpec((1, feat, width), lambda j, me: (j, 0, 0))
    shape = (tensor_size, feat, width)
    return pl.pallas_call(
        functools.partial(expert_grad_kernel, halves),
        grid_spec=pltpu.PrefetchScalarGridSpec(
            num_scalar_prefetch=1,
            grid=(tensor_size,),
            in_specs=[same] * halves + [part] * (2 * halves),
            out_specs=[block, block],
            scratch_shapes=[VMEM((feat, halves * size), BF16)],
        ),
        out_shape=[pltpu.HBM(shape, BF16), pltpu.HBM(shape, BF16)],
        compiler_params=pltpu.CompilerParams(
            vmem_limit_bytes=24 << 20, dimension_semantics=("arbitrary",)
        ),
        cost_estimate=cost(4 * halves * size * feat * units, 12 << 20, cover=cover),
    )(me.reshape(1), *[in_hbm(r) for r in rows], *[in_hbm(a) for pair in wide for a in pair])


def out_grad_kernel(seqs, parts, core_ref, *refs):
    mixed = [refs[s * parts : (s + 1) * parts] for s in range(seqs)]
    low_ref, keep_ref, send_ref, full_ref = refs[seqs * parts :]
    core = core_ref[0]
    shard = low_ref.shape[0] // seqs
    half = keep_ref.shape[1]
    for m in range(parts):
        total = dot_nn(mixed[0][m][:, pl.ds(0, shard)], low_ref[pl.ds(0, shard), :])
        for s in range(1, seqs):
            total += dot_nn(mixed[s][m][...], low_ref[pl.ds(s * shard, shard), :])
        full_ref[...] = total
        keep_ref[m] = full_ref[pl.ds(pl.multiple_of(core * half, half), half), :]
        send_ref[m] = full_ref[pl.ds(pl.multiple_of((1 - core) * half, half), half), :].astype(BF16)


def qkv_grad_kernel(seqs, parts, core_ref, *refs):
    grads = [refs[s * parts : (s + 1) * parts] for s in range(seqs)]
    normed = refs[seqs * parts : seqs * parts + seqs]
    w_ref, keep_ref, send_ref, norm1_ref, full_ref = refs[seqs * parts + seqs :]
    core = core_ref[0]
    shard = grads[0][0].shape[1]
    half = keep_ref.shape[0]
    for s in range(seqs):
        for b in range(parts):
            part = dot_nn(grads[s][b][...], normed[s][pl.ds(b * shard, shard), :])
            if s == 0 and b == 0:
                full_ref[...] = part
            else:
                full_ref[...] += part
    norm1_ref[...] = jnp.sum(full_ref[...] * w_ref[...].astype(F32), axis=0, keepdims=True)
    keep_ref[...] = full_ref[pl.ds(pl.multiple_of(core * half, half), half), :]
    send_ref[...] = full_ref[pl.ds(pl.multiple_of((1 - core) * half, half), half), :].astype(BF16)


def program(tensor_size, expert_size):
    chips = expert_size // 2
    bits = chips.bit_length() - 1

    def over_tensor(values, mask):
        return lax.ppermute(values, "tensor", [(i, i ^ mask) for i in range(tensor_size)])

    def over_core(values):
        return lax.ppermute(values, "expert", [(i, i ^ 1) for i in range(expert_size)])

    def over_chip(values, mask):
        return lax.ppermute(values, "expert", [(i, i ^ (2 * mask)) for i in range(expert_size)])

    def from_tensor(blocks):
        return [blocks[0]] + [over_tensor(blocks[m], m) for m in range(1, tensor_size)]

    def swap_chips(blocks):
        if chips <= 4:
            return [blocks[0]] + [over_chip(blocks[m], m) for m in range(1, chips)]
        chip = lax.axis_index("expert") // 2
        order = chip ^ jnp.arange(chips)
        groups = [[2 * i + core for i in range(chips)] for core in range(2)]
        moved = lax.all_to_all(
            jnp.stack(blocks)[order],
            "expert",
            split_axis=0,
            concat_axis=0,
            tiled=True,
            axis_index_groups=groups,
        )[order]
        return [moved[m] for m in range(chips)]

    def swap_four(pair, last):
        size = last.shape[0]
        one = over_chip(pair, 1)
        return one, over_chip(jnp.concatenate([last, one[size:]], axis=0), 3)

    if chips == 4:
        masks = (1, 3)
    else:
        masks = tuple(1 << bit for bit in range(bits))

    def chip_bit(level):
        chip = lax.axis_index("expert") // 2
        if chips == 4:
            return ((chip ^ (chip >> 1)) & 1) if level == 0 else (chip >> 1) & 1
        return (chip >> level) & 1

    def halves(values, bit):
        half = values.shape[0] // 2
        low, high = values[:half], values[half:]
        return jnp.where(bit == 0, low, high), jnp.where(bit == 0, high, low)

    def joined(mine, theirs, bit):
        return jnp.concatenate(
            [jnp.where(bit == 0, mine, theirs), jnp.where(bit == 0, theirs, mine)], axis=0
        )

    def total_everywhere(values):
        mask = 1
        while mask < tensor_size:
            values = values + over_tensor(values, mask)
            mask *= 2
        values = values + over_core(values)
        for mask in masks:
            values = values + over_chip(values, mask)
        return values

    def total_over_chips(values):
        for level, mask in enumerate(masks):
            keep, send = halves(values, chip_bit(level))
            values = keep + over_chip(send.astype(BF16), mask).astype(F32)
        low = values.astype(BF16)
        for level in reversed(range(bits)):
            low = joined(low, over_chip(low, masks[level]), chip_bit(level))
        return low

    def body(
        tokens,
        out_grad,
        masked,
        route,
        norm1_gain,
        query_key_value_weight,
        output_weight,
        norm2_gain,
        route_weight,
        expert_embed,
        up_weight,
        down_weight,
    ):
        seqs, shard, feat = tokens.shape
        rows_here = seqs * shard
        experts, router = expert_embed.shape
        cap = rows_here // experts
        channels = query_key_value_weight.shape[2]
        units = up_weight.shape[2]
        parts = tensor_size
        me = lax.axis_index("tensor")
        place_index = lax.axis_index("expert")
        chip, core = place_index // 2, place_index % 2
        gain1 = norm1_gain.reshape(1, feat)
        gain2 = norm2_gain.reshape(1, feat)

        w_rows = query_key_value_weight.transpose(0, 2, 1).reshape(3 * channels, feat)
        half_rows = 3 * channels // 2
        w_half = lax.dynamic_slice_in_dim(w_rows, core * half_rows, half_rows, axis=0)
        gathered = []
        for s in range(seqs):
            block = tokens[s] if s == 0 else tie(tokens[s], gathered[-1])
            gathered.append(from_tensor([block] * parts))

        picks = route.reshape(rows_here)
        expert_ids = jnp.arange(experts, dtype=jnp.int32)
        member = (picks[:, None] == expert_ids[None, :]).astype(jnp.int32)
        earlier = jnp.cumsum(member, axis=0) - member
        slot_ids = jnp.sum(earlier * member, axis=1)
        target = (picks ^ chip) * cap + slot_ids
        target = jnp.where(slot_ids < cap, target, -1)
        slot_range = jnp.arange(experts * cap, dtype=jnp.int32)
        placing = (slot_range[:, None] == target[None, :]).astype(BF16)
        member_t = (expert_ids[:, None] == picks[None, :]).astype(F32)
        cotangent = out_grad.reshape(rows_here, feat) * masked.reshape(rows_here, 1).astype(BF16)
        sent_cotangent = dot_nn(placing, cotangent).astype(BF16)
        if experts == 4:
            one, two = swap_four(sent_cotangent[cap : 3 * cap], sent_cotangent[3 * cap :])
            slot_cotangent = [(sent_cotangent, 0), (one, 0), (two, 0), (two, 1)]
        else:
            slot_cotangent = [
                (block, 0)
                for block in swap_chips(
                    [sent_cotangent[g * cap : (g + 1) * cap] for g in range(experts)]
                )
            ]

        normed, qkv, lse, mixed = [], [], [], []
        up_other, down_other = over_core(up_weight[0]), over_core(down_weight[0])
        for s in range(seqs):
            if s == 0:
                gathered[0] = tie(
                    gathered[0], sent_cotangent, member_t, w_half, up_other, down_other
                )
            if s == 1:
                gathered[s] = tie(gathered[s], slot_cotangent[1][0], lse[0])
            rider = (output_weight,) if s == 0 else ()
            n, q, l, blocks = attend(gathered[s], gain1, w_rows, *rider)
            normed.append(n)
            qkv.append(q)
            lse.append(l)
            mixed.append(from_tensor(blocks))

        flat_tokens = tokens.reshape(rows_here, feat)
        route_t = route_weight.T
        ready = tie(mixed, [block for block, _ in slot_cotangent[1:]])
        hidden, gate, *packed = call(
            functools.partial(middle_kernel, seqs, parts, experts),
            [Far(SDS((rows_here, feat), F32)), Far(SDS((8, rows_here), F32))]
            + [SDS((cap + 8, feat), BF16)] * experts,
            [flat_tokens, *[b for blocks in ready for b in blocks]]
            + [gain2, route_t, expert_embed, member_t, Far(placing)],
            4 * rows_here * feat * feat,
        )

        half = experts // 2
        expert_weights = (up_weight[0], up_other, down_weight[0], down_other)
        w_held = tie(w_half, packed)
        w_near = [over_tensor(w_held, m) for m in range(1, parts - 1)]
        if experts == 4:
            one = over_chip(packed[1], 1)
            held = tie(packed[2:], one)
            two, three = over_chip(held[0], 2), over_chip(held[1], 3)
            slot_rows = [(packed[0], 0), (one, 0)]
            low_half = expert(slot_rows[:2], slot_cotangent[:2], cap, *expert_weights, joined=(1,))
            near = over_chip(low_half[1][1], 1)
            three, two, w_near = tie((three, two, w_near), low_half[1])
            w_far = over_tensor(tie(w_half, w_near), parts - 1)
            high_half = expert([(three, 0), (two, 0)], slot_cotangent[2:], cap, *expert_weights)
        else:
            slot_rows = [(block, 0) for block in swap_chips(packed)]
            low_half = expert(slot_rows[:half], slot_cotangent[:half], cap, *expert_weights)
            high_half = expert(slot_rows[half:], slot_cotangent[half:], cap, *expert_weights)
            w_far = over_tensor(tie(w_half, w_near), parts - 1)
            near = ()
        results = [low_half, high_half]
        rows = [r[2] for r in results]
        grad_rows = [r[3] for r in results]
        acts = [r[4] for r in results]
        gups = [r[5] for r in results]
        rows, near = tie((rows, near), w_far)
        up_own, up_send = expert_grad(me, rows, gups, parts)
        up_recv = over_core(up_send)
        w_mine = [*w_near, w_far]
        w_theirs = over_core(jnp.concatenate(w_mine, axis=0))
        down_own, down_send = expert_grad(me, tie(grad_rows, up_send), acts, parts, cover=0)
        if experts == 4:
            back_grad = [
                low_half[1][0],
                near,
                over_chip(high_half[1][1], 2),
                over_chip(high_half[1][0], 3),
            ]
        else:
            back_grad = swap_chips(low_half[1] + high_half[1])

        def first_pair(own, recv, mask):
            return jnp.stack(
                [own[m].astype(F32) + recv[m].astype(F32) for m in (mask, parts - 1)]
            ).astype(BF16)

        up_pair = first_pair(up_own, up_recv, 1)
        back_grad, down_send = tie((back_grad, down_send), up_pair, w_theirs)
        down_recv = over_core(down_send)

        outs = call(
            functools.partial(back_kernel, seqs, parts, experts),
            [
                Far(SDS((rows_here, feat), F32)),
                Far(SDS((rows_here, feat), BF16)),
                SDS((router + 16 + -(-experts // 8) * 8, feat), F32),
            ]
            + [SDS((channels, rows_here), BF16)] * parts,
            [*back_grad, Far(cotangent), Far(hidden)]
            + [Far(block) for block in mixed[0]]
            + [gain2, route_t, expert_embed, member_t, Far(placing)],
            4 * rows_here * feat * feat,
        )
        grad_hidden, grad_low, stats = outs[:3]
        grad_mixed = from_tensor(outs[3:])
        if experts == 4:
            two, three = tie((high_half[0][1], high_half[0][0]), back_grad)
            back = [low_half[0][0], near, over_chip(two, 2), over_chip(three, 3)]
        else:
            back = swap_chips(low_half[0] + high_half[0])

        out_half = channels // 2
        out_keep, out_send = call(
            functools.partial(out_grad_kernel, seqs, parts),
            [SDS((parts, out_half, feat), F32), SDS((parts, out_half, feat), BF16)],
            [Far(b) for blocks in mixed for b in blocks] + [Far(tie(grad_low, back))],
            2 * rows_here * feat * feat,
            [VMEM((channels, feat), F32)],
            scalar=core,
        )
        out_keep = out_keep + over_core(out_send).astype(F32)
        out_held = tie(out_keep, grad_mixed).astype(BF16)
        out_got = [over_tensor(out_held[m], m) for m in range(1, parts)]
        down_pair = first_pair(down_own, down_recv, 2 % parts)

        if parts == 4:
            up_got = over_tensor(tie(up_pair, grad_mixed), 1)
            down_got = over_tensor(tie(down_pair, grad_mixed), 2)
        else:
            up_got, down_got = (), ()

        def second(own, recv, got, mask):
            return (own[mask].astype(F32) + recv[mask].astype(F32) + got[1].astype(F32)).astype(BF16)

        def final(own, recv, got, last):
            total = own[0].astype(F32) + recv[0].astype(F32)
            return (total + got[0].astype(F32) + last.astype(F32))[None]

        def slow_scatter(own, recv):
            total = own[0].astype(F32) + recv[0].astype(F32)
            for m in range(1, parts):
                part = own[m].astype(F32) + recv[m].astype(F32)
                total = total + over_tensor(part.astype(BF16), m).astype(F32)
            return total[None]

        grads, grad_blocks = [], []
        came = tie(grad_mixed, down_pair, out_keep)
        for s in range(seqs):
            if s == 1:
                came = tie(came, grads[0], out_got)
            blocks = attend_back(qkv[s], lse[s], came, s)
            grads.append(blocks)
            grad_blocks.append(from_tensor(blocks))

        split = 3 * channels // 2
        qkv_keep, qkv_send, norm1_grad = call(
            functools.partial(qkv_grad_kernel, seqs, parts),
            [SDS((split, feat), F32), SDS((split, feat), BF16), SDS((1, feat), F32)],
            [b for blocks in grads for b in blocks] + [Far(n) for n in normed] + [Far(w_rows)],
            2 * seqs * parts * shard * 3 * channels * feat,
            [VMEM((3 * channels, feat), F32)],
            scalar=core,
        )
        qkv_keep = qkv_keep + over_core(qkv_send).astype(F32)
        out_part = sum((got.astype(F32) for got in out_got), out_keep[0])
        summed = total_over_chips(jnp.concatenate([qkv_keep, out_part], axis=0))
        other_half = over_core(summed)
        query_key_value_gradient = (
            joined(summed[:split], other_half[:split], core)
            .reshape(3, channels, feat)
            .transpose(0, 2, 1)
            .astype(F32)
        )
        out_proj_grad = joined(summed[split:], other_half[split:], core).astype(F32)

        stats = total_everywhere(
            stats + jnp.pad(norm1_grad, ((router + 1, stats.shape[0] - router - 2), (0, 0)))
        )
        route_grad = stats[:router].T
        norm2_grad = stats[router]
        norm1_grad = stats[router + 1] / norm1_gain
        loads = stats[router + 8, :experts]
        embed_grad = stats[router + 16 : router + 16 + experts, :router]

        (result,) = call(
            functools.partial(out_kernel, experts, cap),
            [Far(SDS((rows_here, feat), F32))],
            [Far(b) for b in tie(back, qkv_send)] + [Far(hidden), gate[:1].T, Far(placing)],
            2 * rows_here * rows_here * feat,
        )

        input_grads = []
        for s in range(seqs):
            (input_part,) = call(
                functools.partial(tail_kernel, parts),
                [Far(SDS((shard, feat), F32))],
                [*tie(grad_blocks[s], qkv_send), Far(w_rows), *[Far(w) for w in w_mine]]
                + [Far(w_theirs), Far(flat_tokens, (shard, feat), s), gain1]
                + [Far(grad_hidden, (shard, feat), s)],
                2 * shard * feat * 3 * channels * parts,
                scalar=core,
            )
            input_grads.append(input_part)

        if parts == 4:
            up_got, down_got = tie((up_got, down_got), grad_blocks)
            up_last = over_tensor(second(up_own, up_recv, up_got, 2), 2)
            down_last = over_tensor(second(down_own, down_recv, down_got, 1), 1)
            up_weight_grad = final(up_own, up_recv, up_got, up_last)
            down_weight_grad = final(down_own, down_recv, down_got, down_last)
        else:
            up_weight_grad = slow_scatter(up_own, up_recv)
            down_weight_grad = slow_scatter(down_own, down_recv)

        return (
            result.reshape(seqs, shard, feat),
            jnp.stack(input_grads),
            loads,
            norm1_grad,
            query_key_value_gradient,
            out_proj_grad,
            norm2_grad,
            route_grad,
            embed_grad,
            up_weight_grad,
            down_weight_grad,
        )

    return body


def solution(mesh):
    return jax.shard_map(
        program(mesh.shape["tensor"], mesh.shape["expert"]),
        mesh=mesh,
        in_specs=(
            P("expert", "tensor", None),
            P("expert", "tensor", None),
            P("expert", "tensor"),
            P("expert", "tensor", None),
            P(),
            P(None, None, "tensor"),
            P("tensor", None),
            P(),
            P(),
            P(),
            P("expert", None, None),
            P("expert", None, None),
        ),
        out_specs=(
            P("expert", "tensor", None),
            P("expert", "tensor", None),
            P(),
            P(),
            P(None, None, "tensor"),
            P("tensor", None),
            P(),
            P(),
            P(),
            P("expert", None, "tensor"),
            P("expert", None, "tensor"),
        ),
        check_vma=False,
    )
```

```python
import functools

import jax
import jax.numpy as jnp
from jax import lax
from jax.experimental import pallas as pl
from jax.experimental.pallas import tpu as pltpu
from jax.sharding import PartitionSpec as P

HEAD = 64
F32 = jnp.float32
BF16 = jnp.bfloat16
LOG2E = 1.4426950408889634
SCALE = HEAD**-0.5
EXACT = lax.Precision.HIGHEST
SDS = jax.ShapeDtypeStruct
VMEM = pltpu.VMEM
COVER = 4

ERFC_SLOPE = 0.44
ERFC = (
    0.248227568,
    0.248777028,
    0.217859919,
    0.214130365,
    -0.0172025688,
    0.293641958,
    -0.276276279,
    0.0708421859,
)


def dot_nn(left, right, precision=None):
    return jnp.dot(left, right, preferred_element_type=F32, precision=precision)


def dot_nt(left, right, precision=None):
    return lax.dot_general(
        left, right, (((1,), (1,)), ((), ())), preferred_element_type=F32, precision=precision
    )


def dot_tn(left, right, precision=None):
    return lax.dot_general(
        left, right, (((0,), (0,)), ((), ())), preferred_element_type=F32, precision=precision
    )


class Far:
    def __init__(self, value, block=None, at=0):
        self.value = value
        self.block = value.shape if block is None else block
        self.at = at


class Loose(Far):
    pass


class Free(Far):
    pass


def start_all(pairs, sems):
    copies = [pltpu.make_async_copy(a, b, sems.at[i]) for i, (a, b) in enumerate(pairs)]
    for copy in copies:
        copy.start()

    def wait():
        for copy in copies:
            copy.wait()

    return wait


def plain(value):
    return value.value if isinstance(value, Far) else value


def in_hbm(value):
    return pltpu.with_memory_space_constraint(value, pltpu.HBM)


def cost(flops, size, transcendentals=0, cover=COVER):
    return pl.CostEstimate(
        flops=flops * cover, bytes_accessed=size * cover, transcendentals=transcendentals * cover
    )


def call(kernel, outs, args, flops, scratch=(), limit=24, transcendentals=0, scalar=None, cover=COVER, aliases=None):
    whole = pl.BlockSpec(memory_space=VMEM)

    def spec(arg):
        if isinstance(arg, Loose):
            return pl.BlockSpec(memory_space=pl.ANY)
        if not isinstance(arg, Far):
            return whole
        if isinstance(arg, (Loose, Free)):
            return pl.BlockSpec(memory_space=pl.ANY)
        where = (arg.at,) + (0,) * (arg.value.ndim - 1)
        return pl.BlockSpec(
            arg.block, lambda i: where, pipeline_mode=pl.Buffered(buffer_count=1)
        )

    specs = [spec(a) for a in args]
    out_specs = [spec(o) for o in outs]
    size = sum(a.size * a.dtype.itemsize for a in map(plain, args))
    size += sum(o.size * o.dtype.itemsize for o in map(plain, outs))
    args = [
        a.value if isinstance(a, Free) else in_hbm(a.value) if isinstance(a, Far) else a for a in args
    ]
    outs = [pltpu.HBM(o.value.shape, o.value.dtype) if isinstance(o, Far) else o for o in outs]
    if scalar is not None:
        specs = [pl.BlockSpec(memory_space=pltpu.SMEM)] + specs
        args = [scalar.reshape(1)] + args
    return pl.pallas_call(
        kernel,
        grid=(1,),
        out_shape=list(outs),
        in_specs=specs,
        out_specs=out_specs,
        scratch_shapes=list(scratch),
        input_output_aliases=aliases or {},
        compiler_params=pltpu.CompilerParams(vmem_limit_bytes=limit << 20),
        cost_estimate=cost(flops, size, transcendentals, cover),
    )(*args)


def centred(x):
    cen = x - jnp.mean(x, axis=1, keepdims=True)
    return cen, lax.rsqrt(jnp.mean(cen * cen, axis=1, keepdims=True) + 1e-05)


def tie(values, *after):
    return lax.optimization_barrier((values, after))[0]


def attend_kernel(parts, channels, riding, *refs):
    tok = refs[:parts]
    gain_ref, w_ref = refs[parts : parts + 2]
    rider = refs[parts + 2 : parts + 2 + riding]
    refs = refs[parts + 2 + riding :]
    normed_out, qkv_out, lse_ref = refs[:3]
    mixed = refs[3 : 3 + parts]
    normed_ref, qkv_ref, sems = refs[3 + parts :]
    shard = tok[0].shape[0]
    for ref in rider:
        for b in range(parts):
            mixed[b][:, pl.ds(shard, ref.shape[1])] = ref[...]
    for b in range(parts):
        cen, inv = centred(tok[b][...].astype(F32))
        rows = (cen * inv * gain_ref[...]).astype(BF16)
        normed_ref[pl.ds(b * shard, shard), :] = rows
        qkv_ref[:, pl.ds(b * shard, shard)] = dot_nt(w_ref[...], rows).astype(BF16)
    copies = [
        pltpu.make_async_copy(normed_ref, normed_out, sems.at[0]),
        pltpu.make_async_copy(qkv_ref, qkv_out, sems.at[1]),
    ]
    for copy in copies:
        copy.start()
    size = 128
    chunks = parts * shard // size

    def head(h, carry):
        off = pl.multiple_of(h * HEAD, HEAD)
        key = qkv_ref[pl.ds(channels + off, HEAD), :].T
        value_t = qkv_ref[pl.ds(2 * channels + off, HEAD), :]
        for b in range(parts):
            query_t = qkv_ref[pl.ds(off, HEAD), pl.ds(b * shard, shard)]
            scores = [dot_nn(key[i * size : (i + 1) * size], query_t) for i in range(chunks)]
            top = None
            for score in scores:
                part = jnp.max(score.reshape(size // 8, 8, shard), axis=0)
                top = part if top is None else jnp.maximum(top, part)
            top = jnp.max(top, axis=0, keepdims=True) * (SCALE * LOG2E)
            total, out = None, None
            for i, score in enumerate(scores):
                expos = jnp.exp2(score * (SCALE * LOG2E) - top)
                part = jnp.sum(expos.reshape(size // 8, 8, shard), axis=0)
                term = dot_nn(value_t[:, i * size : (i + 1) * size], expos.astype(BF16))
                total = part if i == 0 else total + part
                out = term if i == 0 else out + term
            total = jnp.sum(total, axis=0, keepdims=True)
            mixed[b][pl.ds(off, HEAD), pl.ds(0, shard)] = (out * (1.0 / total)).astype(BF16)
            lse_ref[pl.ds(h, 1), pl.ds(b * shard, shard)] = top + jnp.log2(total)
        return carry

    lax.fori_loop(0, channels // HEAD, head, 0)
    for copy in copies:
        copy.wait()


def attend(tok, gain, w_rows, *rider):
    parts = len(tok)
    shard, feat = tok[0].shape
    length = parts * shard
    channels = w_rows.shape[0] // 3
    outs = call(
        functools.partial(attend_kernel, parts, channels, len(rider)),
        [
            Loose(SDS((length, feat), BF16)),
            Loose(SDS((3 * channels, length), BF16)),
            Far(SDS((8, length), F32)),
        ]
        + [SDS((channels, shard + sum(r.shape[1] for r in rider)), BF16)] * parts,
        [*tok, gain, Far(w_rows), *[Far(r) for r in rider]],
        2 * length * feat * 3 * channels + 4 * length * length * channels,
        scratch=[
            VMEM((length, feat), BF16),
            VMEM((3 * channels, length), BF16),
            pltpu.SemaphoreType.DMA((2,)),
        ],
        transcendentals=length * length * channels // HEAD,
    )
    return outs[0], outs[1], outs[2], outs[3:]


def attend_back_kernel(parts, channels, at, *refs):
    qkv_ref, lse_ref = refs[:2]
    shard = qkv_ref.shape[1] // parts
    grad = [ref.at[:, pl.ds(at * shard, shard)] for ref in refs[2 : 2 + parts]]
    refs = refs[2 + parts :]
    outs = refs[:parts]
    key_acc, value_acc = refs[parts:]

    def head(h, carry):
        off = pl.multiple_of(h * HEAD, HEAD)
        key_t = qkv_ref[pl.ds(channels + off, HEAD), :]
        key = key_t.T
        value = qkv_ref[pl.ds(2 * channels + off, HEAD), :].T
        for b in range(parts):
            query_t = qkv_ref[pl.ds(off, HEAD), pl.ds(b * shard, shard)]
            grad_t = grad[b][pl.ds(off, HEAD), :]
            scores = dot_nn(key, query_t)
            probs = jnp.exp2(
                scores * (SCALE * LOG2E) - lse_ref[pl.ds(h, 1), pl.ds(b * shard, shard)]
            )
            grad_probs = dot_nn(value, grad_t)
            inner = jnp.sum(probs * grad_probs, axis=0, keepdims=True)
            grad_scores = (probs * (grad_probs - inner)).astype(BF16)
            value_part = dot_nt(grad_t, probs.astype(BF16))
            key_part = dot_nt(query_t, grad_scores)
            outs[b][pl.ds(off, HEAD), :] = (dot_nn(key_t, grad_scores) * SCALE).astype(BF16)
            if b == 0:
                key_acc[...] = key_part
                value_acc[...] = value_part
            else:
                key_acc[...] += key_part
                value_acc[...] += value_part
        for b in range(parts):
            cols = pl.ds(b * shard, shard)
            outs[b][pl.ds(channels + off, HEAD), :] = (key_acc[:, cols] * SCALE).astype(BF16)
            outs[b][pl.ds(2 * channels + off, HEAD), :] = value_acc[:, cols].astype(BF16)
        return carry

    lax.fori_loop(0, channels // HEAD, head, 0)


def attend_back(qkv, lse, grad, at, cover):
    parts = len(grad)
    channels = grad[0].shape[0]
    length = qkv.shape[1]
    shard = length // parts
    return call(
        functools.partial(attend_back_kernel, parts, channels, at),
        [SDS((3 * channels, shard), BF16)] * parts,
        [Far(qkv), Far(lse), *[Far(g) for g in grad]],
        10 * length * length * channels,
        scratch=[VMEM((HEAD, length), F32)] * 2,
        transcendentals=length * length * channels // HEAD,
        cover=cover,
    )


def gate_parts(raw, embed, member):
    inv = lax.rsqrt(jnp.sum(raw * raw, axis=0, keepdims=True) + 1e-06)
    rows = raw * inv
    embed_inv = lax.rsqrt(jnp.sum(embed * embed, axis=1, keepdims=True) + 1e-06)
    centers = embed * embed_inv
    logits = 3.0 * dot_nn(centers, rows, EXACT)
    expos = jnp.exp(logits - jnp.max(logits, axis=0, keepdims=True))
    probs = expos / jnp.sum(expos, axis=0, keepdims=True)
    gate = jnp.sum(probs * member, axis=0, keepdims=True)
    return inv, rows, embed_inv, centers, probs, gate


def split_rows(row):
    first = row.astype(BF16).astype(F32)
    second = (row - first).astype(BF16).astype(F32)
    third = (row - first) - second
    shape = (8, row.shape[1])
    at = lax.broadcasted_iota(jnp.int32, shape, 0)
    parts = jnp.where(at == 0, first, jnp.where(at == 1, second, jnp.where(at == 2, third, 0.0)))
    return parts.astype(BF16)


def middle_kernel(seqs, parts, groups, *refs):
    refs = list(refs)
    take = lambda n: [refs.pop(0) for _ in range(n)]
    (tok_ref,) = take(1)
    mixed = [take(parts) for _ in range(seqs)]
    gain_ref, route_ref, embed_ref, member_ref, place_ref = take(5)
    hidden_ref, gate_ref, raw_ref, mixed_out, weight_out = take(5)
    packed = take(groups)
    mixed_ref, weight_ref, in_sems, out_sems = take(4)
    rows, feat = tok_ref.shape
    shard = rows // seqs
    channels = mixed[1][0].shape[0]
    cap = rows // groups
    pairs = []
    for m in range(parts):
        at = pl.ds(m * channels, channels)
        pairs.append((mixed[0][m].at[:, pl.ds(shard, feat)], weight_ref.at[at, :]))
        for s in range(seqs):
            pairs.append(
                (mixed[s][m].at[:, pl.ds(0, shard)], mixed_ref.at[at, pl.ds(s * shard, shard)])
            )
    start_all(pairs, in_sems)()
    wait = start_all([(mixed_ref, mixed_out), (weight_ref, weight_out)], out_sems)
    attn = dot_tn(mixed_ref[...], weight_ref[...])
    hidden = tok_ref[...].astype(F32) + attn
    hidden_ref[...] = hidden
    cen, inv = centred(hidden)
    normed = cen * inv * gain_ref[...]
    raw = dot_nt(route_ref[...], normed, EXACT)
    raw_ref[...] = raw
    gate = gate_parts(raw, embed_ref[...], member_ref[...])[-1]
    gate_ref[...] = jnp.broadcast_to(gate, gate_ref.shape)
    low = normed.astype(BF16)
    scalars = split_rows(gate)
    for g in range(groups):
        place = place_ref[pl.ds(g * cap, cap), :]
        packed[g][pl.ds(0, cap), :] = dot_nn(place, low).astype(BF16)
        packed[g][pl.ds(cap, 8), :] = jnp.zeros((8, feat), BF16)
        packed[g][pl.ds(cap, 8), pl.ds(0, cap)] = dot_nt(scalars, place).astype(BF16)
    wait()


def count_digits(rows, devices):
    width = max(1, (256 // devices + 1).bit_length() - 1)
    digits = -(-rows.bit_length() // width)
    return width, digits, 128 if digits <= 6 else 64


def back_kernel(seqs, parts, groups, *refs):
    refs = list(refs)
    take = lambda n: [refs.pop(0) for _ in range(n)]
    packed = take(groups)
    cot_ref, hidden_ref, raw_ref, weight_ref = take(4)
    gain_ref, route_ref, embed_ref, member_ref, place_ref = take(5)
    grad_ref, low_ref, stats_ref = take(3)
    mixed_grad = take(parts)
    (slot_ref,) = take(1)
    rows = hidden_ref.shape[0]
    shard = rows // seqs
    cap = rows // groups
    channels = mixed_grad[0].shape[0]
    scalars = None
    for g in range(groups):
        slot_ref[pl.ds(g * cap, cap), :] = packed[g][pl.ds(0, cap), :]
        scalar = dot_nn(packed[g][pl.ds(cap, 8), pl.ds(0, cap)], place_ref[pl.ds(g * cap, cap), :])
        scalars = scalar if g == 0 else scalars + scalar
    at = lax.broadcasted_iota(jnp.int32, scalars.shape, 0)
    grad_gate = jnp.sum(jnp.where(at < 3, scalars, 0.0), axis=0, keepdims=True)
    cen, inv = centred(hidden_ref[...])
    unit = cen * inv
    gain = gain_ref[...]
    raw_inv, dirs, embed_inv, centers, probs, gate = gate_parts(
        raw_ref[...], embed_ref[...], member_ref[...]
    )
    grad_logits = (3.0 * grad_gate * gate) * (member_ref[...] - probs)
    grad_dirs = dot_tn(centers, grad_logits, EXACT)
    grad_centers = dot_nt(grad_logits, dirs, EXACT)
    grad_raw = raw_inv * (
        grad_dirs - dirs * jnp.sum(dirs * grad_dirs, axis=0, keepdims=True)
    )
    router = route_ref.shape[0]
    experts = embed_ref.shape[0]
    stats_ref[...] = jnp.zeros(stats_ref.shape, F32)
    stats_ref[pl.ds(router + 8, experts), pl.ds(0, router)] = embed_inv * (
        grad_centers - centers * jnp.sum(centers * grad_centers, axis=1, keepdims=True)
    )
    stats_ref[pl.ds(0, router), :] = dot_nn(grad_raw, unit * gain, EXACT)
    count = dot_nt(jnp.ones((8, rows), F32), member_ref[...], EXACT)[:1].astype(jnp.int32)
    width, digits, stride = count_digits(rows, 2 * parts * groups)
    for digit in range(digits):
        part = (count >> (width * digit)) & ((1 << width) - 1)
        stats_ref[pl.ds(router + 1, 1), pl.ds(stride * digit, experts)] = part.astype(F32)
    grad_normed = dot_tn(place_ref[...], slot_ref[...]) + dot_tn(grad_raw, route_ref[...], EXACT)
    stats_ref[pl.ds(router, 1), :] = jnp.sum(grad_normed * unit, axis=0, keepdims=True)
    grad_unit = grad_normed * gain
    grad_hidden = inv * (
        grad_unit
        - jnp.mean(grad_unit, axis=1, keepdims=True)
        - unit * jnp.mean(grad_unit * unit, axis=1, keepdims=True)
    )
    grad_hidden = cot_ref[...].astype(F32) + grad_hidden
    grad_ref[...] = grad_hidden
    low = grad_hidden.astype(BF16)
    low_ref[...] = low
    grad_mixed = dot_nt(weight_ref[...], low).astype(BF16)
    for m in range(parts):
        mixed_grad[m][...] = grad_mixed[m * channels : (m + 1) * channels]


def out_kernel(groups, cap, *refs):
    back = refs[:groups]
    hidden_ref, gate_ref, place_ref, out_ref = refs[groups:]
    mixture = None
    for g in range(groups):
        rows = back[g][pl.ds(back[g].shape[0] - cap, cap), :]
        part = dot_tn(place_ref[pl.ds(g * cap, cap), :], rows)
        mixture = part if g == 0 else mixture + part
    out_ref[...] = hidden_ref[...] + gate_ref[...] * mixture


def tail_kernel(parts, core_ref, *refs):
    refs = list(refs)
    take = lambda n: [refs.pop(0) for _ in range(n)]
    grads = take(parts)
    (weight,) = take(1)
    mine = take(parts - 1)
    theirs, tok_ref, gain_ref, hidden_grad_ref = take(4)
    out_ref, grad_ref, weight_ref, sems = refs[-4:]
    core = core_ref[0]
    rows = weight.shape[0]
    half = rows // 2
    pairs = [(grads[m], grad_ref.at[pl.ds(m * rows, rows), :]) for m in range(parts)]
    pairs.append((weight, weight_ref.at[pl.ds(0, rows), :]))
    for m in range(1, parts):
        near = pl.multiple_of(m * rows + core * half, 16)
        away = pl.multiple_of(m * rows + (1 - core) * half, 16)
        pairs.append((mine[m - 1], weight_ref.at[pl.ds(near, half), :]))
        pairs.append((theirs.at[pl.ds((m - 1) * half, half), :], weight_ref.at[pl.ds(away, half), :]))
    start_all(pairs, sems)()
    grad_normed = dot_tn(grad_ref[...], weight_ref[...])
    cen, inv = centred(tok_ref[...].astype(F32))
    unit = cen * inv
    grad_unit = grad_normed * gain_ref[...]
    out_ref[...] = hidden_grad_ref[...] + inv * (
        grad_unit
        - jnp.mean(grad_unit, axis=1, keepdims=True)
        - unit * jnp.mean(grad_unit * unit, axis=1, keepdims=True)
    )


def gelu_pair(x):
    z = jnp.abs(x) * (0.5**0.5)
    t = 1.0 / (1.0 + ERFC_SLOPE * z)
    poly = jnp.full_like(t, ERFC[-1])
    for value in ERFC[-2::-1]:
        poly = poly * t + value
    bell = jnp.exp2(x * x * (-0.5 * LOG2E))
    tail = (0.5 * bell) * (t * poly)
    cdf = jnp.where(x < 0.0, tail, 1.0 - tail)
    return x * cdf, cdf + x * (bell * 0.3989422804014327)


def expert_kernel(count, steps, *refs):
    refs = list(refs)
    take = lambda n: [refs.pop(0) for _ in range(n)]
    packed, cot = take(count), take(count)
    ups, downs = take(2), take(2)
    cap = cot[0].shape[0]
    returned, grads = [], []
    for i in range(count):
        (ref,) = take(1)
        if ref.shape[0] == cap:
            returned.append(ref)
            grads += take(1)
        else:
            grads.append(ref.at[pl.ds(0, cap + 8), :])
            returned.append(ref.at[pl.ds(cap + 8, cap), :])
    rows_ref, gr_ref = take(2)
    acts, gups = take(2), take(2)
    ret_acc, grad_acc = take(2)
    step = pl.program_id(0)

    def eye():
        shape = (cap, cap)
        return lax.broadcasted_iota(jnp.int32, shape, 0) == lax.broadcasted_iota(jnp.int32, shape, 1)

    @pl.when(step == 0)
    def _():
        for i in range(count):
            part = pl.ds(i * cap, cap)
            rows_ref[part, :] = packed[i][pl.ds(0, cap), :]
            scalars = packed[i][pl.ds(cap, 8), pl.ds(0, cap)].astype(F32)
            at = lax.broadcasted_iota(jnp.int32, scalars.shape, 0)
            row = jnp.sum(jnp.where(at < 3, scalars, 0.0), axis=0, keepdims=True)
            gate = jnp.sum(jnp.where(eye(), row, 0.0), axis=1, keepdims=True)
            gr_ref[part, :] = (gate * cot[i][...].astype(F32)).astype(BF16)

    rows, grad_rows = rows_ref[...], gr_ref[...]
    ret = None
    for h in range(2):
        up_w, down_w = ups[h][...], downs[h][...]
        act, slope = gelu_pair(dot_nn(rows, up_w))
        act = act.astype(BF16)
        gup = (dot_nn(grad_rows, down_w) * slope).astype(BF16)
        acts[h][...] = act
        gups[h][...] = gup
        ret_part = dot_nt(act, down_w)
        grad_part = dot_nt(gup, up_w)
        ret = ret_part if h == 0 else ret + ret_part
        grad = grad_part if h == 0 else grad + grad_part

    @pl.when(step == 0)
    def _():
        ret_acc[...] = ret
        grad_acc[...] = grad

    @pl.when(step > 0)
    def _():
        ret_acc[...] += ret
        grad_acc[...] += grad

    @pl.when(step == steps - 1)
    def _():
        for i in range(count):
            part = pl.ds(i * cap, cap)
            low = ret_acc[part, :].astype(BF16)
            returned[i][...] = low
            product = jnp.sum(low.astype(F32) * cot[i][...].astype(F32), axis=1, keepdims=True)
            row = jnp.sum(jnp.where(eye(), product, 0.0), axis=0, keepdims=True)
            grads[i][pl.ds(0, cap), :] = grad_acc[part, :].astype(BF16)
            grads[i][pl.ds(cap, 8), :] = jnp.zeros((8, grads[i].shape[1]), BF16)
            grads[i][pl.ds(cap, 8), pl.ds(0, cap)] = split_rows(row)


def expert(packed, cot, cap, up_own, up_other, down_own, down_other, joined=()):
    count = len(cot)
    feat, units = up_own.shape
    width = 512 if units % 512 == 0 else units
    steps = units // width
    rows = count * cap

    def same(size, at=0):
        return pl.BlockSpec((size, feat), lambda j: (at, 0))

    weight = pl.BlockSpec((feat, width), lambda j: (0, j))
    wide = pl.BlockSpec((rows, width), lambda j: (0, j))
    sizes = []
    for i in range(count):
        sizes += [2 * cap + 8] if i in joined else [cap, cap + 8]
    outs = pl.pallas_call(
        functools.partial(expert_kernel, count, steps),
        grid=(steps,),
        in_specs=[same(cap + 8, at) for _, at in packed]
        + [same(cap, at) for _, at in cot]
        + [weight] * 4,
        out_specs=[same(size) for size in sizes] + [same(rows)] * 2 + [wide] * 4,
        out_shape=[SDS((size, feat), BF16) for size in sizes]
        + [pltpu.HBM((rows, feat), BF16)] * 2
        + [pltpu.HBM((rows, units), BF16)] * 4,
        scratch_shapes=[VMEM((rows, feat), F32)] * 2,
        compiler_params=pltpu.CompilerParams(
            vmem_limit_bytes=24 << 20, dimension_semantics=("arbitrary",)
        ),
        cost_estimate=cost(
            16 * rows * feat * units, 8 * feat * units + 16 * rows * units, 4 * rows * units
        ),
    )(
        *[a for a, _ in packed],
        *[in_hbm(a) for a, _ in cot],
        *[in_hbm(w) for w in (up_own, up_other, down_own, down_other)],
    )
    back, grads = [], []
    at = 0
    for i in range(count):
        back.append(outs[at])
        if i not in joined:
            at += 1
        grads.append(outs[at])
        at += 1
    return back, grads, outs[at], outs[at + 1], outs[at + 2 : at + 4], outs[at + 4 :]


def expert_grad_kernel(halves, me_ref, *refs):
    refs = list(refs)
    take = lambda n: [refs.pop(0) for _ in range(n)]
    lefts = [take(halves) for _ in range(2)]
    wides = [[take(2) for _ in range(halves)] for _ in range(2)]
    own_ref, other_ref = take(2)
    turned = take(2)
    size = lefts[0][0].shape[0]

    @pl.when(pl.program_id(0) == 0)
    def _():
        for which in range(2):
            for i in range(halves):
                turned[which][:, pl.ds(i * size, size)] = lefts[which][i][...].T

    for which in range(2):
        for h, ref in enumerate((own_ref, other_ref)):
            full = jnp.concatenate([wides[which][i][h][...] for i in range(halves)], axis=0)
            ref[which, 0] = dot_nn(turned[which][...], full).astype(ref.dtype)


def expert_grad(me, rows, grad_rows, gups, acts, tensor_size):
    halves = len(rows)
    size, feat = rows[0].shape
    units = gups[0][0].shape[1]
    width = units // tensor_size
    same = pl.BlockSpec((size, feat), lambda j, me: (0, 0))
    part = pl.BlockSpec((size, width), lambda j, me: (0, me[0] ^ j))
    block = pl.BlockSpec((2, 1, feat, width), lambda j, me: (0, j, 0, 0))
    shape = (2, tensor_size, feat, width)
    wides = [a for pairs in (gups, acts) for pair in pairs for a in pair]
    return pl.pallas_call(
        functools.partial(expert_grad_kernel, halves),
        grid_spec=pltpu.PrefetchScalarGridSpec(
            num_scalar_prefetch=1,
            grid=(tensor_size,),
            in_specs=[same] * (2 * halves) + [part] * (4 * halves),
            out_specs=[block, block],
            scratch_shapes=[VMEM((feat, halves * size), BF16)] * 2,
        ),
        out_shape=[pltpu.HBM(shape, BF16), pltpu.HBM(shape, BF16)],
        compiler_params=pltpu.CompilerParams(
            vmem_limit_bytes=24 << 20, dimension_semantics=("arbitrary",)
        ),
        cost_estimate=cost(8 * halves * size * feat * units, 24 << 20),
    )(me.reshape(1), *[in_hbm(a) for a in (*rows, *grad_rows, *wides)])


def out_grad_kernel(core_ref, mixed_ref, low_ref, keep_ref, send_ref, full_ref):
    core = core_ref[0]
    parts, half, _ = keep_ref.shape
    full_ref[...] = dot_nn(mixed_ref[...], low_ref[...])
    for m in range(parts):
        near = pl.multiple_of((2 * m + core) * half, half)
        away = pl.multiple_of((2 * m + 1 - core) * half, half)
        keep_ref[m] = full_ref[pl.ds(near, half), :]
        send_ref[m] = full_ref[pl.ds(away, half), :].astype(BF16)


def qkv_grad_kernel(seqs, parts, core_ref, *refs):
    grads = [refs[s * parts : (s + 1) * parts] for s in range(seqs)]
    normed = refs[seqs * parts : seqs * parts + seqs]
    w_ref, keep_ref, send_ref, norm1_ref, full_ref, grad_ref, sems = refs[seqs * parts + seqs :]
    send_ref, extra_ref = send_ref.at[pl.ds(0, keep_ref.shape[0]), :], send_ref
    core = core_ref[0]
    shard = grads[0][0].shape[1]
    half = keep_ref.shape[0]
    pairs = []
    for s in range(seqs):
        for b in range(parts):
            pairs.append((grads[s][b], grad_ref.at[s, :, pl.ds(b * shard, shard)]))
    start_all(pairs, sems)()
    total = dot_nn(grad_ref[0], normed[0][...])
    for s in range(1, seqs):
        total += dot_nn(grad_ref[s], normed[s][...])
    full_ref[...] = total
    norm1 = jnp.sum(total * w_ref[...].astype(F32), axis=0, keepdims=True)
    norm1_ref[...] = norm1
    terms = jnp.concatenate([split_rows(norm1), split_rows(jnp.zeros_like(norm1))], axis=0)
    extra_ref[pl.ds(keep_ref.shape[0], 16), :] = terms
    keep_ref[...] = full_ref[pl.ds(pl.multiple_of(core * half, half), half), :]
    send_ref[...] = full_ref[pl.ds(pl.multiple_of((1 - core) * half, half), half), :].astype(BF16)


def program(tensor_size, expert_size):
    chips = expert_size // 2
    bits = chips.bit_length() - 1

    def over_tensor(values, mask):
        return lax.ppermute(values, "tensor", [(i, i ^ mask) for i in range(tensor_size)])

    def over_core(values):
        return lax.ppermute(values, "expert", [(i, i ^ 1) for i in range(expert_size)])

    def over_chip(values, mask):
        return lax.ppermute(values, "expert", [(i, i ^ (2 * mask)) for i in range(expert_size)])

    def from_tensor(blocks):
        return [blocks[0]] + [over_tensor(blocks[m], m) for m in range(1, tensor_size)]

    def swap_chips(blocks):
        if chips <= 4:
            return [blocks[0]] + [over_chip(blocks[m], m) for m in range(1, chips)]
        chip = lax.axis_index("expert") // 2
        order = chip ^ jnp.arange(chips)
        groups = [[2 * i + core for i in range(chips)] for core in range(2)]
        moved = lax.all_to_all(
            jnp.stack(blocks)[order],
            "expert",
            split_axis=0,
            concat_axis=0,
            tiled=True,
            axis_index_groups=groups,
        )[order]
        return [moved[m] for m in range(chips)]

    if chips == 4:
        masks = (1, 3)
    else:
        masks = tuple(1 << bit for bit in range(bits))

    def chip_bit(level):
        chip = lax.axis_index("expert") // 2
        if chips == 4:
            return ((chip ^ (chip >> 1)) & 1) if level == 0 else (chip >> 1) & 1
        return (chip >> level) & 1

    def halves(values, bit):
        half = values.shape[0] // 2
        low, high = values[:half], values[half:]
        return jnp.where(bit == 0, low, high), jnp.where(bit == 0, high, low)

    def joined(mine, theirs, bit):
        return jnp.concatenate(
            [jnp.where(bit == 0, mine, theirs), jnp.where(bit == 0, theirs, mine)], axis=0
        )

    def body(
        tokens,
        out_grad,
        masked,
        route,
        norm1_gain,
        query_key_value_weight,
        output_weight,
        norm2_gain,
        route_weight,
        expert_embed,
        up_weight,
        down_weight,
    ):
        seqs, shard, feat = tokens.shape
        rows_here = seqs * shard
        experts, router = expert_embed.shape
        cap = rows_here // experts
        channels = query_key_value_weight.shape[2]
        units = up_weight.shape[2]
        parts = tensor_size
        me = lax.axis_index("tensor")
        place_index = lax.axis_index("expert")
        chip, core = place_index // 2, place_index % 2
        gain1 = norm1_gain.reshape(1, feat)
        gain2 = norm2_gain.reshape(1, feat)

        w_rows = query_key_value_weight.transpose(0, 2, 1).reshape(3 * channels, feat)
        half_rows = 3 * channels // 2
        w_half = lax.dynamic_slice_in_dim(w_rows, core * half_rows, half_rows, axis=0)
        gathered = [from_tensor([tokens[0]] * parts)]
        for s in range(1, seqs):
            gathered.append(from_tensor([tie(tokens[s], gathered[-1])] * parts))

        picks = route.reshape(rows_here)
        expert_ids = jnp.arange(experts, dtype=jnp.int32)
        member = (picks[:, None] == expert_ids[None, :]).astype(jnp.int32)
        earlier = jnp.cumsum(member, axis=0) - member
        slot_ids = jnp.sum(earlier * member, axis=1)
        target = (picks ^ chip) * cap + slot_ids
        target = jnp.where(slot_ids < cap, target, -1)
        slot_range = jnp.arange(experts * cap, dtype=jnp.int32)
        placing = (slot_range[:, None] == target[None, :]).astype(BF16)
        member_t = (expert_ids[:, None] == picks[None, :]).astype(F32)
        cotangent = out_grad.reshape(rows_here, feat) * masked.reshape(rows_here, 1).astype(BF16)
        sent_cotangent = dot_nn(placing, cotangent).astype(BF16)
        if experts == 4:
            cot_one = over_chip(sent_cotangent[cap : 3 * cap], 1)
            cot_held = jnp.concatenate([sent_cotangent[3 * cap :], cot_one[cap:]], axis=0)
            slot_cotangent = [(sent_cotangent, 0), (cot_one, 0)]
        else:
            slot_cotangent = [
                (block, 0)
                for block in swap_chips(
                    [sent_cotangent[g * cap : (g + 1) * cap] for g in range(experts)]
                )
            ]

        normed, qkv, lse, mixed = [], [], [], []
        up_other, down_other = over_core(up_weight[0]), over_core(down_weight[0])
        for s in range(seqs):
            if s == 0:
                gathered[0] = tie(
                    gathered[0], sent_cotangent, member_t, w_half, up_other, down_other
                )
            if s == 1:
                gathered[s] = tie(gathered[s], slot_cotangent[1][0], lse[0])
                if experts == 4:
                    cot_two = over_chip(tie(cot_held, lse[0]), 3)
                    slot_cotangent += [(cot_two, 0), (cot_two, 1)]
            rider = (output_weight,) if s == 0 else ()
            n, q, l, blocks = attend(gathered[s], gain1, w_rows, *rider)
            normed.append(n)
            qkv.append(q)
            lse.append(l)
            mixed.append(from_tensor(blocks if s == 0 else tie(blocks, mixed[0][1:])))

        flat_tokens = tokens.reshape(rows_here, feat)
        route_t = route_weight.T
        ready = tie(mixed, [block for block, _ in slot_cotangent[1:]])
        copies = parts * (seqs + 1)
        hidden, gate, raw, mixed_all, out_weight_all, *packed = call(
            functools.partial(middle_kernel, seqs, parts, experts),
            [
                Far(SDS((rows_here, feat), F32)),
                Far(SDS((8, rows_here), F32)),
                Far(SDS((router, rows_here), F32)),
                Loose(SDS((feat, rows_here), BF16)),
                Loose(SDS((feat, feat), BF16)),
            ]
            + [SDS((cap + 8, feat), BF16)] * experts,
            [Far(flat_tokens), *[Free(b) for blocks in ready for b in blocks]]
            + [gain2, route_t, expert_embed, member_t, Far(placing)],
            4 * rows_here * feat * feat,
            scratch=[
                VMEM((feat, rows_here), BF16),
                VMEM((feat, feat), BF16),
                pltpu.SemaphoreType.DMA((copies,)),
                pltpu.SemaphoreType.DMA((2,)),
            ],
        )

        half = experts // 2
        expert_weights = (up_weight[0], up_other, down_weight[0], down_other)
        w_held = tie(w_half, packed)
        w_near = [over_tensor(w_held, m) for m in range(1, parts - 1)]
        if experts == 4:
            one = over_chip(packed[1], 1)
            held = tie(packed[2:], one)
            two, three = over_chip(held[0], 2), over_chip(held[1], 3)
            slot_rows = [(packed[0], 0), (one, 0)]
            low_half = expert(slot_rows[:2], slot_cotangent[:2], cap, *expert_weights, joined=(1,))
            near = over_chip(low_half[1][1], 1)
            three, two, w_near = tie((three, two, w_near), low_half[1])
            w_far = over_tensor(tie(w_half, w_near), parts - 1)
            high_half = expert([(three, 0), (two, 0)], slot_cotangent[2:], cap, *expert_weights)
        else:
            slot_rows = [(block, 0) for block in swap_chips(packed)]
            low_half = expert(slot_rows[:half], slot_cotangent[:half], cap, *expert_weights)
            high_half = expert(slot_rows[half:], slot_cotangent[half:], cap, *expert_weights)
            w_far = over_tensor(tie(w_half, w_near), parts - 1)
            near = ()
        results = [low_half, high_half]
        rows = [r[2] for r in results]
        grad_rows = [r[3] for r in results]
        acts = [r[4] for r in results]
        gups = [r[5] for r in results]
        w_mine = [*w_near, w_far]
        rows, near = tie((rows, near), w_far)
        grad_own, grad_send = expert_grad(me, rows, grad_rows, gups, acts, parts)
        if experts == 4:
            back_grad = [
                low_half[1][0],
                near,
                over_chip(high_half[1][1], 2),
                over_chip(high_half[1][0], 3),
            ]
        else:
            back_grad = swap_chips(low_half[1] + high_half[1])
        back_grad, grad_send, w_mine = tie((back_grad, grad_send, w_mine), grad_send)
        grad_recv = over_core(grad_send)
        w_theirs = over_core(jnp.concatenate(w_mine, axis=0))

        def first_pair(own, recv, mask):
            return jnp.stack(
                [own[m].astype(F32) + recv[m].astype(F32) for m in (mask, parts - 1)]
            ).astype(BF16)

        outs = call(
            functools.partial(back_kernel, seqs, parts, experts),
            [
                Far(SDS((rows_here, feat), F32)),
                Far(SDS((rows_here, feat), BF16)),
                SDS((router + 8 + -(-experts // 8) * 8, feat), F32),
            ]
            + [SDS((channels, rows_here), BF16)] * parts,
            [*back_grad, Far(cotangent), Far(hidden), Far(raw), Far(out_weight_all)]
            + [gain2, route_t, expert_embed, member_t, Far(placing)],
            4 * rows_here * feat * feat,
            scratch=[VMEM((rows_here, feat), BF16)],
        )
        grad_hidden, grad_low, stats = outs[:3]
        grad_mixed = from_tensor(outs[3:])
        if experts == 4:
            two, three = tie((high_half[0][1], high_half[0][0]), grad_mixed)
            back = [low_half[0][0], near, over_chip(two, 2), over_chip(three, 3)]
        else:
            back = swap_chips(low_half[0] + high_half[0])

        up_own, down_own = grad_own[0], grad_own[1]
        up_recv, down_recv = grad_recv[0], grad_recv[1]
        up_recv, down_recv = tie((up_recv, down_recv), grad_mixed[1])
        up_pair = first_pair(up_own, up_recv, 1)
        down_pair = first_pair(down_own, down_recv, 2 % parts)

        out_half = channels // 2
        out_keep, out_send = call(
            out_grad_kernel,
            [SDS((parts, out_half, feat), F32), SDS((parts, out_half, feat), BF16)],
            [Far(mixed_all), Far(tie(grad_low, up_pair, down_pair, grad_mixed[2:]))],
            2 * rows_here * feat * feat,
            [VMEM((feat, feat), F32)],
            scalar=core,
        )
        out_keep = out_keep + over_core(out_send).astype(F32)
        stat_high = lax.reduce_precision(stats, 8, 7)
        stat_low = lax.reduce_precision(stats - stat_high, 8, 7)
        stat_terms = jnp.concatenate([stat_high, stat_low], axis=0).astype(BF16)
        out_ride = [
            jnp.concatenate([out_keep[m].astype(BF16), stat_terms], axis=0) for m in range(1, parts)
        ]

        if parts == 4:
            up_got = over_tensor(tie(up_pair, grad_mixed), 1)
            down_got = over_tensor(tie(down_pair, grad_mixed), 2)
        else:
            up_got, down_got = (), ()

        def second(own, recv, got, mask):
            return (own[mask].astype(F32) + recv[mask].astype(F32) + got[1].astype(F32)).astype(BF16)

        def final(own, recv, got, last):
            total = own[0].astype(F32) + recv[0].astype(F32)
            return (total + got[0].astype(F32) + last.astype(F32))[None]

        def slow_scatter(own, recv):
            total = own[0].astype(F32) + recv[0].astype(F32)
            for m in range(1, parts):
                part = own[m].astype(F32) + recv[m].astype(F32)
                total = total + over_tensor(part.astype(BF16), m).astype(F32)
            return total[None]

        grads = []
        came = tie(grad_mixed, out_send)
        for s in range(seqs):
            if s == 1:
                came = tie(came, grads[0], back, w_theirs)
            grads.append(
                attend_back(qkv[s], lse[s], came, s, cover=COVER if s == 0 else 0)
            )
            if s == 0:
                out_held = tie(out_ride, grads[0])
                out_got = [over_tensor(out_held[m - 1], m) for m in range(1, parts)]
        split = 3 * channels // 2
        qkv_keep, qkv_send, norm1_grad = call(
            functools.partial(qkv_grad_kernel, seqs, parts),
            [SDS((split, feat), F32), SDS((split + 16, feat), BF16), SDS((1, feat), F32)],
            [Free(b) for blocks in tie(grads, up_got, down_got, out_got) for b in blocks]
            + [Far(n) for n in normed]
            + [Far(w_rows)],
            2 * seqs * parts * shard * 3 * channels * feat,
            [
                VMEM((3 * channels, feat), F32),
                VMEM((seqs, 3 * channels, parts * shard), BF16),
                pltpu.SemaphoreType.DMA((seqs * parts,)),
            ],
            scalar=core,
            cover=0,
        )
        out_half = out_keep.shape[1]
        out_part = sum((got[:out_half].astype(F32) for got in out_got), out_keep[0])
        size = stats.shape[0]

        def both_terms(terms):
            return terms[:size].astype(F32) + terms[size:].astype(F32)

        terms = [both_terms(t) for t in [stat_terms] + [got[out_half:] for got in out_got]]
        while len(terms) > 1:
            terms = [terms[i] + terms[i + 1] for i in range(0, len(terms), 2)]
        stats = terms[0] + over_core(terms[0])

        grad_blocks = [from_tensor(tie(grads[0], grads[-1]))]
        qkv_recv = over_core(qkv_send)
        (result,) = call(
            functools.partial(out_kernel, experts, cap),
            [Far(SDS((rows_here, feat), F32))],
            [Far(b) for b in tie(back, qkv_send)] + [Far(hidden), gate[:1].T, Far(placing)],
            2 * rows_here * rows_here * feat,
            cover=0,
        )

        def tail(s, *after):
            before = [Free(input_grads[-1])] if s > 0 else []
            (input_part,) = call(
                functools.partial(tail_kernel, parts),
                [Far(SDS((rows_here, feat), F32), (shard, feat), s)],
                [*map(Free, tie(grad_blocks[s], *after)), Free(w_rows), *map(Free, w_mine)]
                + [Free(w_theirs), Far(flat_tokens, (shard, feat), s), gain1]
                + [Far(grad_hidden, (shard, feat), s), *before],
                2 * shard * feat * 3 * channels * parts,
                [
                    VMEM((parts * 3 * channels, shard), BF16),
                    VMEM((parts * 3 * channels, feat), BF16),
                    pltpu.SemaphoreType.DMA((3 * parts - 1,)),
                ],
                scalar=core,
                aliases={2 * parts + 5: 0} if s > 0 else None,
            )
            return input_part

        qkv_keep, _ = tie((qkv_keep + qkv_recv[:split].astype(F32), result), result)
        norm1_grad = norm1_grad + jnp.sum(qkv_recv[split : split + 3].astype(F32), axis=0, keepdims=True)
        stats = stats + jnp.pad(norm1_grad, ((router + 2, size - router - 3), (0, 0)))
        values = jnp.concatenate([qkv_keep, out_part, stats], axis=0)
        values = jnp.pad(values, ((0, -values.shape[0] % (8 << bits)), (0, 0)))
        input_grads = []
        up_last = down_last = ()
        for level, mask in enumerate(masks):
            keep, send = halves(values, chip_bit(level))
            send = send.astype(BF16)
            came = over_chip(send, mask)
            if level == 0:
                grad_blocks.append(from_tensor(tie(grads[1], grad_blocks[0], send)))
                input_grads.append(tail(0, send))
                came, keep = tie((came, keep), input_grads[0])
            values = keep + came.astype(F32)
        summed = values.astype(BF16)
        if parts == 4:
            held = tie((up_got, down_got), grad_blocks[1], send)
            up_held = second(up_own, up_recv, held[0], 2)
            down_held = second(down_own, down_recv, held[1], 1)
            up_last = over_tensor(up_held, 2)
            down_last = over_tensor(down_held, 1)
            input_grads.append(tail(1, up_held, down_held, summed))
            up_last, down_last = tie((up_last, down_last), input_grads[1])
        else:
            input_grads.append(tail(1, summed))
        for level in reversed(range(bits)):
            summed = joined(summed, over_chip(summed, masks[level]), chip_bit(level))
        other_half = over_core(summed[: split + out_half])
        stats = summed[split + out_half :].astype(F32)
        norm1_grad = stats[router + 2 : router + 3]
        mask = 1
        while mask < tensor_size:
            norm1_grad = norm1_grad + over_tensor(norm1_grad, mask)
            mask *= 2
        query_key_value_gradient = (
            joined(summed[:split], other_half[:split], core)
            .reshape(3, channels, feat)
            .transpose(0, 2, 1)
            .astype(F32)
        )
        ends = slice(split, split + out_half)
        out_proj_grad = joined(summed[ends], other_half[ends], core).astype(F32)
        if parts == 4:
            up_weight_grad = final(up_own, up_recv, up_got, up_last)
            down_weight_grad = final(down_own, down_recv, down_got, down_last)
        else:
            up_weight_grad = slow_scatter(up_own, up_recv)
            down_weight_grad = slow_scatter(down_own, down_recv)
        route_grad = stats[:router].T
        norm2_grad = stats[router]
        norm1_grad = norm1_grad[0] / norm1_gain
        width, digits, stride = count_digits(rows_here, 2 * parts * experts)
        loads = sum(
            stats[router + 1, stride * i : stride * i + experts] * float(1 << (width * i))
            for i in range(digits)
        )
        embed_grad = stats[router + 8 : router + 8 + experts, :router]

        return (
            result.reshape(seqs, shard, feat),
            input_grads[-1].reshape(seqs, shard, feat),
            loads,
            norm1_grad,
            query_key_value_gradient,
            out_proj_grad,
            norm2_grad,
            route_grad,
            embed_grad,
            up_weight_grad,
            down_weight_grad,
        )

    return body


def solution(mesh):
    return jax.shard_map(
        program(mesh.shape["tensor"], mesh.shape["expert"]),
        mesh=mesh,
        in_specs=(
            P("expert", "tensor", None),
            P("expert", "tensor", None),
            P("expert", "tensor"),
            P("expert", "tensor", None),
            P(),
            P(None, None, "tensor"),
            P("tensor", None),
            P(),
            P(),
            P(),
            P("expert", None, None),
            P("expert", None, None),
        ),
        out_specs=(
            P("expert", "tensor", None),
            P("expert", "tensor", None),
            P(),
            P(),
            P(None, None, "tensor"),
            P("tensor", None),
            P(),
            P(),
            P(),
            P("expert", None, "tensor"),
            P("expert", None, "tensor"),
        ),
        check_vma=False,
    )
```

```python
import functools

import jax
import jax.numpy as jnp
from jax import lax
from jax.experimental import pallas as pl
from jax.experimental.pallas import tpu as pltpu
from jax.sharding import PartitionSpec as P

HEAD = 64
F32 = jnp.float32
BF16 = jnp.bfloat16
LOG2E = 1.4426950408889634
SCALE = HEAD**-0.5
EXACT = lax.Precision.HIGHEST
SDS = jax.ShapeDtypeStruct
VMEM = pltpu.VMEM
COVER = 4
LAST_COVER = 0

ERFC_SLOPE = 0.44
ERFC = (
    0.248227568,
    0.248777028,
    0.217859919,
    0.214130365,
    -0.0172025688,
    0.293641958,
    -0.276276279,
    0.0708421859,
)


def dot_nn(left, right, precision=None):
    return jnp.dot(left, right, preferred_element_type=F32, precision=precision)


def dot_nt(left, right, precision=None):
    return lax.dot_general(
        left, right, (((1,), (1,)), ((), ())), preferred_element_type=F32, precision=precision
    )


def dot_tn(left, right, precision=None):
    return lax.dot_general(
        left, right, (((0,), (0,)), ((), ())), preferred_element_type=F32, precision=precision
    )


class Far:
    def __init__(self, value, block=None, at=0):
        self.value = value
        self.block = value.shape if block is None else block
        self.at = at


class Here(Far):
    pass


class Loose(Far):
    pass


class Free(Far):
    pass


def start_all(pairs, sems):
    copies = [pltpu.make_async_copy(a, b, sems.at[i]) for i, (a, b) in enumerate(pairs)]
    for copy in copies:
        copy.start()

    def wait():
        for copy in copies:
            copy.wait()

    return wait


def plain(value):
    return value.value if isinstance(value, Far) else value


def in_hbm(value):
    return pltpu.with_memory_space_constraint(value, pltpu.HBM)


def cost(flops, size, transcendentals=0, cover=COVER):
    return pl.CostEstimate(
        flops=flops * cover, bytes_accessed=size * cover, transcendentals=transcendentals * cover
    )


def call(kernel, outs, args, flops, scratch=(), limit=24, transcendentals=0, scalar=None, cover=COVER, aliases=None):
    whole = pl.BlockSpec(memory_space=VMEM)

    def spec(arg):
        if isinstance(arg, Loose):
            return pl.BlockSpec(memory_space=pl.ANY)
        if not isinstance(arg, Far):
            return whole
        if isinstance(arg, (Loose, Free)):
            return pl.BlockSpec(memory_space=pl.ANY)
        where = arg.at if isinstance(arg.at, tuple) else (arg.at,)
        where += (0,) * (arg.value.ndim - len(where))
        return pl.BlockSpec(
            arg.block, lambda i: where, pipeline_mode=pl.Buffered(buffer_count=1)
        )

    specs = [spec(a) for a in args]
    out_specs = [spec(o) for o in outs]
    size = sum(a.size * a.dtype.itemsize for a in map(plain, args))
    size += sum(o.size * o.dtype.itemsize for o in map(plain, outs))
    args = [
        a.value if isinstance(a, (Free, Here)) else in_hbm(a.value) if isinstance(a, Far) else a for a in args
    ]
    outs = [pltpu.HBM(o.value.shape, o.value.dtype) if isinstance(o, Far) else o for o in outs]
    if scalar is not None:
        specs = [pl.BlockSpec(memory_space=pltpu.SMEM)] + specs
        args = [scalar.reshape(1)] + args
    return pl.pallas_call(
        kernel,
        grid=(1,),
        out_shape=list(outs),
        in_specs=specs,
        out_specs=out_specs,
        scratch_shapes=list(scratch),
        input_output_aliases=aliases or {},
        compiler_params=pltpu.CompilerParams(vmem_limit_bytes=limit << 20),
        cost_estimate=cost(flops, size, transcendentals, cover),
    )(*args)


def centred(x):
    cen = x - jnp.mean(x, axis=1, keepdims=True)
    return cen, lax.rsqrt(jnp.mean(cen * cen, axis=1, keepdims=True) + 1e-05)


def tie(values, *after):
    return lax.optimization_barrier((values, after))[0]


def attend_kernel(parts, pieces, channels, riding, *refs):
    tok = refs[: sum(pieces)]
    refs = refs[sum(pieces) :]
    gain_ref, w_ref = refs[:2]
    rider = refs[2 : 2 + riding]
    refs = refs[2 + riding :]
    normed_out, qkv_out, lse_ref = refs[:3]
    mixed = refs[3 : 3 + parts]
    normed_ref, qkv_ref, sems = refs[3 + parts :]
    shard = tok[0].shape[0]
    for ref in rider:
        for b in range(parts):
            mixed[b][:, pl.ds(shard, ref.shape[1])] = ref[...]
    at = 0
    for ref in tok:
        size = ref.shape[0]
        cen, inv = centred(ref[...].astype(F32))
        rows = (cen * inv * gain_ref[...]).astype(BF16)
        normed_ref[pl.ds(at, size), :] = rows
        qkv_ref[:, pl.ds(at, size)] = dot_nt(w_ref[...], rows).astype(BF16)
        at += size
    copies = [
        pltpu.make_async_copy(normed_ref, normed_out, sems.at[0]),
        pltpu.make_async_copy(qkv_ref, qkv_out, sems.at[1]),
    ]
    for copy in copies:
        copy.start()
    size = 128
    chunks = parts * shard // size

    def head(h, carry):
        off = pl.multiple_of(h * HEAD, HEAD)
        key = qkv_ref[pl.ds(channels + off, HEAD), :].T
        value_t = qkv_ref[pl.ds(2 * channels + off, HEAD), :]
        for b in range(parts):
            query_t = qkv_ref[pl.ds(off, HEAD), pl.ds(b * shard, shard)]
            scores = [dot_nn(key[i * size : (i + 1) * size], query_t) for i in range(chunks)]
            top = None
            for score in scores:
                part = jnp.max(score.reshape(size // 8, 8, shard), axis=0)
                top = part if top is None else jnp.maximum(top, part)
            top = jnp.max(top, axis=0, keepdims=True) * (SCALE * LOG2E)
            total, out = None, None
            for i, score in enumerate(scores):
                expos = jnp.exp2(score * (SCALE * LOG2E) - top)
                part = jnp.sum(expos.reshape(size // 8, 8, shard), axis=0)
                term = dot_nn(value_t[:, i * size : (i + 1) * size], expos.astype(BF16))
                total = part if i == 0 else total + part
                out = term if i == 0 else out + term
            total = jnp.sum(total, axis=0, keepdims=True)
            mixed[b][pl.ds(off, HEAD), pl.ds(0, shard)] = (out * (1.0 / total)).astype(BF16)
            lse_ref[pl.ds(h, 1), pl.ds(b * shard, shard)] = top + jnp.log2(total)
        return carry

    lax.fori_loop(0, channels // HEAD, head, 0)
    for copy in copies:
        copy.wait()


def attend(tok, gain, w_rows, *rider):
    parts = len(tok)
    shard, feat = tok[0].shape
    length = parts * shard
    channels = w_rows.shape[0] // 3
    pieces = [len(block) if isinstance(block, tuple) else 1 for block in tok]
    tok = jax.tree.leaves(tok)
    outs = call(
        functools.partial(attend_kernel, parts, pieces, channels, len(rider)),
        [
            Loose(SDS((length, feat), BF16)),
            Loose(SDS((3 * channels, length), BF16)),
            Far(SDS((8, length), F32)),
        ]
        + [SDS((channels, shard + sum(r.shape[1] for r in rider)), BF16)] * parts,
        [*tok, gain, Far(w_rows), *[Far(r) for r in rider]],
        2 * length * feat * 3 * channels + 4 * length * length * channels,
        scratch=[
            VMEM((length, feat), BF16),
            VMEM((3 * channels, length), BF16),
            pltpu.SemaphoreType.DMA((2,)),
        ],
        transcendentals=length * length * channels // HEAD,
    )
    return outs[0], outs[1], outs[2], outs[3:]


def attend_back_kernel(parts, channels, at, *refs):
    qkv_ref, lse_ref = refs[:2]
    shard = qkv_ref.shape[1] // parts
    grad = [ref.at[:, pl.ds(at * shard, shard)] for ref in refs[2 : 2 + parts]]
    refs = refs[2 + parts :]
    outs = refs[:parts]
    key_acc, value_acc = refs[parts:]

    def head(h, carry):
        off = pl.multiple_of(h * HEAD, HEAD)
        key_t = qkv_ref[pl.ds(channels + off, HEAD), :]
        key = key_t.T
        value = qkv_ref[pl.ds(2 * channels + off, HEAD), :].T
        for b in range(parts):
            query_t = qkv_ref[pl.ds(off, HEAD), pl.ds(b * shard, shard)]
            grad_t = grad[b][pl.ds(off, HEAD), :]
            scores = dot_nn(key, query_t)
            probs = jnp.exp2(
                scores * (SCALE * LOG2E) - lse_ref[pl.ds(h, 1), pl.ds(b * shard, shard)]
            )
            grad_probs = dot_nn(value, grad_t)
            inner = jnp.sum(probs * grad_probs, axis=0, keepdims=True)
            grad_scores = (probs * (grad_probs - inner)).astype(BF16)
            value_part = dot_nt(grad_t, probs.astype(BF16))
            key_part = dot_nt(query_t, grad_scores)
            outs[b][pl.ds(off, HEAD), :] = (dot_nn(key_t, grad_scores) * SCALE).astype(BF16)
            if b == 0:
                key_acc[...] = key_part
                value_acc[...] = value_part
            else:
                key_acc[...] += key_part
                value_acc[...] += value_part
        for b in range(parts):
            cols = pl.ds(b * shard, shard)
            outs[b][pl.ds(channels + off, HEAD), :] = (key_acc[:, cols] * SCALE).astype(BF16)
            outs[b][pl.ds(2 * channels + off, HEAD), :] = value_acc[:, cols].astype(BF16)
        return carry

    lax.fori_loop(0, channels // HEAD, head, 0)


def attend_back(qkv, lse, grad, at, cover):
    parts = len(grad)
    channels = grad[0].shape[0]
    length = qkv.shape[1]
    shard = length // parts
    return call(
        functools.partial(attend_back_kernel, parts, channels, at),
        [SDS((3 * channels, shard), BF16)] * parts,
        [Far(qkv), Far(lse), *[Far(g) for g in grad]],
        10 * length * length * channels,
        scratch=[VMEM((HEAD, length), F32)] * 2,
        transcendentals=length * length * channels // HEAD,
        cover=cover,
    )


def gate_parts(raw, embed, member):
    inv = lax.rsqrt(jnp.sum(raw * raw, axis=0, keepdims=True) + 1e-06)
    rows = raw * inv
    embed_inv = lax.rsqrt(jnp.sum(embed * embed, axis=1, keepdims=True) + 1e-06)
    centers = embed * embed_inv
    logits = 3.0 * dot_nn(centers, rows, EXACT)
    expos = jnp.exp(logits - jnp.max(logits, axis=0, keepdims=True))
    probs = expos / jnp.sum(expos, axis=0, keepdims=True)
    gate = jnp.sum(probs * member, axis=0, keepdims=True)
    return inv, rows, embed_inv, centers, probs, gate


def split_rows(row):
    first = row.astype(BF16).astype(F32)
    second = (row - first).astype(BF16).astype(F32)
    third = (row - first) - second
    shape = (8, row.shape[1])
    at = lax.broadcasted_iota(jnp.int32, shape, 0)
    parts = jnp.where(at == 0, first, jnp.where(at == 1, second, jnp.where(at == 2, third, 0.0)))
    return parts.astype(BF16)


def middle_kernel(seqs, parts, groups, *refs):
    refs = list(refs)
    take = lambda n: [refs.pop(0) for _ in range(n)]
    (tok_ref,) = take(1)
    mixed = [take(parts) for _ in range(seqs)]
    gain_ref, route_ref, embed_ref, member_ref, place_ref = take(5)
    hidden_ref, gate_ref, raw_ref, mixed_out, weight_out = take(5)
    packed = take(groups)
    mixed_ref, weight_ref, in_sems, out_sems = take(4)
    rows, feat = tok_ref.shape
    shard = rows // seqs
    channels = mixed[1][0].shape[0]
    cap = rows // groups
    pairs = []
    for m in range(parts):
        at = pl.ds(m * channels, channels)
        pairs.append((mixed[0][m].at[:, pl.ds(shard, feat)], weight_ref.at[at, :]))
        for s in range(seqs):
            pairs.append(
                (mixed[s][m].at[:, pl.ds(0, shard)], mixed_ref.at[at, pl.ds(s * shard, shard)])
            )
    start_all(pairs, in_sems)()
    wait = start_all([(mixed_ref, mixed_out), (weight_ref, weight_out)], out_sems)
    attn = dot_tn(mixed_ref[...], weight_ref[...])
    hidden = tok_ref[...].astype(F32) + attn
    hidden_ref[...] = hidden
    cen, inv = centred(hidden)
    normed = cen * inv * gain_ref[...]
    raw = dot_nt(route_ref[...], normed, EXACT)
    raw_ref[...] = raw
    gate = gate_parts(raw, embed_ref[...], member_ref[...])[-1]
    gate_ref[...] = jnp.broadcast_to(gate, gate_ref.shape)
    low = normed.astype(BF16)
    scalars = split_rows(gate)
    for g in range(groups):
        place = place_ref[pl.ds(g * cap, cap), :]
        packed[g][pl.ds(0, cap), :] = dot_nn(place, low).astype(BF16)
        packed[g][pl.ds(cap, 8), :] = jnp.zeros((8, feat), BF16)
        packed[g][pl.ds(cap, 8), pl.ds(0, cap)] = dot_nt(scalars, place).astype(BF16)
    wait()


def count_digits(rows, devices):
    width = max(1, (256 // devices + 1).bit_length() - 1)
    digits = -(-rows.bit_length() // width)
    return width, digits, 128 if digits <= 6 else 64


def back_kernel(seqs, parts, groups, *refs):
    refs = list(refs)
    take = lambda n: [refs.pop(0) for _ in range(n)]
    packed = take(groups)
    cot_ref, hidden_ref, raw_ref, weight_ref = take(4)
    gain_ref, route_ref, embed_ref, member_ref, place_ref = take(5)
    grad_ref, low_ref, stats_ref = take(3)
    mixed_grad = take(parts)
    (slot_ref,) = take(1)
    rows = hidden_ref.shape[0]
    shard = rows // seqs
    cap = rows // groups
    channels = mixed_grad[0].shape[0]
    scalars = None
    for g in range(groups):
        slot_ref[pl.ds(g * cap, cap), :] = packed[g][pl.ds(0, cap), :]
        scalar = dot_nn(packed[g][pl.ds(cap, 8), pl.ds(0, cap)], place_ref[pl.ds(g * cap, cap), :])
        scalars = scalar if g == 0 else scalars + scalar
    at = lax.broadcasted_iota(jnp.int32, scalars.shape, 0)
    grad_gate = jnp.sum(jnp.where(at < 3, scalars, 0.0), axis=0, keepdims=True)
    cen, inv = centred(hidden_ref[...])
    unit = cen * inv
    gain = gain_ref[...]
    raw_inv, dirs, embed_inv, centers, probs, gate = gate_parts(
        raw_ref[...], embed_ref[...], member_ref[...]
    )
    grad_logits = (3.0 * grad_gate * gate) * (member_ref[...] - probs)
    grad_dirs = dot_tn(centers, grad_logits, EXACT)
    grad_centers = dot_nt(grad_logits, dirs, EXACT)
    grad_raw = raw_inv * (
        grad_dirs - dirs * jnp.sum(dirs * grad_dirs, axis=0, keepdims=True)
    )
    router = route_ref.shape[0]
    experts = embed_ref.shape[0]
    stats_ref[...] = jnp.zeros(stats_ref.shape, F32)
    stats_ref[pl.ds(router + 8, experts), pl.ds(0, router)] = embed_inv * (
        grad_centers - centers * jnp.sum(centers * grad_centers, axis=1, keepdims=True)
    )
    stats_ref[pl.ds(0, router), :] = dot_nn(grad_raw, unit * gain, EXACT)
    count = dot_nt(jnp.ones((8, rows), F32), member_ref[...], EXACT)[:1].astype(jnp.int32)
    width, digits, stride = count_digits(rows, 2 * parts * groups)
    for digit in range(digits):
        part = (count >> (width * digit)) & ((1 << width) - 1)
        stats_ref[pl.ds(router + 1, 1), pl.ds(stride * digit, experts)] = part.astype(F32)
    grad_normed = dot_tn(place_ref[...], slot_ref[...]) + dot_tn(grad_raw, route_ref[...], EXACT)
    stats_ref[pl.ds(router, 1), :] = jnp.sum(grad_normed * unit, axis=0, keepdims=True)
    grad_unit = grad_normed * gain
    grad_hidden = inv * (
        grad_unit
        - jnp.mean(grad_unit, axis=1, keepdims=True)
        - unit * jnp.mean(grad_unit * unit, axis=1, keepdims=True)
    )
    grad_hidden = cot_ref[...].astype(F32) + grad_hidden
    grad_ref[...] = grad_hidden
    low = grad_hidden.astype(BF16)
    low_ref[...] = low
    grad_mixed = dot_nt(weight_ref[...], low).astype(BF16)
    for m in range(parts):
        mixed_grad[m][...] = grad_mixed[m * channels : (m + 1) * channels]


def out_kernel(groups, cap, *refs):
    back = refs[:groups]
    hidden_ref, gate_ref, place_ref, out_ref = refs[groups:]
    mixture = None
    for g in range(groups):
        rows = back[g][pl.ds(back[g].shape[0] - cap, cap), :]
        part = dot_tn(place_ref[pl.ds(g * cap, cap), :], rows)
        mixture = part if g == 0 else mixture + part
    out_ref[...] = hidden_ref[...] + gate_ref[...].T[:, :1] * mixture


def tail_kernel(parts, core_ref, *refs):
    refs = list(refs)
    take = lambda n: [refs.pop(0) for _ in range(n)]
    grads = take(parts)
    (weight,) = take(1)
    mine = take(parts - 1)
    theirs, tok_ref, gain_ref, hidden_grad_ref = take(4)
    out_ref, grad_ref, weight_ref, sems = refs[-4:]
    core = core_ref[0]
    rows = weight.shape[0]
    half = rows // 2
    pairs = [(grads[m], grad_ref.at[pl.ds(m * rows, rows), :]) for m in range(parts)]
    pairs.append((weight, weight_ref.at[pl.ds(0, rows), :]))
    for m in range(1, parts):
        near = pl.multiple_of(m * rows + core * half, 16)
        away = pl.multiple_of(m * rows + (1 - core) * half, 16)
        pairs.append((mine[m - 1], weight_ref.at[pl.ds(near, half), :]))
        pairs.append((theirs.at[pl.ds((m - 1) * half, half), :], weight_ref.at[pl.ds(away, half), :]))
    start_all(pairs, sems)()
    grad_normed = dot_tn(grad_ref[...], weight_ref[...])
    cen, inv = centred(tok_ref[...].astype(F32))
    unit = cen * inv
    grad_unit = grad_normed * gain_ref[...]
    out_ref[...] = hidden_grad_ref[...] + inv * (
        grad_unit
        - jnp.mean(grad_unit, axis=1, keepdims=True)
        - unit * jnp.mean(grad_unit * unit, axis=1, keepdims=True)
    )


def gelu_pair(x):
    z = jnp.abs(x) * (0.5**0.5)
    t = 1.0 / (1.0 + ERFC_SLOPE * z)
    poly = jnp.full_like(t, ERFC[-1])
    for value in ERFC[-2::-1]:
        poly = poly * t + value
    bell = jnp.exp2(x * x * (-0.5 * LOG2E))
    tail = (0.5 * bell) * (t * poly)
    cdf = jnp.where(x < 0.0, tail, 1.0 - tail)
    return x * cdf, cdf + x * (bell * 0.3989422804014327)


def expert_kernel(count, steps, *refs):
    refs = list(refs)
    take = lambda n: [refs.pop(0) for _ in range(n)]
    packed, cot = take(count), take(count)
    ups, downs = take(2), take(2)
    cap = cot[0].shape[0]
    returned, grads = [], []
    for i in range(count):
        (ref,) = take(1)
        if ref.shape[0] == cap:
            returned.append(ref)
            grads += take(1)
        else:
            grads.append(ref.at[pl.ds(0, cap + 8), :])
            returned.append(ref.at[pl.ds(cap + 8, cap), :])
    rows_ref, gr_ref = take(2)
    acts, gups = take(2), take(2)
    ret_acc, grad_acc = take(2)
    step = pl.program_id(0)

    def eye():
        shape = (cap, cap)
        return lax.broadcasted_iota(jnp.int32, shape, 0) == lax.broadcasted_iota(jnp.int32, shape, 1)

    @pl.when(step == 0)
    def _():
        for i in range(count):
            part = pl.ds(i * cap, cap)
            rows_ref[part, :] = packed[i][pl.ds(0, cap), :]
            scalars = packed[i][pl.ds(cap, 8), pl.ds(0, cap)].astype(F32)
            at = lax.broadcasted_iota(jnp.int32, scalars.shape, 0)
            row = jnp.sum(jnp.where(at < 3, scalars, 0.0), axis=0, keepdims=True)
            gate = jnp.sum(jnp.where(eye(), row, 0.0), axis=1, keepdims=True)
            gr_ref[part, :] = (gate * cot[i][...].astype(F32)).astype(BF16)

    rows, grad_rows = rows_ref[...], gr_ref[...]
    ret = None
    for h in range(2):
        up_w, down_w = ups[h][...], downs[h][...]
        act, slope = gelu_pair(dot_nn(rows, up_w))
        act = act.astype(BF16)
        gup = (dot_nn(grad_rows, down_w) * slope).astype(BF16)
        acts[h][...] = act
        gups[h][...] = gup
        ret_part = dot_nt(act, down_w)
        grad_part = dot_nt(gup, up_w)
        ret = ret_part if h == 0 else ret + ret_part
        grad = grad_part if h == 0 else grad + grad_part

    @pl.when(step == 0)
    def _():
        ret_acc[...] = ret
        grad_acc[...] = grad

    @pl.when(step > 0)
    def _():
        ret_acc[...] += ret
        grad_acc[...] += grad

    @pl.when(step == steps - 1)
    def _():
        for i in range(count):
            part = pl.ds(i * cap, cap)
            low = ret_acc[part, :].astype(BF16)
            returned[i][...] = low
            product = jnp.sum(low.astype(F32) * cot[i][...].astype(F32), axis=1, keepdims=True)
            row = jnp.sum(jnp.where(eye(), product, 0.0), axis=0, keepdims=True)
            grads[i][pl.ds(0, cap), :] = grad_acc[part, :].astype(BF16)
            grads[i][pl.ds(cap, 8), :] = jnp.zeros((8, grads[i].shape[1]), BF16)
            grads[i][pl.ds(cap, 8), pl.ds(0, cap)] = split_rows(row)


def expert(packed, cot, cap, up_own, up_other, down_own, down_other, joined=()):
    count = len(cot)
    feat, units = up_own.shape
    width = 512 if units % 512 == 0 else units
    steps = units // width
    rows = count * cap

    def same(size, at=0):
        return pl.BlockSpec((size, feat), lambda j: (at, 0))

    weight = pl.BlockSpec((feat, width), lambda j: (0, j))
    wide = pl.BlockSpec((rows, width), lambda j: (0, j))
    sizes = []
    for i in range(count):
        sizes += [2 * cap + 8] if i in joined else [cap, cap + 8]
    outs = pl.pallas_call(
        functools.partial(expert_kernel, count, steps),
        grid=(steps,),
        in_specs=[same(cap + 8, at) for _, at in packed]
        + [same(cap, at) for _, at in cot]
        + [weight] * 4,
        out_specs=[same(size) for size in sizes] + [same(rows)] * 2 + [wide] * 4,
        out_shape=[SDS((size, feat), BF16) for size in sizes]
        + [pltpu.HBM((rows, feat), BF16)] * 2
        + [pltpu.HBM((rows, units), BF16)] * 4,
        scratch_shapes=[VMEM((rows, feat), F32)] * 2,
        compiler_params=pltpu.CompilerParams(
            vmem_limit_bytes=24 << 20, dimension_semantics=("arbitrary",)
        ),
        cost_estimate=cost(
            16 * rows * feat * units, 8 * feat * units + 16 * rows * units, 4 * rows * units
        ),
    )(
        *[a for a, _ in packed],
        *[in_hbm(a) for a, _ in cot],
        *[in_hbm(w) for w in (up_own, up_other, down_own, down_other)],
    )
    back, grads = [], []
    at = 0
    for i in range(count):
        back.append(outs[at])
        if i not in joined:
            at += 1
        grads.append(outs[at])
        at += 1
    return back, grads, outs[at], outs[at + 1], outs[at + 2 : at + 4], outs[at + 4 :]


def expert_grad_kernel(halves, me_ref, *refs):
    refs = list(refs)
    take = lambda n: [refs.pop(0) for _ in range(n)]
    lefts = [take(halves) for _ in range(2)]
    wides = [[take(2) for _ in range(halves)] for _ in range(2)]
    own_ref, other_ref = take(2)
    turned = take(2)
    size = lefts[0][0].shape[0]

    @pl.when(pl.program_id(0) == 0)
    def _():
        for which in range(2):
            for i in range(halves):
                turned[which][:, pl.ds(i * size, size)] = lefts[which][i][...].T

    for which in range(2):
        for h, ref in enumerate((own_ref, other_ref)):
            full = jnp.concatenate([wides[which][i][h][...] for i in range(halves)], axis=0)
            ref[which, 0] = dot_nn(turned[which][...], full).astype(ref.dtype)


def expert_grad(me, rows, grad_rows, gups, acts, tensor_size):
    halves = len(rows)
    size, feat = rows[0].shape
    units = gups[0][0].shape[1]
    width = units // tensor_size
    same = pl.BlockSpec((size, feat), lambda j, me: (0, 0))
    part = pl.BlockSpec((size, width), lambda j, me: (0, me[0] ^ j))
    block = pl.BlockSpec((2, 1, feat, width), lambda j, me: (0, j, 0, 0))
    shape = (2, tensor_size, feat, width)
    wides = [a for pairs in (gups, acts) for pair in pairs for a in pair]
    return pl.pallas_call(
        functools.partial(expert_grad_kernel, halves),
        grid_spec=pltpu.PrefetchScalarGridSpec(
            num_scalar_prefetch=1,
            grid=(tensor_size,),
            in_specs=[same] * (2 * halves) + [part] * (4 * halves),
            out_specs=[block, block],
            scratch_shapes=[VMEM((feat, halves * size), BF16)] * 2,
        ),
        out_shape=[pltpu.HBM(shape, BF16), pltpu.HBM(shape, BF16)],
        compiler_params=pltpu.CompilerParams(
            vmem_limit_bytes=24 << 20, dimension_semantics=("arbitrary",)
        ),
        cost_estimate=cost(8 * halves * size * feat * units, 24 << 20),
    )(me.reshape(1), *[in_hbm(a) for a in (*rows, *grad_rows, *wides)])


def pair_kernel(*refs):
    for i in range(2):
        for j in range(2):
            own, recv = refs[4 * i + 2 * j : 4 * i + 2 * j + 2]
            refs[8 + i][j] = (own[0, 0].astype(F32) + recv[0, 0].astype(F32)).astype(BF16)


def first_pairs(own, recv, picks):
    feat, width = own.shape[2:]
    block = (1, 1, feat, width)
    args = []
    for which in range(2):
        for m in picks[which]:
            args += [Far(own, block, (which, m)), Here(recv, block, (which, m))]
    return call(pair_kernel, [SDS((2, feat, width), BF16)] * 2, args, 4 * feat * width)


def out_grad_kernel(core_ref, mixed_ref, low_ref, keep_ref, send_ref, full_ref):
    core = core_ref[0]
    parts, half, _ = keep_ref.shape
    full_ref[...] = dot_nn(mixed_ref[...], low_ref[...])
    for m in range(parts):
        near = pl.multiple_of((2 * m + core) * half, half)
        away = pl.multiple_of((2 * m + 1 - core) * half, half)
        keep_ref[m] = full_ref[pl.ds(near, half), :]
        send_ref[m] = full_ref[pl.ds(away, half), :].astype(BF16)


def qkv_grad_kernel(seqs, parts, core_ref, *refs):
    grads = [refs[s * parts : (s + 1) * parts] for s in range(seqs)]
    normed = refs[seqs * parts : seqs * parts + seqs]
    w_ref, keep_ref, send_ref, norm1_ref, full_ref, grad_ref, sems = refs[seqs * parts + seqs :]
    send_ref, extra_ref = send_ref.at[pl.ds(0, keep_ref.shape[0]), :], send_ref
    core = core_ref[0]
    shard = grads[0][0].shape[1]
    half = keep_ref.shape[0]
    pairs = []
    for s in range(seqs):
        for b in range(parts):
            pairs.append((grads[s][b], grad_ref.at[s, :, pl.ds(b * shard, shard)]))
    start_all(pairs, sems)()
    total = dot_nn(grad_ref[0], normed[0][...])
    for s in range(1, seqs):
        total += dot_nn(grad_ref[s], normed[s][...])
    full_ref[...] = total
    norm1 = jnp.sum(total * w_ref[...].astype(F32), axis=0, keepdims=True)
    norm1_ref[...] = norm1
    terms = jnp.concatenate([split_rows(norm1), split_rows(jnp.zeros_like(norm1))], axis=0)
    extra_ref[pl.ds(keep_ref.shape[0], 16), :] = terms
    keep_ref[...] = full_ref[pl.ds(pl.multiple_of(core * half, half), half), :]
    send_ref[...] = full_ref[pl.ds(pl.multiple_of((1 - core) * half, half), half), :].astype(BF16)


def program(tensor_size, expert_size):
    chips = expert_size // 2
    bits = chips.bit_length() - 1

    def over_tensor(values, mask):
        return lax.ppermute(values, "tensor", [(i, i ^ mask) for i in range(tensor_size)])

    def over_core(values):
        return lax.ppermute(values, "expert", [(i, i ^ 1) for i in range(expert_size)])

    def over_chip(values, mask):
        return lax.ppermute(values, "expert", [(i, i ^ (2 * mask)) for i in range(expert_size)])

    def from_tensor(blocks):
        return [blocks[0]] + [over_tensor(blocks[m], m) for m in range(1, tensor_size)]

    def gather_first(block):
        if tensor_size != 4:
            return from_tensor([block] * tensor_size)
        half = block.shape[0] // 2
        one, two = over_tensor(block, 1), over_tensor(block, 2)
        low, high = over_tensor(one[:half], 2), over_tensor(two[half:], 1)
        return [block, one, two, (low, high)]

    def swap_chips(blocks):
        if chips <= 4:
            return [blocks[0]] + [over_chip(blocks[m], m) for m in range(1, chips)]
        chip = lax.axis_index("expert") // 2
        order = chip ^ jnp.arange(chips)
        groups = [[2 * i + core for i in range(chips)] for core in range(2)]
        moved = lax.all_to_all(
            jnp.stack(blocks)[order],
            "expert",
            split_axis=0,
            concat_axis=0,
            tiled=True,
            axis_index_groups=groups,
        )[order]
        return [moved[m] for m in range(chips)]

    if chips == 4:
        masks = (1, 3)
    else:
        masks = tuple(1 << bit for bit in range(bits))

    def chip_bit(level):
        chip = lax.axis_index("expert") // 2
        if chips == 4:
            return ((chip ^ (chip >> 1)) & 1) if level == 0 else (chip >> 1) & 1
        return (chip >> level) & 1

    def halves(values, bit):
        half = values.shape[0] // 2
        low, high = values[:half], values[half:]
        return jnp.where(bit == 0, low, high), jnp.where(bit == 0, high, low)

    def joined(mine, theirs, bit):
        return jnp.concatenate(
            [jnp.where(bit == 0, mine, theirs), jnp.where(bit == 0, theirs, mine)], axis=0
        )

    def body(
        tokens,
        out_grad,
        masked,
        route,
        norm1_gain,
        query_key_value_weight,
        output_weight,
        norm2_gain,
        route_weight,
        expert_embed,
        up_weight,
        down_weight,
    ):
        seqs, shard, feat = tokens.shape
        rows_here = seqs * shard
        experts, router = expert_embed.shape
        cap = rows_here // experts
        channels = query_key_value_weight.shape[2]
        units = up_weight.shape[2]
        parts = tensor_size
        me = lax.axis_index("tensor")
        place_index = lax.axis_index("expert")
        chip, core = place_index // 2, place_index % 2
        gain1 = norm1_gain.reshape(1, feat)
        gain2 = norm2_gain.reshape(1, feat)

        w_rows = query_key_value_weight.transpose(0, 2, 1).reshape(3 * channels, feat)
        half_rows = 3 * channels // 2
        w_half = lax.dynamic_slice_in_dim(w_rows, core * half_rows, half_rows, axis=0)
        gathered = [gather_first(tokens[0])]
        for s in range(1, seqs):
            gathered.append(from_tensor([tie(tokens[s], gathered[-1])] * parts))

        picks = route.reshape(rows_here)
        expert_ids = jnp.arange(experts, dtype=jnp.int32)
        member = (picks[:, None] == expert_ids[None, :]).astype(jnp.int32)
        earlier = jnp.cumsum(member, axis=0) - member
        slot_ids = jnp.sum(earlier * member, axis=1)
        target = (picks ^ chip) * cap + slot_ids
        target = jnp.where(slot_ids < cap, target, -1)
        slot_range = jnp.arange(experts * cap, dtype=jnp.int32)
        placing = (slot_range[:, None] == target[None, :]).astype(BF16)
        member_t = (expert_ids[:, None] == picks[None, :]).astype(F32)
        cotangent = out_grad.reshape(rows_here, feat) * masked.reshape(rows_here, 1).astype(BF16)
        sent_cotangent = dot_nn(placing, cotangent).astype(BF16)
        if experts == 4:
            cot_one = over_chip(sent_cotangent[cap : 3 * cap], 1)
            cot_held = jnp.concatenate([sent_cotangent[3 * cap :], cot_one[cap:]], axis=0)
            slot_cotangent = [(sent_cotangent, 0), (cot_one, 0)]
        else:
            slot_cotangent = [
                (block, 0)
                for block in swap_chips(
                    [sent_cotangent[g * cap : (g + 1) * cap] for g in range(experts)]
                )
            ]

        normed, qkv, lse, mixed = [], [], [], []
        up_other, down_other = over_core(up_weight[0]), over_core(down_weight[0])
        for s in range(seqs):
            if s == 0:
                gathered[0] = tie(
                    gathered[0], sent_cotangent, member_t, w_half, up_other, down_other
                )
            if s == 1:
                gathered[s] = tie(gathered[s], slot_cotangent[1][0], lse[0])
                if experts == 4:
                    cot_two = over_chip(tie(cot_held, lse[0]), 3)
                    slot_cotangent += [(cot_two, 0), (cot_two, 1)]
            rider = (output_weight,) if s == 0 else ()
            n, q, l, blocks = attend(gathered[s], gain1, w_rows, *rider)
            normed.append(n)
            qkv.append(q)
            lse.append(l)
            mixed.append(from_tensor(blocks if s == 0 else tie(blocks, mixed[0][1:])))

        flat_tokens = tokens.reshape(rows_here, feat)
        route_t = route_weight.T
        ready = tie(mixed, [block for block, _ in slot_cotangent[1:]])
        copies = parts * (seqs + 1)
        hidden, gate, raw, mixed_all, out_weight_all, *packed = call(
            functools.partial(middle_kernel, seqs, parts, experts),
            [
                Far(SDS((rows_here, feat), F32)),
                Far(SDS((8, rows_here), F32)),
                Far(SDS((router, rows_here), F32)),
                Loose(SDS((feat, rows_here), BF16)),
                Loose(SDS((feat, feat), BF16)),
            ]
            + [SDS((cap + 8, feat), BF16)] * experts,
            [Far(flat_tokens), *[Free(b) for blocks in ready for b in blocks]]
            + [gain2, route_t, expert_embed, member_t, Far(placing)],
            4 * rows_here * feat * feat,
            scratch=[
                VMEM((feat, rows_here), BF16),
                VMEM((feat, feat), BF16),
                pltpu.SemaphoreType.DMA((copies,)),
                pltpu.SemaphoreType.DMA((2,)),
            ],
        )

        half = experts // 2
        expert_weights = (up_weight[0], up_other, down_weight[0], down_other)
        w_held = tie(w_half, packed)
        w_near = [over_tensor(w_held, m) for m in range(1, parts - 1)]
        if experts == 4:
            one = over_chip(packed[1], 1)
            held = tie(packed[2:], one)
            two, three = over_chip(held[0], 2), over_chip(held[1], 3)
            slot_rows = [(packed[0], 0), (one, 0)]
            low_half = expert(slot_rows[:2], slot_cotangent[:2], cap, *expert_weights, joined=(1,))
            near = over_chip(low_half[1][1], 1)
            three, two, w_near = tie((three, two, w_near), low_half[1])
            w_far = over_tensor(tie(w_half, w_near), parts - 1)
            high_half = expert([(three, 0), (two, 0)], slot_cotangent[2:], cap, *expert_weights)
        else:
            slot_rows = [(block, 0) for block in swap_chips(packed)]
            low_half = expert(slot_rows[:half], slot_cotangent[:half], cap, *expert_weights)
            high_half = expert(slot_rows[half:], slot_cotangent[half:], cap, *expert_weights)
            w_far = over_tensor(tie(w_half, w_near), parts - 1)
            near = ()
        results = [low_half, high_half]
        rows = [r[2] for r in results]
        grad_rows = [r[3] for r in results]
        acts = [r[4] for r in results]
        gups = [r[5] for r in results]
        w_mine = [*w_near, w_far]
        rows, near = tie((rows, near), w_far)
        grad_own, grad_send = expert_grad(me, rows, grad_rows, gups, acts, parts)
        if experts == 4:
            back_grad = [
                low_half[1][0],
                near,
                over_chip(high_half[1][1], 2),
                over_chip(high_half[1][0], 3),
            ]
        else:
            back_grad = swap_chips(low_half[1] + high_half[1])
        back_grad, grad_send, w_mine = tie((back_grad, grad_send, w_mine), grad_send)
        grad_recv = over_core(grad_send)
        w_theirs = over_core(jnp.concatenate(w_mine, axis=0))

        outs = call(
            functools.partial(back_kernel, seqs, parts, experts),
            [
                Far(SDS((rows_here, feat), F32)),
                Far(SDS((rows_here, feat), BF16)),
                SDS((router + 8 + -(-experts // 8) * 8, feat), F32),
            ]
            + [SDS((channels, rows_here), BF16)] * parts,
            [*back_grad, Far(cotangent), Far(hidden), Far(raw), Far(out_weight_all)]
            + [gain2, route_t, expert_embed, member_t, Far(placing)],
            4 * rows_here * feat * feat,
            scratch=[VMEM((rows_here, feat), BF16)],
        )
        grad_hidden, grad_low, stats = outs[:3]
        grad_mixed = from_tensor(outs[3:])
        if experts == 4:
            two, three = tie((high_half[0][1], high_half[0][0]), grad_mixed[1])
            back = [low_half[0][0], near, over_chip(two, 2), over_chip(three, 3)]
        else:
            back = swap_chips(low_half[0] + high_half[0])

        grad_recv = tie(grad_recv, grad_mixed[1])
        up_own, down_own = grad_own[0], grad_own[1]
        up_recv, down_recv = grad_recv[0], grad_recv[1]
        up_pair, down_pair = first_pairs(grad_own, grad_recv, ((1, parts - 1), (2, parts - 1)))

        out_half = channels // 2
        out_keep, out_send = call(
            out_grad_kernel,
            [SDS((parts, out_half, feat), F32), SDS((parts, out_half, feat), BF16)],
            [Far(mixed_all), Far(tie(grad_low, up_pair, down_pair))],
            2 * rows_here * feat * feat,
            [VMEM((feat, feat), F32)],
            scalar=core,
        )
        out_keep = out_keep + over_core(out_send).astype(F32)
        stat_high = lax.reduce_precision(stats, 8, 7)
        stat_low = lax.reduce_precision(stats - stat_high, 8, 7)
        stat_terms = jnp.concatenate([stat_high, stat_low], axis=0).astype(BF16)
        out_ride = [
            jnp.concatenate([out_keep[m].astype(BF16), stat_terms], axis=0) for m in range(1, parts)
        ]

        if parts == 4:
            up_got = over_tensor(tie(up_pair, grad_mixed), 1)
            down_got = over_tensor(tie(down_pair, grad_mixed), 2)
        else:
            up_got, down_got = (), ()

        def second(own, recv, got, mask):
            return (own[mask].astype(F32) + recv[mask].astype(F32) + got[1].astype(F32)).astype(BF16)

        def final(own, recv, got, last):
            total = own[0].astype(F32) + recv[0].astype(F32)
            return (total + got[0].astype(F32) + last.astype(F32))[None]

        def slow_scatter(own, recv):
            total = own[0].astype(F32) + recv[0].astype(F32)
            for m in range(1, parts):
                part = own[m].astype(F32) + recv[m].astype(F32)
                total = total + over_tensor(part.astype(BF16), m).astype(F32)
            return total[None]

        grads = []
        came = tie(grad_mixed, out_send, w_theirs)
        for s in range(seqs):
            if s == 1:
                came = tie(came, grads[0])
            grads.append(
                attend_back(qkv[s], lse[s], came, s, cover=COVER if s == 0 else LAST_COVER)
            )
            if s == 0:
                out_held = tie(out_ride, grads[0], back)
                out_got = [over_tensor(out_held[m - 1], m) for m in range(1, parts)]
        split = 3 * channels // 2
        qkv_keep, qkv_send, norm1_grad = call(
            functools.partial(qkv_grad_kernel, seqs, parts),
            [SDS((split, feat), F32), SDS((split + 16, feat), BF16), SDS((1, feat), F32)],
            [Free(b) for blocks in tie(grads, up_got, down_got) for b in blocks]
            + [Far(n) for n in normed]
            + [Far(w_rows)],
            2 * seqs * parts * shard * 3 * channels * feat,
            [
                VMEM((3 * channels, feat), F32),
                VMEM((seqs, 3 * channels, parts * shard), BF16),
                pltpu.SemaphoreType.DMA((seqs * parts,)),
            ],
            scalar=core,
            cover=0,
        )
        out_half = out_keep.shape[1]
        out_part = sum((got[:out_half].astype(F32) for got in out_got), out_keep[0])
        size = stats.shape[0]

        def both_terms(terms):
            return terms[:size].astype(F32) + terms[size:].astype(F32)

        terms = [both_terms(t) for t in [stat_terms] + [got[out_half:] for got in out_got]]
        while len(terms) > 1:
            terms = [terms[i] + terms[i + 1] for i in range(0, len(terms), 2)]
        stats = terms[0] + over_core(terms[0])

        (result,) = call(
            functools.partial(out_kernel, experts, cap),
            [Far(SDS((rows_here, feat), F32))],
            [Far(b) for b in tie(back, qkv_send)] + [Far(hidden), Far(gate), Far(placing)],
            2 * rows_here * rows_here * feat,
            cover=0,
        )
        out_got, up_got, down_got = tie((out_got, up_got, down_got), result)
        grad_blocks = [from_tensor(tie(grads[0], out_got, up_got, down_got))]
        qkv_recv = over_core(qkv_send)
        def tail(s, *after):
            before = [Free(input_grads[-1])] if s > 0 else []
            (input_part,) = call(
                functools.partial(tail_kernel, parts),
                [Far(SDS((rows_here, feat), F32), (shard, feat), s)],
                [*map(Free, tie(grad_blocks[s], *after)), Free(w_rows)]
                + [Free(in_hbm(w)) for w in (*w_mine, w_theirs)]
                + [Far(flat_tokens, (shard, feat), s), gain1]
                + [Far(grad_hidden, (shard, feat), s), *before],
                2 * shard * feat * 3 * channels * parts,
                [
                    VMEM((parts * 3 * channels, shard), BF16),
                    VMEM((parts * 3 * channels, feat), BF16),
                    pltpu.SemaphoreType.DMA((3 * parts - 1,)),
                ],
                scalar=core,
                aliases={2 * parts + 5: 0} if s > 0 else None,
            )
            return input_part

        qkv_keep = qkv_keep + qkv_recv[:split].astype(F32)
        norm1_grad = norm1_grad + jnp.sum(qkv_recv[split : split + 3].astype(F32), axis=0, keepdims=True)
        stats = stats + jnp.pad(norm1_grad, ((router + 2, size - router - 3), (0, 0)))
        values = jnp.concatenate([qkv_keep, out_part, stats], axis=0)
        values = jnp.pad(values, ((0, -values.shape[0] % (8 << bits)), (0, 0)))
        input_grads = []
        up_last = down_last = ()
        for level, mask in enumerate(masks):
            keep, send = halves(values, chip_bit(level))
            send = send.astype(BF16)
            came = over_chip(send, mask)
            if level == 0:
                grad_blocks.append(from_tensor(tie(grads[1], grad_blocks[0])))
                input_grads.append(tail(0, send))
                came, keep = tie((came, keep), input_grads[0])
            if level == 1:
                came = tie(came, grad_blocks[1])
            values = keep + came.astype(F32)
        summed = values.astype(BF16)
        if parts == 4:
            held = tie((up_got, down_got), send)
            up_held = second(up_own, up_recv, held[0], 2)
            down_held = second(down_own, down_recv, held[1], 1)
            up_last = over_tensor(up_held, 2)
            down_last = over_tensor(down_held, 1)
            input_grads.append(tail(1, up_held, down_held, summed))
            up_last, down_last = tie((up_last, down_last), input_grads[1])
        else:
            input_grads.append(tail(1, summed))
        for level in reversed(range(bits)):
            summed = joined(summed, over_chip(summed, masks[level]), chip_bit(level))
        other_half = over_core(summed[: split + out_half])
        stats = summed[split + out_half :].astype(F32)
        query_key_value_gradient = (
            joined(summed[:split], other_half[:split], core)
            .reshape(3, channels, feat)
            .transpose(0, 2, 1)
            .astype(F32)
        )
        ends = slice(split, split + out_half)
        out_proj_grad = joined(summed[ends], other_half[ends], core).astype(F32)
        if parts == 4:
            up_weight_grad = final(up_own, up_recv, up_got, up_last)
            down_weight_grad = final(down_own, down_recv, down_got, down_last)
        else:
            up_weight_grad = slow_scatter(up_own, up_recv)
            down_weight_grad = slow_scatter(down_own, down_recv)

        beside = [(up_weight_grad, down_weight_grad), (query_key_value_gradient, out_proj_grad)]
        norm1_grad = stats[router + 2 : router + 3]
        mask = 1
        while mask < tensor_size:
            came = over_tensor(norm1_grad, mask)
            if beside:
                came = tie(came, beside.pop(0))
            norm1_grad = norm1_grad + came
            mask *= 2
        route_grad = stats[:router].T
        norm2_grad = stats[router]
        norm1_grad = norm1_grad[0] / norm1_gain
        width, digits, stride = count_digits(rows_here, 2 * parts * experts)
        loads = sum(
            stats[router + 1, stride * i : stride * i + experts] * float(1 << (width * i))
            for i in range(digits)
        )
        embed_grad = stats[router + 8 : router + 8 + experts, :router]

        return (
            result.reshape(seqs, shard, feat),
            input_grads[-1].reshape(seqs, shard, feat),
            loads,
            norm1_grad,
            query_key_value_gradient,
            out_proj_grad,
            norm2_grad,
            route_grad,
            embed_grad,
            up_weight_grad,
            down_weight_grad,
        )

    return body


def solution(mesh):
    return jax.shard_map(
        program(mesh.shape["tensor"], mesh.shape["expert"]),
        mesh=mesh,
        in_specs=(
            P("expert", "tensor", None),
            P("expert", "tensor", None),
            P("expert", "tensor"),
            P("expert", "tensor", None),
            P(),
            P(None, None, "tensor"),
            P("tensor", None),
            P(),
            P(),
            P(),
            P("expert", None, None),
            P("expert", None, None),
        ),
        out_specs=(
            P("expert", "tensor", None),
            P("expert", "tensor", None),
            P(),
            P(),
            P(None, None, "tensor"),
            P("tensor", None),
            P(),
            P(),
            P(),
            P("expert", None, "tensor"),
            P("expert", None, "tensor"),
        ),
        check_vma=False,
    )
```

```python
import functools

import jax
import jax.numpy as jnp
from jax import lax
from jax.experimental import pallas as pl
from jax.experimental.pallas import tpu as pltpu
from jax.sharding import PartitionSpec as P

HEAD = 64
F32 = jnp.float32
BF16 = jnp.bfloat16
LOG2E = 1.4426950408889634
SCALE = HEAD**-0.5
EXACT = lax.Precision.HIGHEST
SDS = jax.ShapeDtypeStruct
VMEM = pltpu.VMEM
COVER = 4
LAST_COVER = 0

ERFC_SLOPE = 0.44
ERFC = (
    0.248227568,
    0.248777028,
    0.217859919,
    0.214130365,
    -0.0172025688,
    0.293641958,
    -0.276276279,
    0.0708421859,
)


def dot_nn(left, right, precision=None):
    return jnp.dot(left, right, preferred_element_type=F32, precision=precision)


def dot_nt(left, right, precision=None):
    return lax.dot_general(
        left, right, (((1,), (1,)), ((), ())), preferred_element_type=F32, precision=precision
    )


def dot_tn(left, right, precision=None):
    return lax.dot_general(
        left, right, (((0,), (0,)), ((), ())), preferred_element_type=F32, precision=precision
    )


class Far:
    def __init__(self, value, block=None, at=0):
        self.value = value
        self.block = value.shape if block is None else block
        self.at = at


class Here(Far):
    pass


class Loose(Far):
    pass


class Free(Far):
    pass


def start_all(pairs, sems):
    copies = [pltpu.make_async_copy(a, b, sems.at[i]) for i, (a, b) in enumerate(pairs)]
    for copy in copies:
        copy.start()

    def wait():
        for copy in copies:
            copy.wait()

    return wait


def plain(value):
    return value.value if isinstance(value, Far) else value


def in_hbm(value):
    return pltpu.with_memory_space_constraint(value, pltpu.HBM)


def cost(flops, size, transcendentals=0, cover=COVER):
    return pl.CostEstimate(
        flops=flops * cover, bytes_accessed=size * cover, transcendentals=transcendentals * cover
    )


def call(kernel, outs, args, flops, scratch=(), limit=24, transcendentals=0, scalar=None, cover=COVER, aliases=None):
    whole = pl.BlockSpec(memory_space=VMEM)

    def spec(arg):
        if isinstance(arg, Loose):
            return pl.BlockSpec(memory_space=pl.ANY)
        if not isinstance(arg, Far):
            return whole
        if isinstance(arg, (Loose, Free)):
            return pl.BlockSpec(memory_space=pl.ANY)
        where = arg.at if isinstance(arg.at, tuple) else (arg.at,)
        where += (0,) * (arg.value.ndim - len(where))
        return pl.BlockSpec(
            arg.block, lambda i: where, pipeline_mode=pl.Buffered(buffer_count=1)
        )

    specs = [spec(a) for a in args]
    out_specs = [spec(o) for o in outs]
    size = sum(a.size * a.dtype.itemsize for a in map(plain, args))
    size += sum(o.size * o.dtype.itemsize for o in map(plain, outs))
    args = [
        a.value if isinstance(a, (Free, Here)) else in_hbm(a.value) if isinstance(a, Far) else a for a in args
    ]
    outs = [pltpu.HBM(o.value.shape, o.value.dtype) if isinstance(o, Far) else o for o in outs]
    if scalar is not None:
        specs = [pl.BlockSpec(memory_space=pltpu.SMEM)] + specs
        args = [scalar.reshape(1)] + args
    return pl.pallas_call(
        kernel,
        grid=(1,),
        out_shape=list(outs),
        in_specs=specs,
        out_specs=out_specs,
        scratch_shapes=list(scratch),
        input_output_aliases=aliases or {},
        compiler_params=pltpu.CompilerParams(vmem_limit_bytes=limit << 20),
        cost_estimate=cost(flops, size, transcendentals, cover),
    )(*args)


def centred(x):
    cen = x - jnp.mean(x, axis=1, keepdims=True)
    return cen, lax.rsqrt(jnp.mean(cen * cen, axis=1, keepdims=True) + 1e-05)


def tie(values, *after):
    return lax.optimization_barrier((values, after))[0]


def attend_kernel(parts, pieces, channels, riding, *refs):
    tok = refs[: sum(pieces)]
    refs = refs[sum(pieces) :]
    gain_ref, w_ref = refs[:2]
    rider = refs[2 : 2 + riding]
    refs = refs[2 + riding :]
    normed_out, qkv_out, lse_ref = refs[:3]
    mixed = refs[3 : 3 + parts]
    normed_ref, qkv_ref, sems = refs[3 + parts :]
    shard = tok[0].shape[0]
    for ref in rider:
        for b in range(parts):
            mixed[b][:, pl.ds(shard, ref.shape[1])] = ref[...]
    at = 0
    for ref in tok:
        size = ref.shape[0]
        cen, inv = centred(ref[...].astype(F32))
        rows = (cen * inv * gain_ref[...]).astype(BF16)
        normed_ref[pl.ds(at, size), :] = rows
        qkv_ref[:, pl.ds(at, size)] = dot_nt(w_ref[...], rows).astype(BF16)
        at += size
    copies = [
        pltpu.make_async_copy(normed_ref, normed_out, sems.at[0]),
        pltpu.make_async_copy(qkv_ref, qkv_out, sems.at[1]),
    ]
    for copy in copies:
        copy.start()
    size = 128
    chunks = parts * shard // size

    def head(h, carry):
        off = pl.multiple_of(h * HEAD, HEAD)
        key = qkv_ref[pl.ds(channels + off, HEAD), :].T
        value_t = qkv_ref[pl.ds(2 * channels + off, HEAD), :]
        for b in range(parts):
            query_t = qkv_ref[pl.ds(off, HEAD), pl.ds(b * shard, shard)]
            scores = [dot_nn(key[i * size : (i + 1) * size], query_t) for i in range(chunks)]
            top = None
            for score in scores:
                part = jnp.max(score.reshape(size // 8, 8, shard), axis=0)
                top = part if top is None else jnp.maximum(top, part)
            top = jnp.max(top, axis=0, keepdims=True) * (SCALE * LOG2E)
            total, out = None, None
            for i, score in enumerate(scores):
                expos = jnp.exp2(score * (SCALE * LOG2E) - top)
                part = jnp.sum(expos.reshape(size // 8, 8, shard), axis=0)
                term = dot_nn(value_t[:, i * size : (i + 1) * size], expos.astype(BF16))
                total = part if i == 0 else total + part
                out = term if i == 0 else out + term
            total = jnp.sum(total, axis=0, keepdims=True)
            mixed[b][pl.ds(off, HEAD), pl.ds(0, shard)] = (out * (1.0 / total)).astype(BF16)
            lse_ref[pl.ds(h, 1), pl.ds(b * shard, shard)] = top + jnp.log2(total)
        return carry

    lax.fori_loop(0, channels // HEAD, head, 0)
    for copy in copies:
        copy.wait()


def attend(tok, gain, w_rows, *rider):
    parts = len(tok)
    shard, feat = tok[0].shape
    length = parts * shard
    channels = w_rows.shape[0] // 3
    pieces = [len(block) if isinstance(block, tuple) else 1 for block in tok]
    tok = jax.tree.leaves(tok)
    outs = call(
        functools.partial(attend_kernel, parts, pieces, channels, len(rider)),
        [
            Loose(SDS((length, feat), BF16)),
            Loose(SDS((3 * channels, length), BF16)),
            Far(SDS((8, length), F32)),
        ]
        + [SDS((channels, shard + sum(r.shape[1] for r in rider)), BF16)] * parts,
        [*tok, gain, Far(w_rows), *[Far(r) for r in rider]],
        2 * length * feat * 3 * channels + 4 * length * length * channels,
        scratch=[
            VMEM((length, feat), BF16),
            VMEM((3 * channels, length), BF16),
            pltpu.SemaphoreType.DMA((2,)),
        ],
        transcendentals=length * length * channels // HEAD,
    )
    return outs[0], outs[1], outs[2], outs[3:]


def attend_back_kernel(parts, channels, at, *refs):
    qkv_ref, lse_ref = refs[:2]
    shard = qkv_ref.shape[1] // parts
    grad = [ref.at[:, pl.ds(at * shard, shard)] for ref in refs[2 : 2 + parts]]
    refs = refs[2 + parts :]
    outs = refs[:parts]
    key_acc, value_acc = refs[parts:]

    def head(h, carry):
        off = pl.multiple_of(h * HEAD, HEAD)
        key_t = qkv_ref[pl.ds(channels + off, HEAD), :]
        key = key_t.T
        value = qkv_ref[pl.ds(2 * channels + off, HEAD), :].T
        for b in range(parts):
            query_t = qkv_ref[pl.ds(off, HEAD), pl.ds(b * shard, shard)]
            grad_t = grad[b][pl.ds(off, HEAD), :]
            scores = dot_nn(key, query_t)
            probs = jnp.exp2(
                scores * (SCALE * LOG2E) - lse_ref[pl.ds(h, 1), pl.ds(b * shard, shard)]
            )
            grad_probs = dot_nn(value, grad_t)
            inner = jnp.sum(probs * grad_probs, axis=0, keepdims=True)
            grad_scores = (probs * (grad_probs - inner)).astype(BF16)
            value_part = dot_nt(grad_t, probs.astype(BF16))
            key_part = dot_nt(query_t, grad_scores)
            outs[b][pl.ds(off, HEAD), :] = (dot_nn(key_t, grad_scores) * SCALE).astype(BF16)
            if b == 0:
                key_acc[...] = key_part
                value_acc[...] = value_part
            else:
                key_acc[...] += key_part
                value_acc[...] += value_part
        for b in range(parts):
            cols = pl.ds(b * shard, shard)
            outs[b][pl.ds(channels + off, HEAD), :] = (key_acc[:, cols] * SCALE).astype(BF16)
            outs[b][pl.ds(2 * channels + off, HEAD), :] = value_acc[:, cols].astype(BF16)
        return carry

    lax.fori_loop(0, channels // HEAD, head, 0)


def attend_back(qkv, lse, grad, at, cover):
    parts = len(grad)
    channels = grad[0].shape[0]
    length = qkv.shape[1]
    shard = length // parts
    return call(
        functools.partial(attend_back_kernel, parts, channels, at),
        [SDS((3 * channels, shard), BF16)] * parts,
        [Far(qkv), Far(lse), *[Far(g) for g in grad]],
        10 * length * length * channels,
        scratch=[VMEM((HEAD, length), F32)] * 2,
        transcendentals=length * length * channels // HEAD,
        cover=cover,
    )


def gate_parts(raw, embed, member):
    inv = lax.rsqrt(jnp.sum(raw * raw, axis=0, keepdims=True) + 1e-06)
    rows = raw * inv
    embed_inv = lax.rsqrt(jnp.sum(embed * embed, axis=1, keepdims=True) + 1e-06)
    centers = embed * embed_inv
    logits = 3.0 * dot_nn(centers, rows, EXACT)
    expos = jnp.exp(logits - jnp.max(logits, axis=0, keepdims=True))
    probs = expos / jnp.sum(expos, axis=0, keepdims=True)
    gate = jnp.sum(probs * member, axis=0, keepdims=True)
    return inv, rows, embed_inv, centers, probs, gate


def split_rows(row):
    first = row.astype(BF16).astype(F32)
    second = (row - first).astype(BF16).astype(F32)
    third = (row - first) - second
    shape = (8, row.shape[1])
    at = lax.broadcasted_iota(jnp.int32, shape, 0)
    parts = jnp.where(at == 0, first, jnp.where(at == 1, second, jnp.where(at == 2, third, 0.0)))
    return parts.astype(BF16)


def middle_kernel(seqs, parts, groups, *refs):
    refs = list(refs)
    take = lambda n: [refs.pop(0) for _ in range(n)]
    (tok_ref,) = take(1)
    mixed = [take(parts) for _ in range(seqs)]
    gain_ref, route_ref, embed_ref, member_ref, place_ref = take(5)
    hidden_ref, gate_ref, raw_ref, mixed_out, weight_out = take(5)
    packed = take(groups)
    mixed_ref, weight_ref, in_sems, out_sems = take(4)
    rows, feat = tok_ref.shape
    shard = rows // seqs
    channels = mixed[1][0].shape[0]
    cap = rows // groups
    pairs = []
    for m in range(parts):
        at = pl.ds(m * channels, channels)
        pairs.append((mixed[0][m].at[:, pl.ds(shard, feat)], weight_ref.at[at, :]))
        for s in range(seqs):
            pairs.append(
                (mixed[s][m].at[:, pl.ds(0, shard)], mixed_ref.at[at, pl.ds(s * shard, shard)])
            )
    start_all(pairs, in_sems)()
    wait = start_all([(mixed_ref, mixed_out), (weight_ref, weight_out)], out_sems)
    attn = dot_tn(mixed_ref[...], weight_ref[...])
    hidden = tok_ref[...].astype(F32) + attn
    hidden_ref[...] = hidden
    cen, inv = centred(hidden)
    normed = cen * inv * gain_ref[...]
    raw = dot_nt(route_ref[...], normed, EXACT)
    raw_ref[...] = raw
    gate = gate_parts(raw, embed_ref[...], member_ref[...])[-1]
    gate_ref[...] = jnp.broadcast_to(gate, gate_ref.shape)
    low = normed.astype(BF16)
    scalars = split_rows(gate)
    for g in range(groups):
        place = place_ref[pl.ds(g * cap, cap), :]
        packed[g][pl.ds(0, cap), :] = dot_nn(place, low).astype(BF16)
        packed[g][pl.ds(cap, 8), :] = jnp.zeros((8, feat), BF16)
        packed[g][pl.ds(cap, 8), pl.ds(0, cap)] = dot_nt(scalars, place).astype(BF16)
    wait()


def count_digits(rows, devices):
    width = max(1, (256 // devices + 1).bit_length() - 1)
    digits = -(-rows.bit_length() // width)
    return width, digits, 128 if digits <= 6 else 64


def back_kernel(seqs, parts, groups, *refs):
    refs = list(refs)
    take = lambda n: [refs.pop(0) for _ in range(n)]
    packed = take(groups)
    cot_ref, hidden_ref, raw_ref, weight_ref = take(4)
    gain_ref, route_ref, embed_ref, member_ref, place_ref = take(5)
    grad_ref, low_ref, stats_ref = take(3)
    mixed_grad = take(parts)
    (slot_ref,) = take(1)
    rows = hidden_ref.shape[0]
    shard = rows // seqs
    cap = rows // groups
    channels = mixed_grad[0].shape[0]
    scalars = None
    for g in range(groups):
        slot_ref[pl.ds(g * cap, cap), :] = packed[g][pl.ds(0, cap), :]
        scalar = dot_nn(packed[g][pl.ds(cap, 8), pl.ds(0, cap)], place_ref[pl.ds(g * cap, cap), :])
        scalars = scalar if g == 0 else scalars + scalar
    at = lax.broadcasted_iota(jnp.int32, scalars.shape, 0)
    grad_gate = jnp.sum(jnp.where(at < 3, scalars, 0.0), axis=0, keepdims=True)
    cen, inv = centred(hidden_ref[...])
    unit = cen * inv
    gain = gain_ref[...]
    raw_inv, dirs, embed_inv, centers, probs, gate = gate_parts(
        raw_ref[...], embed_ref[...], member_ref[...]
    )
    grad_logits = (3.0 * grad_gate * gate) * (member_ref[...] - probs)
    grad_dirs = dot_tn(centers, grad_logits, EXACT)
    grad_centers = dot_nt(grad_logits, dirs, EXACT)
    grad_raw = raw_inv * (
        grad_dirs - dirs * jnp.sum(dirs * grad_dirs, axis=0, keepdims=True)
    )
    router = route_ref.shape[0]
    experts = embed_ref.shape[0]
    stats_ref[...] = jnp.zeros(stats_ref.shape, F32)
    stats_ref[pl.ds(router + 8, experts), pl.ds(0, router)] = embed_inv * (
        grad_centers - centers * jnp.sum(centers * grad_centers, axis=1, keepdims=True)
    )
    stats_ref[pl.ds(0, router), :] = dot_nn(grad_raw, unit * gain, EXACT)
    count = dot_nt(jnp.ones((8, rows), F32), member_ref[...], EXACT)[:1].astype(jnp.int32)
    width, digits, stride = count_digits(rows, 2 * parts * groups)
    for digit in range(digits):
        part = (count >> (width * digit)) & ((1 << width) - 1)
        stats_ref[pl.ds(router + 1, 1), pl.ds(stride * digit, experts)] = part.astype(F32)
    grad_normed = dot_tn(place_ref[...], slot_ref[...]) + dot_tn(grad_raw, route_ref[...], EXACT)
    stats_ref[pl.ds(router, 1), :] = jnp.sum(grad_normed * unit, axis=0, keepdims=True)
    grad_unit = grad_normed * gain
    grad_hidden = inv * (
        grad_unit
        - jnp.mean(grad_unit, axis=1, keepdims=True)
        - unit * jnp.mean(grad_unit * unit, axis=1, keepdims=True)
    )
    grad_hidden = cot_ref[...].astype(F32) + grad_hidden
    grad_ref[...] = grad_hidden
    low = grad_hidden.astype(BF16)
    low_ref[...] = low
    grad_mixed = dot_nt(weight_ref[...], low).astype(BF16)
    for m in range(parts):
        mixed_grad[m][...] = grad_mixed[m * channels : (m + 1) * channels]


def out_kernel(groups, cap, *refs):
    back = refs[:groups]
    hidden_ref, gate_ref, place_ref, out_ref = refs[groups:]
    mixture = None
    for g in range(groups):
        rows = back[g][pl.ds(back[g].shape[0] - cap, cap), :]
        part = dot_tn(place_ref[pl.ds(g * cap, cap), :], rows)
        mixture = part if g == 0 else mixture + part
    out_ref[...] = hidden_ref[...] + gate_ref[...].T[:, :1] * mixture


def tail_kernel(parts, core_ref, *refs):
    refs = list(refs)
    take = lambda n: [refs.pop(0) for _ in range(n)]
    grads = take(parts)
    (weight,) = take(1)
    mine = take(parts - 1)
    theirs, tok_ref, gain_ref, hidden_grad_ref = take(4)
    out_ref, grad_ref, weight_ref, sems = refs[-4:]
    core = core_ref[0]
    rows = weight.shape[0]
    half = rows // 2
    pairs = [(grads[m], grad_ref.at[pl.ds(m * rows, rows), :]) for m in range(parts)]
    pairs.append((weight, weight_ref.at[pl.ds(0, rows), :]))
    for m in range(1, parts):
        near = pl.multiple_of(m * rows + core * half, 16)
        away = pl.multiple_of(m * rows + (1 - core) * half, 16)
        pairs.append((mine[m - 1], weight_ref.at[pl.ds(near, half), :]))
        pairs.append((theirs.at[pl.ds((m - 1) * half, half), :], weight_ref.at[pl.ds(away, half), :]))
    start_all(pairs, sems)()
    grad_normed = dot_tn(grad_ref[...], weight_ref[...])
    cen, inv = centred(tok_ref[...].astype(F32))
    unit = cen * inv
    grad_unit = grad_normed * gain_ref[...]
    out_ref[...] = hidden_grad_ref[...] + inv * (
        grad_unit
        - jnp.mean(grad_unit, axis=1, keepdims=True)
        - unit * jnp.mean(grad_unit * unit, axis=1, keepdims=True)
    )


def gelu_pair(x):
    z = jnp.abs(x) * (0.5**0.5)
    t = 1.0 / (1.0 + ERFC_SLOPE * z)
    poly = jnp.full_like(t, ERFC[-1])
    for value in ERFC[-2::-1]:
        poly = poly * t + value
    bell = jnp.exp2(x * x * (-0.5 * LOG2E))
    tail = (0.5 * bell) * (t * poly)
    cdf = jnp.where(x < 0.0, tail, 1.0 - tail)
    return x * cdf, cdf + x * (bell * 0.3989422804014327)


def expert_kernel(count, steps, *refs):
    refs = list(refs)
    take = lambda n: [refs.pop(0) for _ in range(n)]
    packed, cot = take(count), take(count)
    ups, downs = take(2), take(2)
    cap = cot[0].shape[0]
    returned, grads = [], []
    for i in range(count):
        (ref,) = take(1)
        if ref.shape[0] == cap:
            returned.append(ref)
            grads += take(1)
        else:
            grads.append(ref.at[pl.ds(0, cap + 8), :])
            returned.append(ref.at[pl.ds(cap + 8, cap), :])
    rows_ref, gr_ref = take(2)
    acts, gups = take(2), take(2)
    ret_acc, grad_acc = take(2)
    step = pl.program_id(0)

    def eye():
        shape = (cap, cap)
        return lax.broadcasted_iota(jnp.int32, shape, 0) == lax.broadcasted_iota(jnp.int32, shape, 1)

    @pl.when(step == 0)
    def _():
        for i in range(count):
            part = pl.ds(i * cap, cap)
            rows_ref[part, :] = packed[i][pl.ds(0, cap), :]
            scalars = packed[i][pl.ds(cap, 8), pl.ds(0, cap)].astype(F32)
            at = lax.broadcasted_iota(jnp.int32, scalars.shape, 0)
            row = jnp.sum(jnp.where(at < 3, scalars, 0.0), axis=0, keepdims=True)
            gate = jnp.sum(jnp.where(eye(), row, 0.0), axis=1, keepdims=True)
            gr_ref[part, :] = (gate * cot[i][...].astype(F32)).astype(BF16)

    rows, grad_rows = rows_ref[...], gr_ref[...]
    ret = None
    for h in range(2):
        up_w, down_w = ups[h][...], downs[h][...]
        act, slope = gelu_pair(dot_nn(rows, up_w))
        act = act.astype(BF16)
        gup = (dot_nn(grad_rows, down_w) * slope).astype(BF16)
        acts[h][...] = act
        gups[h][...] = gup
        ret_part = dot_nt(act, down_w)
        grad_part = dot_nt(gup, up_w)
        ret = ret_part if h == 0 else ret + ret_part
        grad = grad_part if h == 0 else grad + grad_part

    @pl.when(step == 0)
    def _():
        ret_acc[...] = ret
        grad_acc[...] = grad

    @pl.when(step > 0)
    def _():
        ret_acc[...] += ret
        grad_acc[...] += grad

    @pl.when(step == steps - 1)
    def _():
        for i in range(count):
            part = pl.ds(i * cap, cap)
            low = ret_acc[part, :].astype(BF16)
            returned[i][...] = low
            product = jnp.sum(low.astype(F32) * cot[i][...].astype(F32), axis=1, keepdims=True)
            row = jnp.sum(jnp.where(eye(), product, 0.0), axis=0, keepdims=True)
            grads[i][pl.ds(0, cap), :] = grad_acc[part, :].astype(BF16)
            grads[i][pl.ds(cap, 8), :] = jnp.zeros((8, grads[i].shape[1]), BF16)
            grads[i][pl.ds(cap, 8), pl.ds(0, cap)] = split_rows(row)


def expert(packed, cot, cap, up_own, up_other, down_own, down_other, joined=()):
    count = len(cot)
    feat, units = up_own.shape
    width = 512 if units % 512 == 0 else units
    steps = units // width
    rows = count * cap

    def same(size, at=0):
        return pl.BlockSpec((size, feat), lambda j: (at, 0))

    weight = pl.BlockSpec((feat, width), lambda j: (0, j))
    wide = pl.BlockSpec((rows, width), lambda j: (0, j))
    sizes = []
    for i in range(count):
        sizes += [2 * cap + 8] if i in joined else [cap, cap + 8]
    outs = pl.pallas_call(
        functools.partial(expert_kernel, count, steps),
        grid=(steps,),
        in_specs=[same(cap + 8, at) for _, at in packed]
        + [same(cap, at) for _, at in cot]
        + [weight] * 4,
        out_specs=[same(size) for size in sizes] + [same(rows)] * 2 + [wide] * 4,
        out_shape=[SDS((size, feat), BF16) for size in sizes]
        + [pltpu.HBM((rows, feat), BF16)] * 2
        + [pltpu.HBM((rows, units), BF16)] * 4,
        scratch_shapes=[VMEM((rows, feat), F32)] * 2,
        compiler_params=pltpu.CompilerParams(
            vmem_limit_bytes=24 << 20, dimension_semantics=("arbitrary",)
        ),
        cost_estimate=cost(
            16 * rows * feat * units, 8 * feat * units + 16 * rows * units, 4 * rows * units
        ),
    )(
        *[a for a, _ in packed],
        *[in_hbm(a) for a, _ in cot],
        *[in_hbm(w) for w in (up_own, up_other, down_own, down_other)],
    )
    back, grads = [], []
    at = 0
    for i in range(count):
        back.append(outs[at])
        if i not in joined:
            at += 1
        grads.append(outs[at])
        at += 1
    return back, grads, outs[at], outs[at + 1], outs[at + 2 : at + 4], outs[at + 4 :]


def expert_grad_kernel(halves, me_ref, *refs):
    refs = list(refs)
    take = lambda n: [refs.pop(0) for _ in range(n)]
    lefts = [take(halves) for _ in range(2)]
    wides = [[take(2) for _ in range(halves)] for _ in range(2)]
    own_ref, other_ref = take(2)
    turned = take(2)
    size = lefts[0][0].shape[0]

    @pl.when(pl.program_id(0) == 0)
    def _():
        for which in range(2):
            for i in range(halves):
                turned[which][:, pl.ds(i * size, size)] = lefts[which][i][...].T

    for which in range(2):
        for h, ref in enumerate((own_ref, other_ref)):
            full = jnp.concatenate([wides[which][i][h][...] for i in range(halves)], axis=0)
            ref[which, 0] = dot_nn(turned[which][...], full).astype(ref.dtype)


def expert_grad(me, rows, grad_rows, gups, acts, tensor_size):
    halves = len(rows)
    size, feat = rows[0].shape
    units = gups[0][0].shape[1]
    width = units // tensor_size
    same = pl.BlockSpec((size, feat), lambda j, me: (0, 0))
    part = pl.BlockSpec((size, width), lambda j, me: (0, me[0] ^ j))
    block = pl.BlockSpec((2, 1, feat, width), lambda j, me: (0, j, 0, 0))
    shape = (2, tensor_size, feat, width)
    wides = [a for pairs in (gups, acts) for pair in pairs for a in pair]
    return pl.pallas_call(
        functools.partial(expert_grad_kernel, halves),
        grid_spec=pltpu.PrefetchScalarGridSpec(
            num_scalar_prefetch=1,
            grid=(tensor_size,),
            in_specs=[same] * (2 * halves) + [part] * (4 * halves),
            out_specs=[block, block],
            scratch_shapes=[VMEM((feat, halves * size), BF16)] * 2,
        ),
        out_shape=[pltpu.HBM(shape, BF16), pltpu.HBM(shape, BF16)],
        compiler_params=pltpu.CompilerParams(
            vmem_limit_bytes=24 << 20, dimension_semantics=("arbitrary",)
        ),
        cost_estimate=cost(8 * halves * size * feat * units, 24 << 20),
    )(me.reshape(1), *[in_hbm(a) for a in (*rows, *grad_rows, *wides)])


def pair_kernel(*refs):
    for i in range(2):
        for j in range(2):
            own, recv = refs[4 * i + 2 * j : 4 * i + 2 * j + 2]
            refs[8 + i][j] = (own[0, 0].astype(F32) + recv[0, 0].astype(F32)).astype(BF16)


def first_pairs(own, recv, picks):
    feat, width = own.shape[2:]
    block = (1, 1, feat, width)
    args = []
    for which in range(2):
        for m in picks[which]:
            args += [Far(own, block, (which, m)), Here(recv, block, (which, m))]
    return call(pair_kernel, [SDS((2, feat, width), BF16)] * 2, args, 4 * feat * width)


def out_grad_kernel(core_ref, mixed_ref, low_ref, keep_ref, send_ref, full_ref):
    core = core_ref[0]
    parts, half, _ = keep_ref.shape
    full_ref[...] = dot_nn(mixed_ref[...], low_ref[...])
    for m in range(parts):
        near = pl.multiple_of((2 * m + core) * half, half)
        away = pl.multiple_of((2 * m + 1 - core) * half, half)
        keep_ref[m] = full_ref[pl.ds(near, half), :]
        send_ref[m] = full_ref[pl.ds(away, half), :].astype(BF16)


def qkv_grad_kernel(seqs, parts, core_ref, *refs):
    grads = [refs[s * parts : (s + 1) * parts] for s in range(seqs)]
    normed = refs[seqs * parts : seqs * parts + seqs]
    w_ref, keep_ref, send_ref, norm1_ref, full_ref, grad_ref, sems = refs[seqs * parts + seqs :]
    send_ref, extra_ref = send_ref.at[pl.ds(0, keep_ref.shape[0]), :], send_ref
    core = core_ref[0]
    shard = grads[0][0].shape[1]
    half = keep_ref.shape[0]
    pairs = []
    for s in range(seqs):
        for b in range(parts):
            pairs.append((grads[s][b], grad_ref.at[s, :, pl.ds(b * shard, shard)]))
    start_all(pairs, sems)()
    total = dot_nn(grad_ref[0], normed[0][...])
    for s in range(1, seqs):
        total += dot_nn(grad_ref[s], normed[s][...])
    full_ref[...] = total
    norm1 = jnp.sum(total * w_ref[...].astype(F32), axis=0, keepdims=True)
    norm1_ref[...] = norm1
    terms = jnp.concatenate([split_rows(norm1), split_rows(jnp.zeros_like(norm1))], axis=0)
    extra_ref[pl.ds(keep_ref.shape[0], 16), :] = terms
    keep_ref[...] = full_ref[pl.ds(pl.multiple_of(core * half, half), half), :]
    send_ref[...] = full_ref[pl.ds(pl.multiple_of((1 - core) * half, half), half), :].astype(BF16)


def program(tensor_size, expert_size):
    chips = expert_size // 2
    bits = chips.bit_length() - 1

    def over_tensor(values, mask):
        return lax.ppermute(values, "tensor", [(i, i ^ mask) for i in range(tensor_size)])

    def over_core(values):
        return lax.ppermute(values, "expert", [(i, i ^ 1) for i in range(expert_size)])

    def over_chip(values, mask):
        return lax.ppermute(values, "expert", [(i, i ^ (2 * mask)) for i in range(expert_size)])

    def from_tensor(blocks):
        return [blocks[0]] + [over_tensor(blocks[m], m) for m in range(1, tensor_size)]

    def gather_first(block):
        if tensor_size != 4:
            return from_tensor([block] * tensor_size)
        half = block.shape[0] // 2
        one, two = over_tensor(block, 1), over_tensor(block, 2)
        low, high = over_tensor(one[:half], 2), over_tensor(two[half:], 1)
        return [block, one, two, (low, high)]

    def swap_chips(blocks):
        if chips <= 4:
            return [blocks[0]] + [over_chip(blocks[m], m) for m in range(1, chips)]
        chip = lax.axis_index("expert") // 2
        order = chip ^ jnp.arange(chips)
        groups = [[2 * i + core for i in range(chips)] for core in range(2)]
        moved = lax.all_to_all(
            jnp.stack(blocks)[order],
            "expert",
            split_axis=0,
            concat_axis=0,
            tiled=True,
            axis_index_groups=groups,
        )[order]
        return [moved[m] for m in range(chips)]

    if chips == 4:
        masks = (1, 3)
    else:
        masks = tuple(1 << bit for bit in range(bits))

    def chip_bit(level):
        chip = lax.axis_index("expert") // 2
        if chips == 4:
            return ((chip ^ (chip >> 1)) & 1) if level == 0 else (chip >> 1) & 1
        return (chip >> level) & 1

    def halves(values, bit):
        half = values.shape[0] // 2
        low, high = values[:half], values[half:]
        return jnp.where(bit == 0, low, high), jnp.where(bit == 0, high, low)

    def joined(mine, theirs, bit):
        return jnp.concatenate(
            [jnp.where(bit == 0, mine, theirs), jnp.where(bit == 0, theirs, mine)], axis=0
        )

    def body(
        tokens,
        out_grad,
        masked,
        route,
        norm1_gain,
        query_key_value_weight,
        output_weight,
        norm2_gain,
        route_weight,
        expert_embed,
        up_weight,
        down_weight,
    ):
        seqs, shard, feat = tokens.shape
        rows_here = seqs * shard
        experts, router = expert_embed.shape
        cap = rows_here // experts
        channels = query_key_value_weight.shape[2]
        units = up_weight.shape[2]
        parts = tensor_size
        me = lax.axis_index("tensor")
        place_index = lax.axis_index("expert")
        chip, core = place_index // 2, place_index % 2
        gain1 = norm1_gain.reshape(1, feat)
        gain2 = norm2_gain.reshape(1, feat)

        w_rows = query_key_value_weight.transpose(0, 2, 1).reshape(3 * channels, feat)
        half_rows = 3 * channels // 2
        w_half = lax.dynamic_slice_in_dim(w_rows, core * half_rows, half_rows, axis=0)
        gathered = [gather_first(tokens[0])]
        for s in range(1, seqs):
            gathered.append(from_tensor([tie(tokens[s], gathered[-1])] * parts))

        picks = route.reshape(rows_here)
        expert_ids = jnp.arange(experts, dtype=jnp.int32)
        member = (picks[:, None] == expert_ids[None, :]).astype(jnp.int32)
        earlier = jnp.cumsum(member, axis=0) - member
        slot_ids = jnp.sum(earlier * member, axis=1)
        target = (picks ^ chip) * cap + slot_ids
        target = jnp.where(slot_ids < cap, target, -1)
        slot_range = jnp.arange(experts * cap, dtype=jnp.int32)
        placing = (slot_range[:, None] == target[None, :]).astype(BF16)
        member_t = (expert_ids[:, None] == picks[None, :]).astype(F32)
        cotangent = out_grad.reshape(rows_here, feat) * masked.reshape(rows_here, 1).astype(BF16)
        sent_cotangent = dot_nn(placing, cotangent).astype(BF16)
        if experts == 4:
            cot_one = over_chip(sent_cotangent[cap : 3 * cap], 1)
            cot_held = jnp.concatenate([sent_cotangent[3 * cap :], cot_one[cap:]], axis=0)
            slot_cotangent = [(sent_cotangent, 0), (cot_one, 0)]
        else:
            slot_cotangent = [
                (block, 0)
                for block in swap_chips(
                    [sent_cotangent[g * cap : (g + 1) * cap] for g in range(experts)]
                )
            ]

        normed, qkv, lse, mixed = [], [], [], []
        up_other, down_other = over_core(up_weight[0]), over_core(down_weight[0])
        for s in range(seqs):
            if s == 0:
                gathered[0] = tie(
                    gathered[0], sent_cotangent, member_t, w_half, up_other, down_other
                )
            if s == 1:
                gathered[s] = tie(gathered[s], slot_cotangent[1][0], lse[0])
                if experts == 4:
                    cot_two = over_chip(tie(cot_held, lse[0]), 3)
                    slot_cotangent += [(cot_two, 0), (cot_two, 1)]
            rider = (output_weight,) if s == 0 else ()
            n, q, l, blocks = attend(gathered[s], gain1, w_rows, *rider)
            normed.append(n)
            qkv.append(q)
            lse.append(l)
            mixed.append(from_tensor(blocks if s == 0 else tie(blocks, mixed[0][1:])))

        flat_tokens = tokens.reshape(rows_here, feat)
        route_t = route_weight.T
        ready = tie(mixed, [block for block, _ in slot_cotangent[1:]])
        copies = parts * (seqs + 1)
        hidden, gate, raw, mixed_all, out_weight_all, *packed = call(
            functools.partial(middle_kernel, seqs, parts, experts),
            [
                Far(SDS((rows_here, feat), F32)),
                Far(SDS((8, rows_here), F32)),
                Far(SDS((router, rows_here), F32)),
                Loose(SDS((feat, rows_here), BF16)),
                Loose(SDS((feat, feat), BF16)),
            ]
            + [SDS((cap + 8, feat), BF16)] * experts,
            [Far(flat_tokens), *[Free(b) for blocks in ready for b in blocks]]
            + [gain2, route_t, expert_embed, member_t, Far(placing)],
            4 * rows_here * feat * feat,
            scratch=[
                VMEM((feat, rows_here), BF16),
                VMEM((feat, feat), BF16),
                pltpu.SemaphoreType.DMA((copies,)),
                pltpu.SemaphoreType.DMA((2,)),
            ],
        )

        half = experts // 2
        expert_weights = (up_weight[0], up_other, down_weight[0], down_other)
        w_held = tie(w_half, packed)
        w_near = [over_tensor(w_held, m) for m in range(1, parts - 1)]
        if experts == 4:
            one = over_chip(packed[1], 1)
            held = tie(packed[2:], one)
            two, three = over_chip(held[0], 2), over_chip(held[1], 3)
            slot_rows = [(packed[0], 0), (one, 0)]
            low_half = expert(slot_rows[:2], slot_cotangent[:2], cap, *expert_weights, joined=(1,))
            near = over_chip(low_half[1][1], 1)
            three, two, w_near = tie((three, two, w_near), low_half[1])
            w_far = over_tensor(tie(w_half, w_near), parts - 1)
            high_half = expert([(three, 0), (two, 0)], slot_cotangent[2:], cap, *expert_weights)
        else:
            slot_rows = [(block, 0) for block in swap_chips(packed)]
            low_half = expert(slot_rows[:half], slot_cotangent[:half], cap, *expert_weights)
            high_half = expert(slot_rows[half:], slot_cotangent[half:], cap, *expert_weights)
            w_far = over_tensor(tie(w_half, w_near), parts - 1)
            near = ()
        results = [low_half, high_half]
        rows = [r[2] for r in results]
        grad_rows = [r[3] for r in results]
        acts = [r[4] for r in results]
        gups = [r[5] for r in results]
        w_mine = [*w_near, w_far]
        rows, near = tie((rows, near), w_far)
        grad_own, grad_send = expert_grad(me, rows, grad_rows, gups, acts, parts)
        if experts == 4:
            back_grad = [
                low_half[1][0],
                near,
                over_chip(high_half[1][1], 2),
                over_chip(high_half[1][0], 3),
            ]
        else:
            back_grad = swap_chips(low_half[1] + high_half[1])
        back_grad, grad_send, w_mine = tie((back_grad, grad_send, w_mine), grad_send)
        grad_recv = over_core(grad_send)
        w_theirs = over_core(jnp.concatenate(w_mine, axis=0))

        outs = call(
            functools.partial(back_kernel, seqs, parts, experts),
            [
                Far(SDS((rows_here, feat), F32)),
                Far(SDS((rows_here, feat), BF16)),
                SDS((router + 8 + -(-experts // 8) * 8, feat), F32),
            ]
            + [SDS((channels, rows_here), BF16)] * parts,
            [*back_grad, Far(cotangent), Far(hidden), Far(raw), Far(out_weight_all)]
            + [gain2, route_t, expert_embed, member_t, Far(placing)],
            4 * rows_here * feat * feat,
            scratch=[VMEM((rows_here, feat), BF16)],
        )
        grad_hidden, grad_low, stats = outs[:3]
        grad_mixed = from_tensor(outs[3:])
        up_own, down_own = grad_own[0], grad_own[1]
        up_recv, down_recv = grad_recv[0], grad_recv[1]
        up_pair, down_pair = first_pairs(grad_own, grad_recv, ((1, parts - 1), (2, parts - 1)))

        out_half = channels // 2
        out_keep, out_send = call(
            out_grad_kernel,
            [SDS((parts, out_half, feat), F32), SDS((parts, out_half, feat), BF16)],
            [Far(mixed_all), Far(tie(grad_low, up_pair, down_pair))],
            2 * rows_here * feat * feat,
            [VMEM((feat, feat), F32)],
            scalar=core,
        )
        out_keep = out_keep + over_core(out_send).astype(F32)
        stat_high = lax.reduce_precision(stats, 8, 7)
        stat_low = lax.reduce_precision(stats - stat_high, 8, 7)
        stat_terms = jnp.concatenate([stat_high, stat_low], axis=0).astype(BF16)
        out_ride = [
            jnp.concatenate([out_keep[m].astype(BF16), stat_terms], axis=0) for m in range(1, parts)
        ]

        if experts == 4:
            two, three = tie((high_half[0][1], high_half[0][0]), out_send)
            back = [low_half[0][0], near, over_chip(two, 2), over_chip(three, 3)]
        else:
            back = swap_chips(low_half[0] + high_half[0])

        if parts == 4:
            up_got = over_tensor(tie(up_pair, grad_mixed), 1)
            down_got = over_tensor(tie(down_pair, grad_mixed), 2)
        else:
            up_got, down_got = (), ()

        def second(own, recv, got, mask):
            return (own[mask].astype(F32) + recv[mask].astype(F32) + got[1].astype(F32)).astype(BF16)

        def final(own, recv, got, last):
            total = own[0].astype(F32) + recv[0].astype(F32)
            return (total + got[0].astype(F32) + last.astype(F32))[None]

        def slow_scatter(own, recv):
            total = own[0].astype(F32) + recv[0].astype(F32)
            for m in range(1, parts):
                part = own[m].astype(F32) + recv[m].astype(F32)
                total = total + over_tensor(part.astype(BF16), m).astype(F32)
            return total[None]

        grads = []
        came = tie(grad_mixed, out_send, w_theirs)
        for s in range(seqs):
            if s == 1:
                came = tie(came, grads[0])
            grads.append(
                attend_back(qkv[s], lse[s], came, s, cover=COVER if s == 0 else LAST_COVER)
            )
            if s == 0:
                out_held = tie(out_ride, grads[0], back)
                out_got = [over_tensor(out_held[m - 1], m) for m in range(1, parts)]
        split = 3 * channels // 2
        qkv_keep, qkv_send, norm1_grad = call(
            functools.partial(qkv_grad_kernel, seqs, parts),
            [SDS((split, feat), F32), SDS((split + 16, feat), BF16), SDS((1, feat), F32)],
            [Free(b) for blocks in tie(grads, up_got, down_got) for b in blocks]
            + [Far(n) for n in normed]
            + [Far(w_rows)],
            2 * seqs * parts * shard * 3 * channels * feat,
            [
                VMEM((3 * channels, feat), F32),
                VMEM((seqs, 3 * channels, parts * shard), BF16),
                pltpu.SemaphoreType.DMA((seqs * parts,)),
            ],
            scalar=core,
            cover=0,
        )
        out_half = out_keep.shape[1]
        out_part = sum((got[:out_half].astype(F32) for got in out_got), out_keep[0])
        size = stats.shape[0]

        def both_terms(terms):
            return terms[:size].astype(F32) + terms[size:].astype(F32)

        terms = [both_terms(t) for t in [stat_terms] + [got[out_half:] for got in out_got]]
        while len(terms) > 1:
            terms = [terms[i] + terms[i + 1] for i in range(0, len(terms), 2)]
        stats = terms[0] + over_core(terms[0])

        grad_blocks = [from_tensor(tie(grads[0], out_got, up_got, down_got))]
        qkv_recv = over_core(qkv_send)
        def tail(s, *after):
            before = [Free(input_grads[-1])] if s > 0 else []
            (input_part,) = call(
                functools.partial(tail_kernel, parts),
                [Far(SDS((rows_here, feat), F32), (shard, feat), s)],
                [*map(Free, tie(grad_blocks[s], *after)), Free(w_rows)]
                + [Free(in_hbm(w)) for w in (*w_mine, w_theirs)]
                + [Far(flat_tokens, (shard, feat), s), gain1]
                + [Far(grad_hidden, (shard, feat), s), *before],
                2 * shard * feat * 3 * channels * parts,
                [
                    VMEM((parts * 3 * channels, shard), BF16),
                    VMEM((parts * 3 * channels, feat), BF16),
                    pltpu.SemaphoreType.DMA((3 * parts - 1,)),
                ],
                scalar=core,
                aliases={2 * parts + 5: 0} if s > 0 else None,
            )
            return input_part

        qkv_keep = qkv_keep + qkv_recv[:split].astype(F32)
        norm1_grad = norm1_grad + jnp.sum(qkv_recv[split : split + 3].astype(F32), axis=0, keepdims=True)
        stats = stats + jnp.pad(norm1_grad, ((router + 2, size - router - 3), (0, 0)))
        values = jnp.concatenate([qkv_keep, out_part, stats], axis=0)
        values = jnp.pad(values, ((0, -values.shape[0] % (8 << bits)), (0, 0)))
        input_grads = []
        up_last = down_last = ()
        for level, mask in enumerate(masks):
            keep, send = halves(values, chip_bit(level))
            send = send.astype(BF16)
            came = over_chip(send, mask)
            if level == 0:
                (result,) = call(
                    functools.partial(out_kernel, experts, cap),
                    [Far(SDS((rows_here, feat), F32))],
                    [Far(b) for b in tie(back, send)]
                    + [Far(hidden), Far(gate), Far(placing)],
                    2 * rows_here * rows_here * feat,
                    cover=0,
                )
                came = tie(came, result)
            if level == 1:
                grad_blocks.append(from_tensor(tie(grads[1], grad_blocks[0], send)))
                input_grads.append(tail(0, send))
                came = tie(came, input_grads[0])
            values = keep + came.astype(F32)
        summed = values.astype(BF16)
        if parts == 4:
            held = tie((up_got, down_got), summed)
            up_held = second(up_own, up_recv, held[0], 2)
            down_held = second(down_own, down_recv, held[1], 1)
            up_last = over_tensor(up_held, 2)
            down_last = over_tensor(down_held, 1)
            input_grads.append(tail(1, up_held, down_held, summed))
            up_last, down_last = tie((up_last, down_last), input_grads[1])
        else:
            input_grads.append(tail(1, summed))
        for level in reversed(range(bits)):
            summed = joined(summed, over_chip(summed, masks[level]), chip_bit(level))
        other_half = over_core(summed[: split + out_half])
        stats = summed[split + out_half :].astype(F32)
        query_key_value_gradient = (
            joined(summed[:split], other_half[:split], core)
            .reshape(3, channels, feat)
            .transpose(0, 2, 1)
            .astype(F32)
        )
        ends = slice(split, split + out_half)
        out_proj_grad = joined(summed[ends], other_half[ends], core).astype(F32)
        if parts == 4:
            up_weight_grad = final(up_own, up_recv, up_got, up_last)
            down_weight_grad = final(down_own, down_recv, down_got, down_last)
        else:
            up_weight_grad = slow_scatter(up_own, up_recv)
            down_weight_grad = slow_scatter(down_own, down_recv)

        beside = [(up_weight_grad, down_weight_grad), (query_key_value_gradient, out_proj_grad)]
        norm1_grad = stats[router + 2 : router + 3]
        mask = 1
        while mask < tensor_size:
            came = over_tensor(norm1_grad, mask)
            if beside:
                came = tie(came, beside.pop(0))
            norm1_grad = norm1_grad + came
            mask *= 2
        route_grad = stats[:router].T
        norm2_grad = stats[router]
        norm1_grad = norm1_grad[0] / norm1_gain
        width, digits, stride = count_digits(rows_here, 2 * parts * experts)
        loads = sum(
            stats[router + 1, stride * i : stride * i + experts] * float(1 << (width * i))
            for i in range(digits)
        )
        embed_grad = stats[router + 8 : router + 8 + experts, :router]

        return (
            result.reshape(seqs, shard, feat),
            input_grads[-1].reshape(seqs, shard, feat),
            loads,
            norm1_grad,
            query_key_value_gradient,
            out_proj_grad,
            norm2_grad,
            route_grad,
            embed_grad,
            up_weight_grad,
            down_weight_grad,
        )

    return body


def solution(mesh):
    return jax.shard_map(
        program(mesh.shape["tensor"], mesh.shape["expert"]),
        mesh=mesh,
        in_specs=(
            P("expert", "tensor", None),
            P("expert", "tensor", None),
            P("expert", "tensor"),
            P("expert", "tensor", None),
            P(),
            P(None, None, "tensor"),
            P("tensor", None),
            P(),
            P(),
            P(),
            P("expert", None, None),
            P("expert", None, None),
        ),
        out_specs=(
            P("expert", "tensor", None),
            P("expert", "tensor", None),
            P(),
            P(),
            P(None, None, "tensor"),
            P("tensor", None),
            P(),
            P(),
            P(),
            P("expert", None, "tensor"),
            P("expert", None, "tensor"),
        ),
        check_vma=False,
    )
```

```python
import functools

import jax
import jax.numpy as jnp
from jax import lax
from jax.experimental import pallas as pl
from jax.experimental.pallas import tpu as pltpu
from jax.sharding import PartitionSpec as P

HEAD = 64
F32 = jnp.float32
BF16 = jnp.bfloat16
LOG2E = 1.4426950408889634
SCALE = HEAD**-0.5
EXACT = lax.Precision.HIGHEST
SDS = jax.ShapeDtypeStruct
VMEM = pltpu.VMEM
COVER = 4
LAST_COVER = 0

ERFC_SLOPE = 0.44
ERFC = (
    0.248227568,
    0.248777028,
    0.217859919,
    0.214130365,
    -0.0172025688,
    0.293641958,
    -0.276276279,
    0.0708421859,
)


def dot_nn(left, right, precision=None):
    return jnp.dot(left, right, preferred_element_type=F32, precision=precision)


def dot_nt(left, right, precision=None):
    return lax.dot_general(
        left, right, (((1,), (1,)), ((), ())), preferred_element_type=F32, precision=precision
    )


def dot_tn(left, right, precision=None):
    return lax.dot_general(
        left, right, (((0,), (0,)), ((), ())), preferred_element_type=F32, precision=precision
    )


class Far:
    def __init__(self, value, block=None, at=0):
        self.value = value
        self.block = value.shape if block is None else block
        self.at = at


class Here(Far):
    pass


class Loose(Far):
    pass


class Free(Far):
    pass


def start_all(pairs, sems):
    copies = [pltpu.make_async_copy(a, b, sems.at[i]) for i, (a, b) in enumerate(pairs)]
    for copy in copies:
        copy.start()

    def wait():
        for copy in copies:
            copy.wait()

    return wait


def plain(value):
    return value.value if isinstance(value, Far) else value


def in_hbm(value):
    return pltpu.with_memory_space_constraint(value, pltpu.HBM)


def cost(flops, size, transcendentals=0, cover=COVER):
    return pl.CostEstimate(
        flops=flops * cover, bytes_accessed=size * cover, transcendentals=transcendentals * cover
    )


def call(kernel, outs, args, flops, scratch=(), limit=24, transcendentals=0, scalar=None, cover=COVER, aliases=None):
    whole = pl.BlockSpec(memory_space=VMEM)

    def spec(arg):
        if isinstance(arg, Loose):
            return pl.BlockSpec(memory_space=pl.ANY)
        if not isinstance(arg, Far):
            return whole
        if isinstance(arg, (Loose, Free)):
            return pl.BlockSpec(memory_space=pl.ANY)
        where = arg.at if isinstance(arg.at, tuple) else (arg.at,)
        where += (0,) * (arg.value.ndim - len(where))
        return pl.BlockSpec(
            arg.block, lambda i: where, pipeline_mode=pl.Buffered(buffer_count=1)
        )

    specs = [spec(a) for a in args]
    out_specs = [spec(o) for o in outs]
    size = sum(a.size * a.dtype.itemsize for a in map(plain, args))
    size += sum(o.size * o.dtype.itemsize for o in map(plain, outs))
    args = [
        a.value if isinstance(a, (Free, Here)) else in_hbm(a.value) if isinstance(a, Far) else a for a in args
    ]
    outs = [pltpu.HBM(o.value.shape, o.value.dtype) if isinstance(o, Far) else o for o in outs]
    if scalar is not None:
        specs = [pl.BlockSpec(memory_space=pltpu.SMEM)] + specs
        args = [scalar.reshape(1)] + args
    return pl.pallas_call(
        kernel,
        grid=(1,),
        out_shape=list(outs),
        in_specs=specs,
        out_specs=out_specs,
        scratch_shapes=list(scratch),
        input_output_aliases=aliases or {},
        compiler_params=pltpu.CompilerParams(vmem_limit_bytes=limit << 20),
        cost_estimate=cost(flops, size, transcendentals, cover),
    )(*args)


def centred(x):
    cen = x - jnp.mean(x, axis=1, keepdims=True)
    return cen, lax.rsqrt(jnp.mean(cen * cen, axis=1, keepdims=True) + 1e-05)


def tie(values, *after):
    return lax.optimization_barrier((values, after))[0]


def attend_kernel(parts, pieces, channels, riding, *refs):
    tok = refs[: sum(pieces)]
    refs = refs[sum(pieces) :]
    gain_ref, w_ref = refs[:2]
    rider = refs[2 : 2 + riding]
    refs = refs[2 + riding :]
    normed_out, qkv_out, lse_ref = refs[:3]
    mixed = refs[3 : 3 + parts]
    normed_ref, qkv_ref, sems = refs[3 + parts :]
    shard = tok[0].shape[0]
    for ref in rider:
        for b in range(parts):
            mixed[b][:, pl.ds(shard, ref.shape[1])] = ref[...]
    at = 0
    for ref in tok:
        size = ref.shape[0]
        cen, inv = centred(ref[...].astype(F32))
        rows = (cen * inv * gain_ref[...]).astype(BF16)
        normed_ref[pl.ds(at, size), :] = rows
        qkv_ref[:, pl.ds(at, size)] = dot_nt(w_ref[...], rows).astype(BF16)
        at += size
    copies = [
        pltpu.make_async_copy(normed_ref, normed_out, sems.at[0]),
        pltpu.make_async_copy(qkv_ref, qkv_out, sems.at[1]),
    ]
    for copy in copies:
        copy.start()
    size = 128
    chunks = parts * shard // size

    def head(h, carry):
        off = pl.multiple_of(h * HEAD, HEAD)
        key = qkv_ref[pl.ds(channels + off, HEAD), :].T
        value_t = qkv_ref[pl.ds(2 * channels + off, HEAD), :]
        for b in range(parts):
            query_t = qkv_ref[pl.ds(off, HEAD), pl.ds(b * shard, shard)]
            scores = [dot_nn(key[i * size : (i + 1) * size], query_t) for i in range(chunks)]
            top = None
            for score in scores:
                part = jnp.max(score.reshape(size // 8, 8, shard), axis=0)
                top = part if top is None else jnp.maximum(top, part)
            top = jnp.max(top, axis=0, keepdims=True) * (SCALE * LOG2E)
            total, out = None, None
            for i, score in enumerate(scores):
                expos = jnp.exp2(score * (SCALE * LOG2E) - top)
                part = jnp.sum(expos.reshape(size // 8, 8, shard), axis=0)
                term = dot_nn(value_t[:, i * size : (i + 1) * size], expos.astype(BF16))
                total = part if i == 0 else total + part
                out = term if i == 0 else out + term
            total = jnp.sum(total, axis=0, keepdims=True)
            mixed[b][pl.ds(off, HEAD), pl.ds(0, shard)] = (out * (1.0 / total)).astype(BF16)
            lse_ref[pl.ds(h, 1), pl.ds(b * shard, shard)] = top + jnp.log2(total)
        return carry

    lax.fori_loop(0, channels // HEAD, head, 0)
    for copy in copies:
        copy.wait()


def attend(tok, gain, w_rows, *rider):
    parts = len(tok)
    shard, feat = tok[0].shape
    length = parts * shard
    channels = w_rows.shape[0] // 3
    pieces = [len(block) if isinstance(block, tuple) else 1 for block in tok]
    tok = jax.tree.leaves(tok)
    outs = call(
        functools.partial(attend_kernel, parts, pieces, channels, len(rider)),
        [
            Loose(SDS((length, feat), BF16)),
            Loose(SDS((3 * channels, length), BF16)),
            Far(SDS((8, length), F32)),
        ]
        + [SDS((channels, shard + sum(r.shape[1] for r in rider)), BF16)] * parts,
        [*tok, gain, Far(w_rows), *[Far(r) for r in rider]],
        2 * length * feat * 3 * channels + 4 * length * length * channels,
        scratch=[
            VMEM((length, feat), BF16),
            VMEM((3 * channels, length), BF16),
            pltpu.SemaphoreType.DMA((2,)),
        ],
        transcendentals=length * length * channels // HEAD,
    )
    return outs[0], outs[1], outs[2], outs[3:]


def attend_back_kernel(parts, channels, at, *refs):
    qkv_ref, lse_ref = refs[:2]
    shard = qkv_ref.shape[1] // parts
    grad = [ref.at[:, pl.ds(at * shard, shard)] for ref in refs[2 : 2 + parts]]
    refs = refs[2 + parts :]
    outs = refs[:parts]
    key_acc, value_acc = refs[parts:]

    def head(h, carry):
        off = pl.multiple_of(h * HEAD, HEAD)
        key_t = qkv_ref[pl.ds(channels + off, HEAD), :]
        key = key_t.T
        value = qkv_ref[pl.ds(2 * channels + off, HEAD), :].T
        for b in range(parts):
            query_t = qkv_ref[pl.ds(off, HEAD), pl.ds(b * shard, shard)]
            grad_t = grad[b][pl.ds(off, HEAD), :]
            scores = dot_nn(key, query_t)
            probs = jnp.exp2(
                scores * (SCALE * LOG2E) - lse_ref[pl.ds(h, 1), pl.ds(b * shard, shard)]
            )
            grad_probs = dot_nn(value, grad_t)
            inner = jnp.sum(probs * grad_probs, axis=0, keepdims=True)
            grad_scores = (probs * (grad_probs - inner)).astype(BF16)
            value_part = dot_nt(grad_t, probs.astype(BF16))
            key_part = dot_nt(query_t, grad_scores)
            outs[b][pl.ds(off, HEAD), :] = (dot_nn(key_t, grad_scores) * SCALE).astype(BF16)
            if b == 0:
                key_acc[...] = key_part
                value_acc[...] = value_part
            else:
                key_acc[...] += key_part
                value_acc[...] += value_part
        for b in range(parts):
            cols = pl.ds(b * shard, shard)
            outs[b][pl.ds(channels + off, HEAD), :] = (key_acc[:, cols] * SCALE).astype(BF16)
            outs[b][pl.ds(2 * channels + off, HEAD), :] = value_acc[:, cols].astype(BF16)
        return carry

    lax.fori_loop(0, channels // HEAD, head, 0)


def attend_back(qkv, lse, grad, at, cover):
    parts = len(grad)
    channels = grad[0].shape[0]
    length = qkv.shape[1]
    shard = length // parts
    return call(
        functools.partial(attend_back_kernel, parts, channels, at),
        [SDS((3 * channels, shard), BF16)] * parts,
        [Far(qkv), Far(lse), *[Far(g) for g in grad]],
        10 * length * length * channels,
        scratch=[VMEM((HEAD, length), F32)] * 2,
        transcendentals=length * length * channels // HEAD,
        cover=cover,
    )


def gate_parts(raw, embed, member):
    inv = lax.rsqrt(jnp.sum(raw * raw, axis=0, keepdims=True) + 1e-06)
    rows = raw * inv
    embed_inv = lax.rsqrt(jnp.sum(embed * embed, axis=1, keepdims=True) + 1e-06)
    centers = embed * embed_inv
    logits = 3.0 * dot_nn(centers, rows, EXACT)
    expos = jnp.exp(logits - jnp.max(logits, axis=0, keepdims=True))
    probs = expos / jnp.sum(expos, axis=0, keepdims=True)
    gate = jnp.sum(probs * member, axis=0, keepdims=True)
    return inv, rows, embed_inv, centers, probs, gate


def split_rows(row):
    first = row.astype(BF16).astype(F32)
    second = (row - first).astype(BF16).astype(F32)
    third = (row - first) - second
    shape = (8, row.shape[1])
    at = lax.broadcasted_iota(jnp.int32, shape, 0)
    parts = jnp.where(at == 0, first, jnp.where(at == 1, second, jnp.where(at == 2, third, 0.0)))
    return parts.astype(BF16)


def middle_kernel(seqs, parts, groups, *refs):
    refs = list(refs)
    take = lambda n: [refs.pop(0) for _ in range(n)]
    (tok_ref,) = take(1)
    mixed = [take(parts) for _ in range(seqs)]
    gain_ref, route_ref, embed_ref, member_ref, place_ref = take(5)
    hidden_ref, gate_ref, raw_ref, mixed_out, weight_out = take(5)
    packed = take(groups)
    mixed_ref, weight_ref, in_sems, out_sems = take(4)
    rows, feat = tok_ref.shape
    shard = rows // seqs
    channels = mixed[1][0].shape[0]
    cap = rows // groups
    pairs = []
    for m in range(parts):
        at = pl.ds(m * channels, channels)
        pairs.append((mixed[0][m].at[:, pl.ds(shard, feat)], weight_ref.at[at, :]))
        for s in range(seqs):
            pairs.append(
                (mixed[s][m].at[:, pl.ds(0, shard)], mixed_ref.at[at, pl.ds(s * shard, shard)])
            )
    start_all(pairs, in_sems)()
    wait = start_all([(mixed_ref, mixed_out), (weight_ref, weight_out)], out_sems)
    attn = dot_tn(mixed_ref[...], weight_ref[...])
    hidden = tok_ref[...].astype(F32) + attn
    hidden_ref[...] = hidden
    cen, inv = centred(hidden)
    normed = cen * inv * gain_ref[...]
    raw = dot_nt(route_ref[...], normed, EXACT)
    raw_ref[...] = raw
    gate = gate_parts(raw, embed_ref[...], member_ref[...])[-1]
    gate_ref[...] = jnp.broadcast_to(gate, gate_ref.shape)
    low = normed.astype(BF16)
    scalars = split_rows(gate)
    for g in range(groups):
        place = place_ref[pl.ds(g * cap, cap), :]
        packed[g][pl.ds(0, cap), :] = dot_nn(place, low).astype(BF16)
        packed[g][pl.ds(cap, 8), :] = jnp.zeros((8, feat), BF16)
        packed[g][pl.ds(cap, 8), pl.ds(0, cap)] = dot_nt(scalars, place).astype(BF16)
    wait()


def count_digits(rows, devices):
    width = max(1, (256 // devices + 1).bit_length() - 1)
    digits = -(-rows.bit_length() // width)
    return width, digits, 128 if digits <= 6 else 64


def back_kernel(seqs, parts, groups, *refs):
    refs = list(refs)
    take = lambda n: [refs.pop(0) for _ in range(n)]
    packed = take(groups)
    cot_ref, hidden_ref, raw_ref, weight_ref = take(4)
    gain_ref, route_ref, embed_ref, member_ref, place_ref = take(5)
    grad_ref, low_ref, stats_ref = take(3)
    mixed_grad = take(parts)
    (slot_ref,) = take(1)
    rows = hidden_ref.shape[0]
    shard = rows // seqs
    cap = rows // groups
    channels = mixed_grad[0].shape[0]
    scalars = None
    for g in range(groups):
        slot_ref[pl.ds(g * cap, cap), :] = packed[g][pl.ds(0, cap), :]
        scalar = dot_nn(packed[g][pl.ds(cap, 8), pl.ds(0, cap)], place_ref[pl.ds(g * cap, cap), :])
        scalars = scalar if g == 0 else scalars + scalar
    at = lax.broadcasted_iota(jnp.int32, scalars.shape, 0)
    grad_gate = jnp.sum(jnp.where(at < 3, scalars, 0.0), axis=0, keepdims=True)
    cen, inv = centred(hidden_ref[...])
    unit = cen * inv
    gain = gain_ref[...]
    raw_inv, dirs, embed_inv, centers, probs, gate = gate_parts(
        raw_ref[...], embed_ref[...], member_ref[...]
    )
    grad_logits = (3.0 * grad_gate * gate) * (member_ref[...] - probs)
    grad_dirs = dot_tn(centers, grad_logits, EXACT)
    grad_centers = dot_nt(grad_logits, dirs, EXACT)
    grad_raw = raw_inv * (
        grad_dirs - dirs * jnp.sum(dirs * grad_dirs, axis=0, keepdims=True)
    )
    router = route_ref.shape[0]
    experts = embed_ref.shape[0]
    stats_ref[...] = jnp.zeros(stats_ref.shape, F32)
    stats_ref[pl.ds(router + 8, experts), pl.ds(0, router)] = embed_inv * (
        grad_centers - centers * jnp.sum(centers * grad_centers, axis=1, keepdims=True)
    )
    stats_ref[pl.ds(0, router), :] = dot_nn(grad_raw, unit * gain, EXACT)
    count = dot_nt(jnp.ones((8, rows), F32), member_ref[...], EXACT)[:1].astype(jnp.int32)
    width, digits, stride = count_digits(rows, 2 * parts * groups)
    for digit in range(digits):
        part = (count >> (width * digit)) & ((1 << width) - 1)
        stats_ref[pl.ds(router + 1, 1), pl.ds(stride * digit, experts)] = part.astype(F32)
    grad_normed = dot_tn(place_ref[...], slot_ref[...]) + dot_tn(grad_raw, route_ref[...], EXACT)
    stats_ref[pl.ds(router, 1), :] = jnp.sum(grad_normed * unit, axis=0, keepdims=True)
    grad_unit = grad_normed * gain
    grad_hidden = inv * (
        grad_unit
        - jnp.mean(grad_unit, axis=1, keepdims=True)
        - unit * jnp.mean(grad_unit * unit, axis=1, keepdims=True)
    )
    grad_hidden = cot_ref[...].astype(F32) + grad_hidden
    grad_ref[...] = grad_hidden
    low = grad_hidden.astype(BF16)
    low_ref[...] = low
    grad_mixed = dot_nt(weight_ref[...], low).astype(BF16)
    for m in range(parts):
        mixed_grad[m][...] = grad_mixed[m * channels : (m + 1) * channels]


def out_kernel(groups, cap, *refs):
    back = refs[:groups]
    hidden_ref, gate_ref, place_ref, out_ref = refs[groups:]
    mixture = None
    for g in range(groups):
        rows = back[g][pl.ds(back[g].shape[0] - cap, cap), :]
        part = dot_tn(place_ref[pl.ds(g * cap, cap), :], rows)
        mixture = part if g == 0 else mixture + part
    out_ref[...] = hidden_ref[...] + gate_ref[...].T[:, :1] * mixture


def tail_kernel(parts, s, core_ref, *refs):
    refs = list(refs)
    take = lambda n: [refs.pop(0) for _ in range(n)]
    grads = take(parts)
    (weight,) = take(1)
    mine = take(parts - 1)
    theirs, tok_in, gain_ref, hidden_in = take(4)
    out_ref, grad_ref, weight_ref, tok_ref, hidden_grad_ref, sems = refs[-6:]
    shard = tok_ref.shape[0]
    core = core_ref[0]
    rows = weight.shape[0]
    half = rows // 2
    pairs = [(grads[m], grad_ref.at[pl.ds(m * rows, rows), :]) for m in range(parts)]
    pairs.append((weight, weight_ref.at[pl.ds(0, rows), :]))
    for m in range(1, parts):
        near = pl.multiple_of(m * rows + core * half, 16)
        away = pl.multiple_of(m * rows + (1 - core) * half, 16)
        pairs.append((mine[m - 1], weight_ref.at[pl.ds(near, half), :]))
        pairs.append((theirs.at[pl.ds((m - 1) * half, half), :], weight_ref.at[pl.ds(away, half), :]))
    near_tok = start_all([(tok_in.at[pl.ds(s * shard, shard), :], tok_ref)], sems.at[pl.ds(0, 1)])
    pairs.append((hidden_in.at[pl.ds(s * shard, shard), :], hidden_grad_ref))
    wait = start_all(pairs, sems.at[pl.ds(1, len(pairs))])
    near_tok()
    cen, inv = centred(tok_ref[...].astype(F32))
    unit = cen * inv
    wait()
    grad_normed = dot_tn(grad_ref[...], weight_ref[...])
    grad_unit = grad_normed * gain_ref[...]
    out_ref[...] = hidden_grad_ref[...] + inv * (
        grad_unit
        - jnp.mean(grad_unit, axis=1, keepdims=True)
        - unit * jnp.mean(grad_unit * unit, axis=1, keepdims=True)
    )


def gelu_pair(x):
    z = jnp.abs(x) * (0.5**0.5)
    t = 1.0 / (1.0 + ERFC_SLOPE * z)
    poly = jnp.full_like(t, ERFC[-1])
    for value in ERFC[-2::-1]:
        poly = poly * t + value
    bell = jnp.exp2(x * x * (-0.5 * LOG2E))
    tail = (0.5 * bell) * (t * poly)
    cdf = jnp.where(x < 0.0, tail, 1.0 - tail)
    return x * cdf, cdf + x * (bell * 0.3989422804014327)


def expert_kernel(count, steps, *refs):
    refs = list(refs)
    take = lambda n: [refs.pop(0) for _ in range(n)]
    packed, cot = take(count), take(count)
    ups, downs = take(2), take(2)
    cap = cot[0].shape[0]
    returned, grads = [], []
    for i in range(count):
        (ref,) = take(1)
        if ref.shape[0] == cap:
            returned.append(ref)
            grads += take(1)
        else:
            grads.append(ref.at[pl.ds(0, cap + 8), :])
            returned.append(ref.at[pl.ds(cap + 8, cap), :])
    rows_ref, gr_ref = take(2)
    acts, gups = take(2), take(2)
    ret_acc, grad_acc = take(2)
    step = pl.program_id(0)

    def eye():
        shape = (cap, cap)
        return lax.broadcasted_iota(jnp.int32, shape, 0) == lax.broadcasted_iota(jnp.int32, shape, 1)

    @pl.when(step == 0)
    def _():
        for i in range(count):
            part = pl.ds(i * cap, cap)
            rows_ref[part, :] = packed[i][pl.ds(0, cap), :]
            scalars = packed[i][pl.ds(cap, 8), pl.ds(0, cap)].astype(F32)
            at = lax.broadcasted_iota(jnp.int32, scalars.shape, 0)
            row = jnp.sum(jnp.where(at < 3, scalars, 0.0), axis=0, keepdims=True)
            gate = jnp.sum(jnp.where(eye(), row, 0.0), axis=1, keepdims=True)
            gr_ref[part, :] = (gate * cot[i][...].astype(F32)).astype(BF16)

    rows, grad_rows = rows_ref[...], gr_ref[...]
    ret = None
    for h in range(2):
        up_w, down_w = ups[h][...], downs[h][...]
        act, slope = gelu_pair(dot_nn(rows, up_w))
        act = act.astype(BF16)
        gup = (dot_nn(grad_rows, down_w) * slope).astype(BF16)
        acts[h][...] = act
        gups[h][...] = gup
        ret_part = dot_nt(act, down_w)
        grad_part = dot_nt(gup, up_w)
        ret = ret_part if h == 0 else ret + ret_part
        grad = grad_part if h == 0 else grad + grad_part

    @pl.when(step == 0)
    def _():
        ret_acc[...] = ret
        grad_acc[...] = grad

    @pl.when(step > 0)
    def _():
        ret_acc[...] += ret
        grad_acc[...] += grad

    @pl.when(step == steps - 1)
    def _():
        for i in range(count):
            part = pl.ds(i * cap, cap)
            low = ret_acc[part, :].astype(BF16)
            returned[i][...] = low
            product = jnp.sum(low.astype(F32) * cot[i][...].astype(F32), axis=1, keepdims=True)
            row = jnp.sum(jnp.where(eye(), product, 0.0), axis=0, keepdims=True)
            grads[i][pl.ds(0, cap), :] = grad_acc[part, :].astype(BF16)
            grads[i][pl.ds(cap, 8), :] = jnp.zeros((8, grads[i].shape[1]), BF16)
            grads[i][pl.ds(cap, 8), pl.ds(0, cap)] = split_rows(row)


def expert(packed, cot, cap, up_own, up_other, down_own, down_other, joined=()):
    count = len(cot)
    feat, units = up_own.shape
    width = 512 if units % 512 == 0 else units
    steps = units // width
    rows = count * cap

    def same(size, at=0):
        return pl.BlockSpec((size, feat), lambda j: (at, 0))

    weight = pl.BlockSpec((feat, width), lambda j: (0, j))
    wide = pl.BlockSpec((rows, width), lambda j: (0, j))
    sizes = []
    for i in range(count):
        sizes += [2 * cap + 8] if i in joined else [cap, cap + 8]
    outs = pl.pallas_call(
        functools.partial(expert_kernel, count, steps),
        grid=(steps,),
        in_specs=[same(cap + 8, at) for _, at in packed]
        + [same(cap, at) for _, at in cot]
        + [weight] * 4,
        out_specs=[same(size) for size in sizes] + [same(rows)] * 2 + [wide] * 4,
        out_shape=[SDS((size, feat), BF16) for size in sizes]
        + [pltpu.HBM((rows, feat), BF16)] * 2
        + [pltpu.HBM((rows, units), BF16)] * 4,
        scratch_shapes=[VMEM((rows, feat), F32)] * 2,
        compiler_params=pltpu.CompilerParams(
            vmem_limit_bytes=24 << 20, dimension_semantics=("arbitrary",)
        ),
        cost_estimate=cost(
            16 * rows * feat * units, 8 * feat * units + 16 * rows * units, 4 * rows * units
        ),
    )(
        *[a for a, _ in packed],
        *[in_hbm(a) for a, _ in cot],
        *[in_hbm(w) for w in (up_own, up_other, down_own, down_other)],
    )
    back, grads = [], []
    at = 0
    for i in range(count):
        back.append(outs[at])
        if i not in joined:
            at += 1
        grads.append(outs[at])
        at += 1
    return back, grads, outs[at], outs[at + 1], outs[at + 2 : at + 4], outs[at + 4 :]


def expert_grad_kernel(halves, me_ref, *refs):
    refs = list(refs)
    take = lambda n: [refs.pop(0) for _ in range(n)]
    lefts = [take(halves) for _ in range(2)]
    wides = [[take(2) for _ in range(halves)] for _ in range(2)]
    own_ref, other_ref = take(2)
    turned = take(2)
    size = lefts[0][0].shape[0]

    @pl.when(pl.program_id(0) == 0)
    def _():
        for which in range(2):
            for i in range(halves):
                turned[which][:, pl.ds(i * size, size)] = lefts[which][i][...].T

    for which in range(2):
        for h, ref in enumerate((own_ref, other_ref)):
            full = jnp.concatenate([wides[which][i][h][...] for i in range(halves)], axis=0)
            ref[which, 0] = dot_nn(turned[which][...], full).astype(ref.dtype)


def expert_grad(me, rows, grad_rows, gups, acts, tensor_size):
    halves = len(rows)
    size, feat = rows[0].shape
    units = gups[0][0].shape[1]
    width = units // tensor_size
    same = pl.BlockSpec((size, feat), lambda j, me: (0, 0))
    part = pl.BlockSpec((size, width), lambda j, me: (0, me[0] ^ j))
    block = pl.BlockSpec((2, 1, feat, width), lambda j, me: (0, j, 0, 0))
    shape = (2, tensor_size, feat, width)
    wides = [a for pairs in (gups, acts) for pair in pairs for a in pair]
    return pl.pallas_call(
        functools.partial(expert_grad_kernel, halves),
        grid_spec=pltpu.PrefetchScalarGridSpec(
            num_scalar_prefetch=1,
            grid=(tensor_size,),
            in_specs=[same] * (2 * halves) + [part] * (4 * halves),
            out_specs=[block, block],
            scratch_shapes=[VMEM((feat, halves * size), BF16)] * 2,
        ),
        out_shape=[pltpu.HBM(shape, BF16), pltpu.HBM(shape, BF16)],
        compiler_params=pltpu.CompilerParams(
            vmem_limit_bytes=24 << 20, dimension_semantics=("arbitrary",)
        ),
        cost_estimate=cost(8 * halves * size * feat * units, 24 << 20),
    )(me.reshape(1), *[in_hbm(a) for a in (*rows, *grad_rows, *wides)])


def pair_kernel(*refs):
    for i in range(2):
        for j in range(2):
            own, recv = refs[4 * i + 2 * j : 4 * i + 2 * j + 2]
            refs[8 + i][j] = (own[0, 0].astype(F32) + recv[0, 0].astype(F32)).astype(BF16)


def first_pairs(own, recv, picks):
    feat, width = own.shape[2:]
    block = (1, 1, feat, width)
    args = []
    for which in range(2):
        for m in picks[which]:
            args += [Far(own, block, (which, m)), Here(recv, block, (which, m))]
    return call(pair_kernel, [SDS((2, feat, width), BF16)] * 2, args, 4 * feat * width)


def out_grad_kernel(core_ref, mixed_ref, low_ref, keep_ref, send_ref, full_ref):
    core = core_ref[0]
    parts, half, _ = keep_ref.shape
    full_ref[...] = dot_nn(mixed_ref[...], low_ref[...])
    for m in range(parts):
        near = pl.multiple_of((2 * m + core) * half, half)
        away = pl.multiple_of((2 * m + 1 - core) * half, half)
        keep_ref[m] = full_ref[pl.ds(near, half), :]
        send_ref[m] = full_ref[pl.ds(away, half), :].astype(BF16)


def qkv_grad_kernel(seqs, parts, core_ref, *refs):
    grads = [refs[s * parts : (s + 1) * parts] for s in range(seqs)]
    normed = refs[seqs * parts : seqs * parts + seqs]
    w_in, keep_ref, send_ref, norm1_ref = refs[seqs * parts + seqs :][:4]
    full_ref, grad_ref, normed_ref, w_ref, sems = refs[seqs * parts + seqs + 4 :]
    send_ref, extra_ref = send_ref.at[pl.ds(0, keep_ref.shape[0]), :], send_ref
    core = core_ref[0]
    shard = grads[0][0].shape[1]
    half = keep_ref.shape[0]
    pairs = []
    for s in range(seqs):
        for b in range(parts):
            pairs.append((grads[s][b], grad_ref.at[s, :, pl.ds(b * shard, shard)]))
        pairs.append((normed[s], normed_ref.at[s]))
    pairs.append((w_in, w_ref))
    start_all(pairs, sems)()
    total = dot_nn(grad_ref[0], normed_ref[0])
    for s in range(1, seqs):
        total += dot_nn(grad_ref[s], normed_ref[s])
    full_ref[...] = total
    norm1 = jnp.sum(total * w_ref[...].astype(F32), axis=0, keepdims=True)
    norm1_ref[...] = norm1
    terms = jnp.concatenate([split_rows(norm1), split_rows(jnp.zeros_like(norm1))], axis=0)
    extra_ref[pl.ds(keep_ref.shape[0], 16), :] = terms
    keep_ref[...] = full_ref[pl.ds(pl.multiple_of(core * half, half), half), :]
    send_ref[...] = full_ref[pl.ds(pl.multiple_of((1 - core) * half, half), half), :].astype(BF16)


def program(tensor_size, expert_size):
    chips = expert_size // 2
    bits = chips.bit_length() - 1

    def over_tensor(values, mask):
        return lax.ppermute(values, "tensor", [(i, i ^ mask) for i in range(tensor_size)])

    def over_core(values):
        return lax.ppermute(values, "expert", [(i, i ^ 1) for i in range(expert_size)])

    def over_chip(values, mask):
        return lax.ppermute(values, "expert", [(i, i ^ (2 * mask)) for i in range(expert_size)])

    def from_tensor(blocks):
        return [blocks[0]] + [over_tensor(blocks[m], m) for m in range(1, tensor_size)]

    def gather_first(block):
        if tensor_size != 4:
            return from_tensor([block] * tensor_size)
        half = block.shape[0] // 2
        one, two = over_tensor(block, 1), over_tensor(block, 2)
        low, high = over_tensor(one[:half], 2), over_tensor(two[half:], 1)
        return [block, one, two, (low, high)]

    def swap_chips(blocks):
        if chips <= 4:
            return [blocks[0]] + [over_chip(blocks[m], m) for m in range(1, chips)]
        chip = lax.axis_index("expert") // 2
        order = chip ^ jnp.arange(chips)
        groups = [[2 * i + core for i in range(chips)] for core in range(2)]
        moved = lax.all_to_all(
            jnp.stack(blocks)[order],
            "expert",
            split_axis=0,
            concat_axis=0,
            tiled=True,
            axis_index_groups=groups,
        )[order]
        return [moved[m] for m in range(chips)]

    if chips == 4:
        masks = (1, 3)
    else:
        masks = tuple(1 << bit for bit in range(bits))

    def chip_bit(level):
        chip = lax.axis_index("expert") // 2
        if chips == 4:
            return ((chip ^ (chip >> 1)) & 1) if level == 0 else (chip >> 1) & 1
        return (chip >> level) & 1

    def halves(values, bit):
        half = values.shape[0] // 2
        low, high = values[:half], values[half:]
        return jnp.where(bit == 0, low, high), jnp.where(bit == 0, high, low)

    def joined(mine, theirs, bit):
        return jnp.concatenate(
            [jnp.where(bit == 0, mine, theirs), jnp.where(bit == 0, theirs, mine)], axis=0
        )

    def body(
        tokens,
        out_grad,
        masked,
        route,
        norm1_gain,
        query_key_value_weight,
        output_weight,
        norm2_gain,
        route_weight,
        expert_embed,
        up_weight,
        down_weight,
    ):
        seqs, shard, feat = tokens.shape
        rows_here = seqs * shard
        experts, router = expert_embed.shape
        cap = rows_here // experts
        channels = query_key_value_weight.shape[2]
        units = up_weight.shape[2]
        parts = tensor_size
        me = lax.axis_index("tensor")
        place_index = lax.axis_index("expert")
        chip, core = place_index // 2, place_index % 2
        gain1 = norm1_gain.reshape(1, feat)
        gain2 = norm2_gain.reshape(1, feat)

        w_rows = query_key_value_weight.transpose(0, 2, 1).reshape(3 * channels, feat)
        half_rows = 3 * channels // 2
        w_half = lax.dynamic_slice_in_dim(w_rows, core * half_rows, half_rows, axis=0)
        gathered = [gather_first(tokens[0])]
        for s in range(1, seqs):
            gathered.append(from_tensor([tie(tokens[s], gathered[-1])] * parts))

        picks = route.reshape(rows_here)
        expert_ids = jnp.arange(experts, dtype=jnp.int32)
        member = (picks[:, None] == expert_ids[None, :]).astype(jnp.int32)
        earlier = jnp.cumsum(member, axis=0) - member
        slot_ids = jnp.sum(earlier * member, axis=1)
        target = (picks ^ chip) * cap + slot_ids
        target = jnp.where(slot_ids < cap, target, -1)
        slot_range = jnp.arange(experts * cap, dtype=jnp.int32)
        placing = (slot_range[:, None] == target[None, :]).astype(BF16)
        member_t = (expert_ids[:, None] == picks[None, :]).astype(F32)
        cotangent = out_grad.reshape(rows_here, feat) * masked.reshape(rows_here, 1).astype(BF16)
        sent_cotangent = dot_nn(placing, cotangent).astype(BF16)
        if experts == 4:
            cot_one = over_chip(sent_cotangent[cap : 3 * cap], 1)
            cot_held = jnp.concatenate([sent_cotangent[3 * cap :], cot_one[cap:]], axis=0)
            slot_cotangent = [(sent_cotangent, 0), (cot_one, 0)]
        else:
            slot_cotangent = [
                (block, 0)
                for block in swap_chips(
                    [sent_cotangent[g * cap : (g + 1) * cap] for g in range(experts)]
                )
            ]

        normed, qkv, lse, mixed = [], [], [], []
        up_other, down_other = over_core(up_weight[0]), over_core(down_weight[0])
        for s in range(seqs):
            if s == 0:
                gathered[0] = tie(
                    gathered[0], sent_cotangent, member_t, w_half, up_other, down_other
                )
            if s == 1:
                gathered[s] = tie(gathered[s], slot_cotangent[1][0], lse[0])
                if experts == 4:
                    cot_two = over_chip(tie(cot_held, lse[0]), 3)
                    slot_cotangent += [(cot_two, 0), (cot_two, 1)]
            rider = (output_weight,) if s == 0 else ()
            n, q, l, blocks = attend(gathered[s], gain1, w_rows, *rider)
            normed.append(n)
            qkv.append(q)
            lse.append(l)
            mixed.append(from_tensor(blocks if s == 0 else tie(blocks, mixed[0][1:])))

        flat_tokens = tokens.reshape(rows_here, feat)
        route_t = route_weight.T
        ready = tie(mixed, [block for block, _ in slot_cotangent[1:]])
        copies = parts * (seqs + 1)
        hidden, gate, raw, mixed_all, out_weight_all, *packed = call(
            functools.partial(middle_kernel, seqs, parts, experts),
            [
                Far(SDS((rows_here, feat), F32)),
                Far(SDS((8, rows_here), F32)),
                Far(SDS((router, rows_here), F32)),
                Loose(SDS((feat, rows_here), BF16)),
                Loose(SDS((feat, feat), BF16)),
            ]
            + [SDS((cap + 8, feat), BF16)] * experts,
            [Far(flat_tokens), *[Free(b) for blocks in ready for b in blocks]]
            + [gain2, route_t, expert_embed, member_t, Far(placing)],
            4 * rows_here * feat * feat,
            scratch=[
                VMEM((feat, rows_here), BF16),
                VMEM((feat, feat), BF16),
                pltpu.SemaphoreType.DMA((copies,)),
                pltpu.SemaphoreType.DMA((2,)),
            ],
        )

        half = experts // 2
        expert_weights = (up_weight[0], up_other, down_weight[0], down_other)
        w_held = tie(w_half, packed)
        w_near = [over_tensor(w_held, m) for m in range(1, parts - 1)]
        if experts == 4:
            one = over_chip(packed[1], 1)
            held = tie(packed[2:], one)
            two, three = over_chip(held[0], 2), over_chip(held[1], 3)
            slot_rows = [(packed[0], 0), (one, 0)]
            low_half = expert(slot_rows[:2], slot_cotangent[:2], cap, *expert_weights, joined=(1,))
            near = over_chip(low_half[1][1], 1)
            three, two, w_near = tie((three, two, w_near), low_half[1])
            w_far = over_tensor(tie(w_half, w_near), parts - 1)
            high_half = expert([(three, 0), (two, 0)], slot_cotangent[2:], cap, *expert_weights)
        else:
            slot_rows = [(block, 0) for block in swap_chips(packed)]
            low_half = expert(slot_rows[:half], slot_cotangent[:half], cap, *expert_weights)
            high_half = expert(slot_rows[half:], slot_cotangent[half:], cap, *expert_weights)
            w_far = over_tensor(tie(w_half, w_near), parts - 1)
            near = ()
        results = [low_half, high_half]
        rows = [r[2] for r in results]
        grad_rows = [r[3] for r in results]
        acts = [r[4] for r in results]
        gups = [r[5] for r in results]
        w_mine = [*w_near, w_far]
        rows, near = tie((rows, near), w_far)
        grad_own, grad_send = expert_grad(me, rows, grad_rows, gups, acts, parts)
        if experts == 4:
            back_grad = [
                low_half[1][0],
                near,
                over_chip(high_half[1][1], 2),
                over_chip(high_half[1][0], 3),
            ]
        else:
            back_grad = swap_chips(low_half[1] + high_half[1])
        back_grad, grad_send, w_mine = tie((back_grad, grad_send, w_mine), grad_send)
        grad_recv = over_core(grad_send)
        w_theirs = over_core(jnp.concatenate(w_mine, axis=0))

        outs = call(
            functools.partial(back_kernel, seqs, parts, experts),
            [
                Far(SDS((rows_here, feat), F32)),
                Far(SDS((rows_here, feat), BF16)),
                SDS((router + 8 + -(-experts // 8) * 8, feat), F32),
            ]
            + [SDS((channels, rows_here), BF16)] * parts,
            [*back_grad, Far(cotangent), Far(hidden), Far(raw), Far(out_weight_all)]
            + [gain2, route_t, expert_embed, member_t, Far(placing)],
            4 * rows_here * feat * feat,
            scratch=[VMEM((rows_here, feat), BF16)],
        )
        grad_hidden, grad_low, stats = outs[:3]
        grad_mixed = from_tensor(outs[3:])
        up_own, down_own = grad_own[0], grad_own[1]
        up_recv, down_recv = grad_recv[0], grad_recv[1]
        up_pair, down_pair = first_pairs(grad_own, grad_recv, ((1, parts - 1), (2, parts - 1)))

        out_half = channels // 2
        out_keep, out_send = call(
            out_grad_kernel,
            [SDS((parts, out_half, feat), F32), SDS((parts, out_half, feat), BF16)],
            [Far(mixed_all), Far(tie(grad_low, up_pair, down_pair))],
            2 * rows_here * feat * feat,
            [VMEM((feat, feat), F32)],
            scalar=core,
        )
        out_keep = out_keep + over_core(out_send).astype(F32)
        stat_high = lax.reduce_precision(stats, 8, 7)
        stat_low = lax.reduce_precision(stats - stat_high, 8, 7)
        stat_terms = jnp.concatenate([stat_high, stat_low], axis=0).astype(BF16)
        out_ride = [
            jnp.concatenate([out_keep[m].astype(BF16), stat_terms], axis=0) for m in range(1, parts)
        ]

        if experts == 4:
            two, three = tie((high_half[0][1], high_half[0][0]), out_send)
            back = [low_half[0][0], near, over_chip(two, 2), over_chip(three, 3)]
        else:
            back = swap_chips(low_half[0] + high_half[0])

        if parts == 4:
            up_got = over_tensor(tie(up_pair, grad_mixed), 1)
            down_got = over_tensor(tie(down_pair, grad_mixed), 2)
        else:
            up_got, down_got = (), ()

        def second(own, recv, got, mask):
            return (own[mask].astype(F32) + recv[mask].astype(F32) + got[1].astype(F32)).astype(BF16)

        def final(own, recv, got, last):
            total = own[0].astype(F32) + recv[0].astype(F32)
            return (total + got[0].astype(F32) + last.astype(F32))[None]

        def slow_scatter(own, recv):
            total = own[0].astype(F32) + recv[0].astype(F32)
            for m in range(1, parts):
                part = own[m].astype(F32) + recv[m].astype(F32)
                total = total + over_tensor(part.astype(BF16), m).astype(F32)
            return total[None]

        grads = []
        came = tie(grad_mixed, out_send, w_theirs)
        for s in range(seqs):
            if s == 1:
                came = tie(came, grads[0])
            grads.append(
                attend_back(qkv[s], lse[s], came, s, cover=COVER if s == 0 else LAST_COVER)
            )
            if s == 0:
                out_held = tie(out_ride, grads[0], back)
                out_got = [over_tensor(out_held[m - 1], m) for m in range(1, parts)]
        split = 3 * channels // 2
        qkv_keep, qkv_send, norm1_grad = call(
            functools.partial(qkv_grad_kernel, seqs, parts),
            [SDS((split, feat), F32), SDS((split + 16, feat), BF16), SDS((1, feat), F32)],
            [Free(b) for blocks in tie(grads, up_got, down_got) for b in blocks]
            + [Free(in_hbm(n)) for n in normed]
            + [Free(w_rows)],
            2 * seqs * parts * shard * 3 * channels * feat,
            [
                VMEM((3 * channels, feat), F32),
                VMEM((seqs, 3 * channels, parts * shard), BF16),
                VMEM((seqs, parts * shard, feat), BF16),
                VMEM((3 * channels, feat), BF16),
                pltpu.SemaphoreType.DMA((seqs * parts + seqs + 1,)),
            ],
            scalar=core,
            cover=0,
        )
        out_half = out_keep.shape[1]
        out_part = sum((got[:out_half].astype(F32) for got in out_got), out_keep[0])
        size = stats.shape[0]

        def both_terms(terms):
            return terms[:size].astype(F32) + terms[size:].astype(F32)

        terms = [both_terms(t) for t in [stat_terms] + [got[out_half:] for got in out_got]]
        while len(terms) > 1:
            terms = [terms[i] + terms[i + 1] for i in range(0, len(terms), 2)]
        stats = terms[0] + over_core(terms[0])

        grad_blocks = [from_tensor(tie(grads[0], out_got, up_got, down_got))]
        qkv_recv = over_core(qkv_send)
        def tail(s, *after):
            before = [Free(input_grads[-1])] if s > 0 else []
            (input_part,) = call(
                functools.partial(tail_kernel, parts, s),
                [Far(SDS((rows_here, feat), F32), (shard, feat), s)],
                [*map(Free, tie(grad_blocks[s], *after)), Free(w_rows)]
                + [Free(in_hbm(w)) for w in (*w_mine, w_theirs)]
                + [Free(flat_tokens), gain1]
                + [Free(grad_hidden), *before],
                2 * shard * feat * 3 * channels * parts,
                [
                    VMEM((parts * 3 * channels, shard), BF16),
                    VMEM((parts * 3 * channels, feat), BF16),
                    VMEM((shard, feat), BF16),
                    VMEM((shard, feat), F32),
                    pltpu.SemaphoreType.DMA((3 * parts + 1,)),
                ],
                scalar=core,
                aliases={2 * parts + 5: 0} if s > 0 else None,
            )
            return input_part

        qkv_keep = qkv_keep + qkv_recv[:split].astype(F32)
        norm1_grad = norm1_grad + jnp.sum(qkv_recv[split : split + 3].astype(F32), axis=0, keepdims=True)
        stats = stats + jnp.pad(norm1_grad, ((router + 2, size - router - 3), (0, 0)))
        values = jnp.concatenate([qkv_keep, out_part, stats], axis=0)
        values = jnp.pad(values, ((0, -values.shape[0] % (8 << bits)), (0, 0)))
        input_grads = []
        up_last = down_last = ()
        for level, mask in enumerate(masks):
            keep, send = halves(values, chip_bit(level))
            send = send.astype(BF16)
            came = over_chip(send, mask)
            if level == 0:
                (result,) = call(
                    functools.partial(out_kernel, experts, cap),
                    [Far(SDS((rows_here, feat), F32))],
                    [Far(b) for b in tie(back, send)]
                    + [Far(hidden), Far(gate), Far(placing)],
                    2 * rows_here * rows_here * feat,
                    cover=0,
                )
                came = tie(came, result)
            if level == 1:
                grad_blocks.append(from_tensor(tie(grads[1], grad_blocks[0], send)))
                input_grads.append(tail(0, send))
                came = tie(came, input_grads[0])
            values = keep + came.astype(F32)
        summed = values.astype(BF16)
        if parts == 4:
            held = tie((up_got, down_got), summed)
            up_held = second(up_own, up_recv, held[0], 2)
            down_held = second(down_own, down_recv, held[1], 1)
            up_last = over_tensor(up_held, 2)
            down_last = over_tensor(down_held, 1)
            input_grads.append(tail(1, up_held, down_held, summed))
            up_last, down_last = tie((up_last, down_last), input_grads[1])
        else:
            input_grads.append(tail(1, summed))
        for level in reversed(range(bits)):
            summed = joined(summed, over_chip(summed, masks[level]), chip_bit(level))
        other_half = over_core(summed[: split + out_half])
        stats = summed[split + out_half :].astype(F32)
        query_key_value_gradient = (
            joined(summed[:split], other_half[:split], core)
            .reshape(3, channels, feat)
            .transpose(0, 2, 1)
            .astype(F32)
        )
        ends = slice(split, split + out_half)
        out_proj_grad = joined(summed[ends], other_half[ends], core).astype(F32)
        if parts == 4:
            up_weight_grad = final(up_own, up_recv, up_got, up_last)
            down_weight_grad = final(down_own, down_recv, down_got, down_last)
        else:
            up_weight_grad = slow_scatter(up_own, up_recv)
            down_weight_grad = slow_scatter(down_own, down_recv)

        beside = [(up_weight_grad, down_weight_grad), (query_key_value_gradient, out_proj_grad)]
        norm1_grad = stats[router + 2 : router + 3]
        mask = 1
        while mask < tensor_size:
            came = over_tensor(norm1_grad, mask)
            if beside:
                came = tie(came, beside.pop(0))
            norm1_grad = norm1_grad + came
            mask *= 2
        route_grad = stats[:router].T
        norm2_grad = stats[router]
        norm1_grad = norm1_grad[0] / norm1_gain
        width, digits, stride = count_digits(rows_here, 2 * parts * experts)
        loads = sum(
            stats[router + 1, stride * i : stride * i + experts] * float(1 << (width * i))
            for i in range(digits)
        )
        embed_grad = stats[router + 8 : router + 8 + experts, :router]

        return (
            result.reshape(seqs, shard, feat),
            input_grads[-1].reshape(seqs, shard, feat),
            loads,
            norm1_grad,
            query_key_value_gradient,
            out_proj_grad,
            norm2_grad,
            route_grad,
            embed_grad,
            up_weight_grad,
            down_weight_grad,
        )

    return body


def solution(mesh):
    return jax.shard_map(
        program(mesh.shape["tensor"], mesh.shape["expert"]),
        mesh=mesh,
        in_specs=(
            P("expert", "tensor", None),
            P("expert", "tensor", None),
            P("expert", "tensor"),
            P("expert", "tensor", None),
            P(),
            P(None, None, "tensor"),
            P("tensor", None),
            P(),
            P(),
            P(),
            P("expert", None, None),
            P("expert", None, None),
        ),
        out_specs=(
            P("expert", "tensor", None),
            P("expert", "tensor", None),
            P(),
            P(),
            P(None, None, "tensor"),
            P("tensor", None),
            P(),
            P(),
            P(),
            P("expert", None, "tensor"),
            P("expert", None, "tensor"),
        ),
        check_vma=False,
    )
```

```python
import functools

import jax
import jax.numpy as jnp
from jax import lax
from jax.experimental import pallas as pl
from jax.experimental.pallas import tpu as pltpu
from jax.sharding import PartitionSpec as P

HEAD = 64
F32 = jnp.float32
BF16 = jnp.bfloat16
LOG2E = 1.4426950408889634
SCALE = HEAD**-0.5
EXACT = lax.Precision.HIGHEST
SDS = jax.ShapeDtypeStruct
VMEM = pltpu.VMEM
COVER = 4
LAST_COVER = 0

ERFC_SLOPE = 0.44
ERFC = (
    0.248227568,
    0.248777028,
    0.217859919,
    0.214130365,
    -0.0172025688,
    0.293641958,
    -0.276276279,
    0.0708421859,
)


def dot_nn(left, right, precision=None):
    return jnp.dot(left, right, preferred_element_type=F32, precision=precision)


def dot_nt(left, right, precision=None):
    return lax.dot_general(
        left, right, (((1,), (1,)), ((), ())), preferred_element_type=F32, precision=precision
    )


def dot_tn(left, right, precision=None):
    return lax.dot_general(
        left, right, (((0,), (0,)), ((), ())), preferred_element_type=F32, precision=precision
    )


class Far:
    def __init__(self, value, block=None, at=0):
        self.value = value
        self.block = value.shape if block is None else block
        self.at = at


class Here(Far):
    pass


class Loose(Far):
    pass


class Free(Far):
    pass


def start_all(pairs, sems):
    copies = [pltpu.make_async_copy(a, b, sems.at[i]) for i, (a, b) in enumerate(pairs)]
    for copy in copies:
        copy.start()

    def wait():
        for copy in copies:
            copy.wait()

    return wait


def plain(value):
    return value.value if isinstance(value, Far) else value


def in_hbm(value):
    return pltpu.with_memory_space_constraint(value, pltpu.HBM)


def cost(flops, size, transcendentals=0, cover=COVER):
    return pl.CostEstimate(
        flops=flops * cover, bytes_accessed=size * cover, transcendentals=transcendentals * cover
    )


def call(kernel, outs, args, flops, scratch=(), limit=24, transcendentals=0, scalar=None, cover=COVER, aliases=None):
    whole = pl.BlockSpec(memory_space=VMEM)

    def spec(arg):
        if isinstance(arg, Loose):
            return pl.BlockSpec(memory_space=pl.ANY)
        if not isinstance(arg, Far):
            return whole
        if isinstance(arg, (Loose, Free)):
            return pl.BlockSpec(memory_space=pl.ANY)
        where = arg.at if isinstance(arg.at, tuple) else (arg.at,)
        where += (0,) * (arg.value.ndim - len(where))
        return pl.BlockSpec(
            arg.block, lambda i: where, pipeline_mode=pl.Buffered(buffer_count=1)
        )

    specs = [spec(a) for a in args]
    out_specs = [spec(o) for o in outs]
    size = sum(a.size * a.dtype.itemsize for a in map(plain, args))
    size += sum(o.size * o.dtype.itemsize for o in map(plain, outs))
    args = [
        a.value if isinstance(a, (Free, Here)) else in_hbm(a.value) if isinstance(a, Far) else a for a in args
    ]
    outs = [pltpu.HBM(o.value.shape, o.value.dtype) if isinstance(o, Far) else o for o in outs]
    if scalar is not None:
        specs = [pl.BlockSpec(memory_space=pltpu.SMEM)] + specs
        args = [scalar.reshape(1)] + args
    return pl.pallas_call(
        kernel,
        grid=(1,),
        out_shape=list(outs),
        in_specs=specs,
        out_specs=out_specs,
        scratch_shapes=list(scratch),
        input_output_aliases=aliases or {},
        compiler_params=pltpu.CompilerParams(vmem_limit_bytes=limit << 20),
        cost_estimate=cost(flops, size, transcendentals, cover),
    )(*args)


def centred(x):
    cen = x - jnp.mean(x, axis=1, keepdims=True)
    return cen, lax.rsqrt(jnp.mean(cen * cen, axis=1, keepdims=True) + 1e-05)


def tie(values, *after):
    return lax.optimization_barrier((values, after))[0]


def attend_kernel(parts, pieces, channels, riding, *refs):
    tok = refs[: sum(pieces)]
    refs = refs[sum(pieces) :]
    gain_ref, w_ref = refs[:2]
    rider = refs[2 : 2 + riding]
    refs = refs[2 + riding :]
    normed_out, qkv_out, lse_ref = refs[:3]
    mixed = refs[3 : 3 + parts]
    normed_ref, qkv_ref, sems = refs[3 + parts :]
    shard = tok[0].shape[0]
    for ref in rider:
        for b in range(parts):
            mixed[b][:, pl.ds(shard, ref.shape[1])] = ref[...]
    at = 0
    for ref in tok:
        size = ref.shape[0]
        cen, inv = centred(ref[...].astype(F32))
        rows = (cen * inv * gain_ref[...]).astype(BF16)
        normed_ref[pl.ds(at, size), :] = rows
        qkv_ref[:, pl.ds(at, size)] = dot_nt(w_ref[...], rows).astype(BF16)
        at += size
    copies = [
        pltpu.make_async_copy(normed_ref, normed_out, sems.at[0]),
        pltpu.make_async_copy(qkv_ref, qkv_out, sems.at[1]),
    ]
    for copy in copies:
        copy.start()
    size = 128
    chunks = parts * shard // size

    def head(h, carry):
        off = pl.multiple_of(h * HEAD, HEAD)
        key = qkv_ref[pl.ds(channels + off, HEAD), :].T
        value_t = qkv_ref[pl.ds(2 * channels + off, HEAD), :]
        for b in range(parts):
            query_t = qkv_ref[pl.ds(off, HEAD), pl.ds(b * shard, shard)]
            scores = [dot_nn(key[i * size : (i + 1) * size], query_t) for i in range(chunks)]
            top = None
            for score in scores:
                part = jnp.max(score.reshape(size // 8, 8, shard), axis=0)
                top = part if top is None else jnp.maximum(top, part)
            top = jnp.max(top, axis=0, keepdims=True) * (SCALE * LOG2E)
            total, out = None, None
            for i, score in enumerate(scores):
                expos = jnp.exp2(score * (SCALE * LOG2E) - top)
                part = jnp.sum(expos.reshape(size // 8, 8, shard), axis=0)
                term = dot_nn(value_t[:, i * size : (i + 1) * size], expos.astype(BF16))
                total = part if i == 0 else total + part
                out = term if i == 0 else out + term
            total = jnp.sum(total, axis=0, keepdims=True)
            mixed[b][pl.ds(off, HEAD), pl.ds(0, shard)] = (out * (1.0 / total)).astype(BF16)
            lse_ref[pl.ds(h, 1), pl.ds(b * shard, shard)] = top + jnp.log2(total)
        return carry

    lax.fori_loop(0, channels // HEAD, head, 0)
    for copy in copies:
        copy.wait()


def attend(tok, gain, w_rows, *rider):
    parts = len(tok)
    shard, feat = tok[0].shape
    length = parts * shard
    channels = w_rows.shape[0] // 3
    pieces = [len(block) if isinstance(block, tuple) else 1 for block in tok]
    tok = jax.tree.leaves(tok)
    outs = call(
        functools.partial(attend_kernel, parts, pieces, channels, len(rider)),
        [
            Loose(SDS((length, feat), BF16)),
            Loose(SDS((3 * channels, length), BF16)),
            Far(SDS((8, length), F32)),
        ]
        + [SDS((channels, shard + sum(r.shape[1] for r in rider)), BF16)] * parts,
        [*tok, gain, Far(w_rows), *[Far(r) for r in rider]],
        2 * length * feat * 3 * channels + 4 * length * length * channels,
        scratch=[
            VMEM((length, feat), BF16),
            VMEM((3 * channels, length), BF16),
            pltpu.SemaphoreType.DMA((2,)),
        ],
        transcendentals=length * length * channels // HEAD,
    )
    return outs[0], outs[1], outs[2], outs[3:]


def attend_back_kernel(parts, channels, at, *refs):
    qkv_ref, lse_ref = refs[:2]
    shard = qkv_ref.shape[1] // parts
    grad = [ref.at[:, pl.ds(at * shard, shard)] for ref in refs[2 : 2 + parts]]
    refs = refs[2 + parts :]
    outs = refs[:parts]
    key_acc, value_acc = refs[parts:]

    def head(h, carry):
        off = pl.multiple_of(h * HEAD, HEAD)
        key_t = qkv_ref[pl.ds(channels + off, HEAD), :]
        key = key_t.T
        value = qkv_ref[pl.ds(2 * channels + off, HEAD), :].T
        for b in range(parts):
            query_t = qkv_ref[pl.ds(off, HEAD), pl.ds(b * shard, shard)]
            grad_t = grad[b][pl.ds(off, HEAD), :]
            scores = dot_nn(key, query_t)
            probs = jnp.exp2(
                scores * (SCALE * LOG2E) - lse_ref[pl.ds(h, 1), pl.ds(b * shard, shard)]
            )
            grad_probs = dot_nn(value, grad_t)
            inner = jnp.sum(probs * grad_probs, axis=0, keepdims=True)
            grad_scores = (probs * (grad_probs - inner)).astype(BF16)
            value_part = dot_nt(grad_t, probs.astype(BF16))
            key_part = dot_nt(query_t, grad_scores)
            outs[b][pl.ds(off, HEAD), :] = (dot_nn(key_t, grad_scores) * SCALE).astype(BF16)
            if b == 0:
                key_acc[...] = key_part
                value_acc[...] = value_part
            else:
                key_acc[...] += key_part
                value_acc[...] += value_part
        for b in range(parts):
            cols = pl.ds(b * shard, shard)
            outs[b][pl.ds(channels + off, HEAD), :] = (key_acc[:, cols] * SCALE).astype(BF16)
            outs[b][pl.ds(2 * channels + off, HEAD), :] = value_acc[:, cols].astype(BF16)
        return carry

    lax.fori_loop(0, channels // HEAD, head, 0)


def attend_back(qkv, lse, grad, at, cover):
    parts = len(grad)
    channels = grad[0].shape[0]
    length = qkv.shape[1]
    shard = length // parts
    return call(
        functools.partial(attend_back_kernel, parts, channels, at),
        [SDS((3 * channels, shard), BF16)] * parts,
        [Far(qkv), Far(lse), *[Far(g) for g in grad]],
        10 * length * length * channels,
        scratch=[VMEM((HEAD, length), F32)] * 2,
        transcendentals=length * length * channels // HEAD,
        cover=cover,
    )


def gate_parts(raw, embed, member):
    inv = lax.rsqrt(jnp.sum(raw * raw, axis=0, keepdims=True) + 1e-06)
    rows = raw * inv
    embed_inv = lax.rsqrt(jnp.sum(embed * embed, axis=1, keepdims=True) + 1e-06)
    centers = embed * embed_inv
    logits = 3.0 * dot_nn(centers, rows, EXACT)
    expos = jnp.exp(logits - jnp.max(logits, axis=0, keepdims=True))
    probs = expos / jnp.sum(expos, axis=0, keepdims=True)
    gate = jnp.sum(probs * member, axis=0, keepdims=True)
    return inv, rows, embed_inv, centers, probs, gate


def split_rows(row):
    first = row.astype(BF16).astype(F32)
    second = (row - first).astype(BF16).astype(F32)
    third = (row - first) - second
    shape = (8, row.shape[1])
    at = lax.broadcasted_iota(jnp.int32, shape, 0)
    parts = jnp.where(at == 0, first, jnp.where(at == 1, second, jnp.where(at == 2, third, 0.0)))
    return parts.astype(BF16)


def middle_kernel(seqs, parts, groups, *refs):
    refs = list(refs)
    take = lambda n: [refs.pop(0) for _ in range(n)]
    (tok_in,) = take(1)
    mixed = [take(parts) for _ in range(seqs)]
    gain_ref, route_ref, embed_ref, member_ref, place_in = take(5)
    hidden_ref, gate_ref, raw_ref, mixed_out, weight_out = take(5)
    packed = take(groups)
    mixed_ref, weight_ref, tok_ref, place_ref, in_sems, out_sems, late_sems = take(7)
    rows, feat = tok_ref.shape
    shard = rows // seqs
    channels = mixed[1][0].shape[0]
    cap = rows // groups
    pairs = []
    for m in range(parts):
        at = pl.ds(m * channels, channels)
        pairs.append((mixed[0][m].at[:, pl.ds(shard, feat)], weight_ref.at[at, :]))
        for s in range(seqs):
            pairs.append(
                (mixed[s][m].at[:, pl.ds(0, shard)], mixed_ref.at[at, pl.ds(s * shard, shard)])
            )
    first = start_all(pairs, in_sems)
    late = start_all([(tok_in, tok_ref), (place_in, place_ref)], late_sems)
    first()
    wait = start_all([(mixed_ref, mixed_out), (weight_ref, weight_out)], out_sems)
    attn = dot_tn(mixed_ref[...], weight_ref[...])
    late()
    hidden = tok_ref[...].astype(F32) + attn
    hidden_ref[...] = hidden
    cen, inv = centred(hidden)
    normed = cen * inv * gain_ref[...]
    raw = dot_nt(route_ref[...], normed, EXACT)
    raw_ref[...] = raw
    gate = gate_parts(raw, embed_ref[...], member_ref[...])[-1]
    gate_ref[...] = jnp.broadcast_to(gate, gate_ref.shape)
    low = normed.astype(BF16)
    scalars = split_rows(gate)
    for g in range(groups):
        place = place_ref[pl.ds(g * cap, cap), :]
        packed[g][pl.ds(0, cap), :] = dot_nn(place, low).astype(BF16)
        packed[g][pl.ds(cap, 8), :] = jnp.zeros((8, feat), BF16)
        packed[g][pl.ds(cap, 8), pl.ds(0, cap)] = dot_nt(scalars, place).astype(BF16)
    wait()


def count_digits(rows, devices):
    width = max(1, (256 // devices + 1).bit_length() - 1)
    digits = -(-rows.bit_length() // width)
    return width, digits, 128 if digits <= 6 else 64


def back_kernel(seqs, parts, groups, *refs):
    refs = list(refs)
    take = lambda n: [refs.pop(0) for _ in range(n)]
    packed = take(groups)
    cot_ref, hidden_ref, raw_ref, weight_ref = take(4)
    gain_ref, route_ref, embed_ref, member_ref, place_ref = take(5)
    grad_ref, low_ref, stats_ref = take(3)
    mixed_grad = take(parts)
    (slot_ref,) = take(1)
    rows = hidden_ref.shape[0]
    shard = rows // seqs
    cap = rows // groups
    channels = mixed_grad[0].shape[0]
    scalars = None
    for g in range(groups):
        slot_ref[pl.ds(g * cap, cap), :] = packed[g][pl.ds(0, cap), :]
        scalar = dot_nn(packed[g][pl.ds(cap, 8), pl.ds(0, cap)], place_ref[pl.ds(g * cap, cap), :])
        scalars = scalar if g == 0 else scalars + scalar
    at = lax.broadcasted_iota(jnp.int32, scalars.shape, 0)
    grad_gate = jnp.sum(jnp.where(at < 3, scalars, 0.0), axis=0, keepdims=True)
    cen, inv = centred(hidden_ref[...])
    unit = cen * inv
    gain = gain_ref[...]
    raw_inv, dirs, embed_inv, centers, probs, gate = gate_parts(
        raw_ref[...], embed_ref[...], member_ref[...]
    )
    grad_logits = (3.0 * grad_gate * gate) * (member_ref[...] - probs)
    grad_dirs = dot_tn(centers, grad_logits, EXACT)
    grad_centers = dot_nt(grad_logits, dirs, EXACT)
    grad_raw = raw_inv * (
        grad_dirs - dirs * jnp.sum(dirs * grad_dirs, axis=0, keepdims=True)
    )
    router = route_ref.shape[0]
    experts = embed_ref.shape[0]
    stats_ref[...] = jnp.zeros(stats_ref.shape, F32)
    stats_ref[pl.ds(router + 8, experts), pl.ds(0, router)] = embed_inv * (
        grad_centers - centers * jnp.sum(centers * grad_centers, axis=1, keepdims=True)
    )
    stats_ref[pl.ds(0, router), :] = dot_nn(grad_raw, unit * gain, EXACT)
    count = dot_nt(jnp.ones((8, rows), F32), member_ref[...], EXACT)[:1].astype(jnp.int32)
    width, digits, stride = count_digits(rows, 2 * parts * groups)
    for digit in range(digits):
        part = (count >> (width * digit)) & ((1 << width) - 1)
        stats_ref[pl.ds(router + 1, 1), pl.ds(stride * digit, experts)] = part.astype(F32)
    grad_normed = dot_tn(place_ref[...], slot_ref[...]) + dot_tn(grad_raw, route_ref[...], EXACT)
    stats_ref[pl.ds(router, 1), :] = jnp.sum(grad_normed * unit, axis=0, keepdims=True)
    grad_unit = grad_normed * gain
    grad_hidden = inv * (
        grad_unit
        - jnp.mean(grad_unit, axis=1, keepdims=True)
        - unit * jnp.mean(grad_unit * unit, axis=1, keepdims=True)
    )
    grad_hidden = cot_ref[...].astype(F32) + grad_hidden
    grad_ref[...] = grad_hidden
    low = grad_hidden.astype(BF16)
    low_ref[...] = low
    grad_mixed = dot_nt(weight_ref[...], low).astype(BF16)
    for m in range(parts):
        mixed_grad[m][...] = grad_mixed[m * channels : (m + 1) * channels]


def out_kernel(groups, cap, *refs):
    back = refs[:groups]
    hidden_ref, gate_ref, place_ref, out_ref = refs[groups:]
    mixture = None
    for g in range(groups):
        rows = back[g][pl.ds(back[g].shape[0] - cap, cap), :]
        part = dot_tn(place_ref[pl.ds(g * cap, cap), :], rows)
        mixture = part if g == 0 else mixture + part
    out_ref[...] = hidden_ref[...] + gate_ref[...].T[:, :1] * mixture


def tail_kernel(parts, s, core_ref, *refs):
    refs = list(refs)
    take = lambda n: [refs.pop(0) for _ in range(n)]
    grads = take(parts)
    (weight,) = take(1)
    mine = take(parts - 1)
    theirs, tok_in, gain_ref, hidden_in = take(4)
    out_ref, grad_ref, weight_ref, tok_ref, hidden_grad_ref, sems = refs[-6:]
    shard = tok_ref.shape[0]
    core = core_ref[0]
    rows = weight.shape[0]
    half = rows // 2
    pairs = [(grads[m], grad_ref.at[pl.ds(m * rows, rows), :]) for m in range(parts)]
    pairs.append((weight, weight_ref.at[pl.ds(0, rows), :]))
    for m in range(1, parts):
        near = pl.multiple_of(m * rows + core * half, 16)
        away = pl.multiple_of(m * rows + (1 - core) * half, 16)
        pairs.append((mine[m - 1], weight_ref.at[pl.ds(near, half), :]))
        pairs.append((theirs.at[pl.ds((m - 1) * half, half), :], weight_ref.at[pl.ds(away, half), :]))
    near_tok = start_all([(tok_in.at[pl.ds(s * shard, shard), :], tok_ref)], sems.at[pl.ds(0, 1)])
    pairs.append((hidden_in.at[pl.ds(s * shard, shard), :], hidden_grad_ref))
    wait = start_all(pairs, sems.at[pl.ds(1, len(pairs))])
    near_tok()
    cen, inv = centred(tok_ref[...].astype(F32))
    unit = cen * inv
    wait()
    grad_normed = dot_tn(grad_ref[...], weight_ref[...])
    grad_unit = grad_normed * gain_ref[...]
    out_ref[...] = hidden_grad_ref[...] + inv * (
        grad_unit
        - jnp.mean(grad_unit, axis=1, keepdims=True)
        - unit * jnp.mean(grad_unit * unit, axis=1, keepdims=True)
    )


def gelu_pair(x):
    z = jnp.abs(x) * (0.5**0.5)
    t = 1.0 / (1.0 + ERFC_SLOPE * z)
    poly = jnp.full_like(t, ERFC[-1])
    for value in ERFC[-2::-1]:
        poly = poly * t + value
    bell = jnp.exp2(x * x * (-0.5 * LOG2E))
    tail = (0.5 * bell) * (t * poly)
    cdf = jnp.where(x < 0.0, tail, 1.0 - tail)
    return x * cdf, cdf + x * (bell * 0.3989422804014327)


def expert_kernel(count, steps, *refs):
    refs = list(refs)
    take = lambda n: [refs.pop(0) for _ in range(n)]
    packed, cot = take(count), take(count)
    ups, downs = take(2), take(2)
    cap = cot[0].shape[0]
    returned, grads = [], []
    for i in range(count):
        (ref,) = take(1)
        if ref.shape[0] == cap:
            returned.append(ref)
            grads += take(1)
        else:
            grads.append(ref.at[pl.ds(0, cap + 8), :])
            returned.append(ref.at[pl.ds(cap + 8, cap), :])
    rows_ref, gr_ref = take(2)
    acts, gups = take(2), take(2)
    ret_acc, grad_acc = take(2)
    step = pl.program_id(0)

    def eye():
        shape = (cap, cap)
        return lax.broadcasted_iota(jnp.int32, shape, 0) == lax.broadcasted_iota(jnp.int32, shape, 1)

    @pl.when(step == 0)
    def _():
        for i in range(count):
            part = pl.ds(i * cap, cap)
            rows_ref[part, :] = packed[i][pl.ds(0, cap), :]
            scalars = packed[i][pl.ds(cap, 8), pl.ds(0, cap)].astype(F32)
            at = lax.broadcasted_iota(jnp.int32, scalars.shape, 0)
            row = jnp.sum(jnp.where(at < 3, scalars, 0.0), axis=0, keepdims=True)
            gate = jnp.sum(jnp.where(eye(), row, 0.0), axis=1, keepdims=True)
            gr_ref[part, :] = (gate * cot[i][...].astype(F32)).astype(BF16)

    rows, grad_rows = rows_ref[...], gr_ref[...]
    ret = None
    for h in range(2):
        up_w, down_w = ups[h][...], downs[h][...]
        act, slope = gelu_pair(dot_nn(rows, up_w))
        act = act.astype(BF16)
        gup = (dot_nn(grad_rows, down_w) * slope).astype(BF16)
        acts[h][...] = act
        gups[h][...] = gup
        ret_part = dot_nt(act, down_w)
        grad_part = dot_nt(gup, up_w)
        ret = ret_part if h == 0 else ret + ret_part
        grad = grad_part if h == 0 else grad + grad_part

    @pl.when(step == 0)
    def _():
        ret_acc[...] = ret
        grad_acc[...] = grad

    @pl.when(step > 0)
    def _():
        ret_acc[...] += ret
        grad_acc[...] += grad

    @pl.when(step == steps - 1)
    def _():
        for i in range(count):
            part = pl.ds(i * cap, cap)
            low = ret_acc[part, :].astype(BF16)
            returned[i][...] = low
            product = jnp.sum(low.astype(F32) * cot[i][...].astype(F32), axis=1, keepdims=True)
            row = jnp.sum(jnp.where(eye(), product, 0.0), axis=0, keepdims=True)
            grads[i][pl.ds(0, cap), :] = grad_acc[part, :].astype(BF16)
            grads[i][pl.ds(cap, 8), :] = jnp.zeros((8, grads[i].shape[1]), BF16)
            grads[i][pl.ds(cap, 8), pl.ds(0, cap)] = split_rows(row)


def expert(packed, cot, cap, up_own, up_other, down_own, down_other, joined=()):
    count = len(cot)
    feat, units = up_own.shape
    width = 512 if units % 512 == 0 else units
    steps = units // width
    rows = count * cap

    def same(size, at=0):
        return pl.BlockSpec((size, feat), lambda j: (at, 0))

    weight = pl.BlockSpec((feat, width), lambda j: (0, j))
    wide = pl.BlockSpec((rows, width), lambda j: (0, j))
    sizes = []
    for i in range(count):
        sizes += [2 * cap + 8] if i in joined else [cap, cap + 8]
    outs = pl.pallas_call(
        functools.partial(expert_kernel, count, steps),
        grid=(steps,),
        in_specs=[same(cap + 8, at) for _, at in packed]
        + [same(cap, at) for _, at in cot]
        + [weight] * 4,
        out_specs=[same(size) for size in sizes] + [same(rows)] * 2 + [wide] * 4,
        out_shape=[SDS((size, feat), BF16) for size in sizes]
        + [pltpu.HBM((rows, feat), BF16)] * 2
        + [pltpu.HBM((rows, units), BF16)] * 4,
        scratch_shapes=[VMEM((rows, feat), F32)] * 2,
        compiler_params=pltpu.CompilerParams(
            vmem_limit_bytes=24 << 20, dimension_semantics=("arbitrary",)
        ),
        cost_estimate=cost(
            16 * rows * feat * units, 8 * feat * units + 16 * rows * units, 4 * rows * units
        ),
    )(
        *[a for a, _ in packed],
        *[in_hbm(a) for a, _ in cot],
        *[in_hbm(w) for w in (up_own, up_other, down_own, down_other)],
    )
    back, grads = [], []
    at = 0
    for i in range(count):
        back.append(outs[at])
        if i not in joined:
            at += 1
        grads.append(outs[at])
        at += 1
    return back, grads, outs[at], outs[at + 1], outs[at + 2 : at + 4], outs[at + 4 :]


def expert_grad_kernel(halves, me_ref, *refs):
    refs = list(refs)
    take = lambda n: [refs.pop(0) for _ in range(n)]
    lefts = [take(halves) for _ in range(2)]
    wides = [[take(2) for _ in range(halves)] for _ in range(2)]
    own_ref, other_ref = take(2)
    turned = take(2)
    size = lefts[0][0].shape[0]

    @pl.when(pl.program_id(0) == 0)
    def _():
        for which in range(2):
            for i in range(halves):
                turned[which][:, pl.ds(i * size, size)] = lefts[which][i][...].T

    for which in range(2):
        for h, ref in enumerate((own_ref, other_ref)):
            full = jnp.concatenate([wides[which][i][h][...] for i in range(halves)], axis=0)
            ref[which, 0] = dot_nn(turned[which][...], full).astype(ref.dtype)


def expert_grad(me, rows, grad_rows, gups, acts, tensor_size):
    halves = len(rows)
    size, feat = rows[0].shape
    units = gups[0][0].shape[1]
    width = units // tensor_size
    same = pl.BlockSpec((size, feat), lambda j, me: (0, 0))
    part = pl.BlockSpec((size, width), lambda j, me: (0, me[0] ^ j))
    block = pl.BlockSpec((2, 1, feat, width), lambda j, me: (0, j, 0, 0))
    shape = (2, tensor_size, feat, width)
    wides = [a for pairs in (gups, acts) for pair in pairs for a in pair]
    return pl.pallas_call(
        functools.partial(expert_grad_kernel, halves),
        grid_spec=pltpu.PrefetchScalarGridSpec(
            num_scalar_prefetch=1,
            grid=(tensor_size,),
            in_specs=[same] * (2 * halves) + [part] * (4 * halves),
            out_specs=[block, block],
            scratch_shapes=[VMEM((feat, halves * size), BF16)] * 2,
        ),
        out_shape=[pltpu.HBM(shape, BF16), pltpu.HBM(shape, BF16)],
        compiler_params=pltpu.CompilerParams(
            vmem_limit_bytes=24 << 20, dimension_semantics=("arbitrary",)
        ),
        cost_estimate=cost(8 * halves * size * feat * units, 24 << 20),
    )(me.reshape(1), *[in_hbm(a) for a in (*rows, *grad_rows, *wides)])


def pair_kernel(*refs):
    for i in range(2):
        for j in range(2):
            own, recv = refs[4 * i + 2 * j : 4 * i + 2 * j + 2]
            refs[8 + i][j] = (own[0, 0].astype(F32) + recv[0, 0].astype(F32)).astype(BF16)


def first_pairs(own, recv, picks):
    feat, width = own.shape[2:]
    block = (1, 1, feat, width)
    args = []
    for which in range(2):
        for m in picks[which]:
            args += [Far(own, block, (which, m)), Here(recv, block, (which, m))]
    return call(pair_kernel, [SDS((2, feat, width), BF16)] * 2, args, 4 * feat * width)


def out_grad_kernel(core_ref, mixed_ref, low_ref, keep_ref, send_ref, full_ref):
    core = core_ref[0]
    parts, half, _ = keep_ref.shape
    full_ref[...] = dot_nn(mixed_ref[...], low_ref[...])
    for m in range(parts):
        near = pl.multiple_of((2 * m + core) * half, half)
        away = pl.multiple_of((2 * m + 1 - core) * half, half)
        keep_ref[m] = full_ref[pl.ds(near, half), :]
        send_ref[m] = full_ref[pl.ds(away, half), :].astype(BF16)


def qkv_grad_kernel(seqs, parts, core_ref, *refs):
    grads = [refs[s * parts : (s + 1) * parts] for s in range(seqs)]
    normed = refs[seqs * parts : seqs * parts + seqs]
    w_in, keep_ref, send_ref, norm1_ref = refs[seqs * parts + seqs :][:4]
    full_ref, grad_ref, normed_ref, w_ref, sems = refs[seqs * parts + seqs + 4 :]
    send_ref, extra_ref = send_ref.at[pl.ds(0, keep_ref.shape[0]), :], send_ref
    core = core_ref[0]
    shard = grads[0][0].shape[1]
    half = keep_ref.shape[0]
    pairs = []
    for s in range(seqs):
        for b in range(parts):
            pairs.append((grads[s][b], grad_ref.at[s, :, pl.ds(b * shard, shard)]))
        pairs.append((normed[s], normed_ref.at[s]))
    pairs.append((w_in, w_ref))
    start_all(pairs, sems)()
    total = dot_nn(grad_ref[0], normed_ref[0])
    for s in range(1, seqs):
        total += dot_nn(grad_ref[s], normed_ref[s])
    full_ref[...] = total
    norm1 = jnp.sum(total * w_ref[...].astype(F32), axis=0, keepdims=True)
    norm1_ref[...] = norm1
    terms = jnp.concatenate([split_rows(norm1), split_rows(jnp.zeros_like(norm1))], axis=0)
    extra_ref[pl.ds(keep_ref.shape[0], 16), :] = terms
    keep_ref[...] = full_ref[pl.ds(pl.multiple_of(core * half, half), half), :]
    send_ref[...] = full_ref[pl.ds(pl.multiple_of((1 - core) * half, half), half), :].astype(BF16)


def program(tensor_size, expert_size):
    chips = expert_size // 2
    bits = chips.bit_length() - 1

    def over_tensor(values, mask):
        return lax.ppermute(values, "tensor", [(i, i ^ mask) for i in range(tensor_size)])

    def over_core(values):
        return lax.ppermute(values, "expert", [(i, i ^ 1) for i in range(expert_size)])

    def over_chip(values, mask):
        return lax.ppermute(values, "expert", [(i, i ^ (2 * mask)) for i in range(expert_size)])

    def from_tensor(blocks):
        return [blocks[0]] + [over_tensor(blocks[m], m) for m in range(1, tensor_size)]

    def gather_first(block):
        if tensor_size != 4:
            return from_tensor([block] * tensor_size)
        half = block.shape[0] // 2
        one, two = over_tensor(block, 1), over_tensor(block, 2)
        low, high = over_tensor(one[:half], 2), over_tensor(two[half:], 1)
        return [block, one, two, (low, high)]

    def swap_chips(blocks):
        if chips <= 4:
            return [blocks[0]] + [over_chip(blocks[m], m) for m in range(1, chips)]
        chip = lax.axis_index("expert") // 2
        order = chip ^ jnp.arange(chips)
        groups = [[2 * i + core for i in range(chips)] for core in range(2)]
        moved = lax.all_to_all(
            jnp.stack(blocks)[order],
            "expert",
            split_axis=0,
            concat_axis=0,
            tiled=True,
            axis_index_groups=groups,
        )[order]
        return [moved[m] for m in range(chips)]

    if chips == 4:
        masks = (1, 3)
    else:
        masks = tuple(1 << bit for bit in range(bits))

    def chip_bit(level):
        chip = lax.axis_index("expert") // 2
        if chips == 4:
            return ((chip ^ (chip >> 1)) & 1) if level == 0 else (chip >> 1) & 1
        return (chip >> level) & 1

    def halves(values, bit):
        half = values.shape[0] // 2
        low, high = values[:half], values[half:]
        return jnp.where(bit == 0, low, high), jnp.where(bit == 0, high, low)

    def joined(mine, theirs, bit):
        return jnp.concatenate(
            [jnp.where(bit == 0, mine, theirs), jnp.where(bit == 0, theirs, mine)], axis=0
        )

    def body(
        tokens,
        out_grad,
        masked,
        route,
        norm1_gain,
        query_key_value_weight,
        output_weight,
        norm2_gain,
        route_weight,
        expert_embed,
        up_weight,
        down_weight,
    ):
        seqs, shard, feat = tokens.shape
        rows_here = seqs * shard
        experts, router = expert_embed.shape
        cap = rows_here // experts
        channels = query_key_value_weight.shape[2]
        units = up_weight.shape[2]
        parts = tensor_size
        me = lax.axis_index("tensor")
        place_index = lax.axis_index("expert")
        chip, core = place_index // 2, place_index % 2
        gain1 = norm1_gain.reshape(1, feat)
        gain2 = norm2_gain.reshape(1, feat)

        w_rows = query_key_value_weight.transpose(0, 2, 1).reshape(3 * channels, feat)
        half_rows = 3 * channels // 2
        w_half = lax.dynamic_slice_in_dim(w_rows, core * half_rows, half_rows, axis=0)
        gathered = [gather_first(tokens[0])]
        for s in range(1, seqs):
            gathered.append(from_tensor([tie(tokens[s], gathered[-1])] * parts))

        picks = route.reshape(rows_here)
        expert_ids = jnp.arange(experts, dtype=jnp.int32)
        member = (picks[:, None] == expert_ids[None, :]).astype(jnp.int32)
        earlier = jnp.cumsum(member, axis=0) - member
        slot_ids = jnp.sum(earlier * member, axis=1)
        target = (picks ^ chip) * cap + slot_ids
        target = jnp.where(slot_ids < cap, target, -1)
        slot_range = jnp.arange(experts * cap, dtype=jnp.int32)
        placing = (slot_range[:, None] == target[None, :]).astype(BF16)
        member_t = (expert_ids[:, None] == picks[None, :]).astype(F32)
        cotangent = out_grad.reshape(rows_here, feat) * masked.reshape(rows_here, 1).astype(BF16)
        sent_cotangent = dot_nn(placing, cotangent).astype(BF16)
        if experts == 4:
            cot_one = over_chip(sent_cotangent[cap : 3 * cap], 1)
            cot_held = jnp.concatenate([sent_cotangent[3 * cap :], cot_one[cap:]], axis=0)
            slot_cotangent = [(sent_cotangent, 0), (cot_one, 0)]
        else:
            slot_cotangent = [
                (block, 0)
                for block in swap_chips(
                    [sent_cotangent[g * cap : (g + 1) * cap] for g in range(experts)]
                )
            ]

        normed, qkv, lse, mixed = [], [], [], []
        up_other, down_other = over_core(up_weight[0]), over_core(down_weight[0])
        for s in range(seqs):
            if s == 0:
                gathered[0] = tie(
                    gathered[0], sent_cotangent, member_t, w_half, up_other, down_other
                )
            if s == 1:
                gathered[s] = tie(gathered[s], slot_cotangent[1][0], lse[0])
                if experts == 4:
                    cot_two = over_chip(tie(cot_held, lse[0]), 3)
                    slot_cotangent += [(cot_two, 0), (cot_two, 1)]
            rider = (output_weight,) if s == 0 else ()
            n, q, l, blocks = attend(gathered[s], gain1, w_rows, *rider)
            normed.append(n)
            qkv.append(q)
            lse.append(l)
            mixed.append(from_tensor(blocks if s == 0 else tie(blocks, mixed[0][1:])))

        flat_tokens = tokens.reshape(rows_here, feat)
        route_t = route_weight.T
        ready = tie(mixed, [block for block, _ in slot_cotangent[1:]])
        copies = parts * (seqs + 1)
        hidden, gate, raw, mixed_all, out_weight_all, *packed = call(
            functools.partial(middle_kernel, seqs, parts, experts),
            [
                Far(SDS((rows_here, feat), F32)),
                Far(SDS((8, rows_here), F32)),
                Far(SDS((router, rows_here), F32)),
                Loose(SDS((feat, rows_here), BF16)),
                Loose(SDS((feat, feat), BF16)),
            ]
            + [SDS((cap + 8, feat), BF16)] * experts,
            [Free(flat_tokens), *[Free(b) for blocks in ready for b in blocks]]
            + [gain2, route_t, expert_embed, member_t, Free(in_hbm(placing))],
            4 * rows_here * feat * feat,
            scratch=[
                VMEM((feat, rows_here), BF16),
                VMEM((feat, feat), BF16),
                VMEM((rows_here, feat), BF16),
                VMEM((rows_here, rows_here), BF16),
                pltpu.SemaphoreType.DMA((copies,)),
                pltpu.SemaphoreType.DMA((2,)),
                pltpu.SemaphoreType.DMA((2,)),
            ],
        )

        half = experts // 2
        expert_weights = (up_weight[0], up_other, down_weight[0], down_other)
        w_held = tie(w_half, packed)
        w_near = [over_tensor(w_held, m) for m in range(1, parts - 1)]
        if experts == 4:
            one = over_chip(packed[1], 1)
            held = tie(packed[2:], one)
            two, three = over_chip(held[0], 2), over_chip(held[1], 3)
            slot_rows = [(packed[0], 0), (one, 0)]
            low_half = expert(slot_rows[:2], slot_cotangent[:2], cap, *expert_weights, joined=(1,))
            near = over_chip(low_half[1][1], 1)
            three, two, w_near = tie((three, two, w_near), low_half[1])
            w_far = over_tensor(tie(w_half, w_near), parts - 1)
            high_half = expert([(three, 0), (two, 0)], slot_cotangent[2:], cap, *expert_weights)
        else:
            slot_rows = [(block, 0) for block in swap_chips(packed)]
            low_half = expert(slot_rows[:half], slot_cotangent[:half], cap, *expert_weights)
            high_half = expert(slot_rows[half:], slot_cotangent[half:], cap, *expert_weights)
            w_far = over_tensor(tie(w_half, w_near), parts - 1)
            near = ()
        results = [low_half, high_half]
        rows = [r[2] for r in results]
        grad_rows = [r[3] for r in results]
        acts = [r[4] for r in results]
        gups = [r[5] for r in results]
        w_mine = [*w_near, w_far]
        rows, near = tie((rows, near), w_far)
        grad_own, grad_send = expert_grad(me, rows, grad_rows, gups, acts, parts)
        if experts == 4:
            back_grad = [
                low_half[1][0],
                near,
                over_chip(high_half[1][1], 2),
                over_chip(high_half[1][0], 3),
            ]
        else:
            back_grad = swap_chips(low_half[1] + high_half[1])
        back_grad, grad_send, w_mine = tie((back_grad, grad_send, w_mine), grad_send)
        grad_recv = over_core(grad_send)
        w_theirs = over_core(jnp.concatenate(w_mine, axis=0))

        outs = call(
            functools.partial(back_kernel, seqs, parts, experts),
            [
                Far(SDS((rows_here, feat), F32)),
                Far(SDS((rows_here, feat), BF16)),
                SDS((router + 8 + -(-experts // 8) * 8, feat), F32),
            ]
            + [SDS((channels, rows_here), BF16)] * parts,
            [*back_grad, Far(cotangent), Far(hidden), Far(raw), Far(out_weight_all)]
            + [gain2, route_t, expert_embed, member_t, Far(placing)],
            4 * rows_here * feat * feat,
            scratch=[VMEM((rows_here, feat), BF16)],
        )
        grad_hidden, grad_low, stats = outs[:3]
        grad_mixed = from_tensor(outs[3:])
        up_own, down_own = grad_own[0], grad_own[1]
        up_recv, down_recv = grad_recv[0], grad_recv[1]
        up_pair, down_pair = first_pairs(grad_own, grad_recv, ((1, parts - 1), (2, parts - 1)))

        out_half = channels // 2
        out_keep, out_send = call(
            out_grad_kernel,
            [SDS((parts, out_half, feat), F32), SDS((parts, out_half, feat), BF16)],
            [Far(mixed_all), Far(tie(grad_low, up_pair, down_pair))],
            2 * rows_here * feat * feat,
            [VMEM((feat, feat), F32)],
            scalar=core,
        )
        out_keep = out_keep + over_core(out_send).astype(F32)
        stat_high = lax.reduce_precision(stats, 8, 7)
        stat_low = lax.reduce_precision(stats - stat_high, 8, 7)
        stat_terms = jnp.concatenate([stat_high, stat_low], axis=0).astype(BF16)
        out_ride = [
            jnp.concatenate([out_keep[m].astype(BF16), stat_terms], axis=0) for m in range(1, parts)
        ]

        if experts == 4:
            two, three = tie((high_half[0][1], high_half[0][0]), out_send)
            back = [low_half[0][0], near, over_chip(two, 2), over_chip(three, 3)]
        else:
            back = swap_chips(low_half[0] + high_half[0])

        if parts == 4:
            up_got = over_tensor(tie(up_pair, grad_mixed), 1)
            down_got = over_tensor(tie(down_pair, grad_mixed), 2)
        else:
            up_got, down_got = (), ()

        def second(own, recv, got, mask):
            return (own[mask].astype(F32) + recv[mask].astype(F32) + got[1].astype(F32)).astype(BF16)

        def final(own, recv, got, last):
            total = own[0].astype(F32) + recv[0].astype(F32)
            return (total + got[0].astype(F32) + last.astype(F32))[None]

        def slow_scatter(own, recv):
            total = own[0].astype(F32) + recv[0].astype(F32)
            for m in range(1, parts):
                part = own[m].astype(F32) + recv[m].astype(F32)
                total = total + over_tensor(part.astype(BF16), m).astype(F32)
            return total[None]

        grads = []
        came = tie(grad_mixed, out_send, w_theirs)
        for s in range(seqs):
            if s == 1:
                came = tie(came, grads[0])
            grads.append(
                attend_back(qkv[s], lse[s], came, s, cover=COVER if s == 0 else LAST_COVER)
            )
            if s == 0:
                out_held = tie(out_ride, grads[0], back)
                out_got = [over_tensor(out_held[m - 1], m) for m in range(1, parts)]
        split = 3 * channels // 2
        qkv_keep, qkv_send, norm1_grad = call(
            functools.partial(qkv_grad_kernel, seqs, parts),
            [SDS((split, feat), F32), SDS((split + 16, feat), BF16), SDS((1, feat), F32)],
            [Free(b) for blocks in tie(grads, up_got, down_got) for b in blocks]
            + [Free(in_hbm(n)) for n in normed]
            + [Free(w_rows)],
            2 * seqs * parts * shard * 3 * channels * feat,
            [
                VMEM((3 * channels, feat), F32),
                VMEM((seqs, 3 * channels, parts * shard), BF16),
                VMEM((seqs, parts * shard, feat), BF16),
                VMEM((3 * channels, feat), BF16),
                pltpu.SemaphoreType.DMA((seqs * parts + seqs + 1,)),
            ],
            scalar=core,
            cover=0,
        )
        out_half = out_keep.shape[1]
        out_part = sum((got[:out_half].astype(F32) for got in out_got), out_keep[0])
        size = stats.shape[0]

        def both_terms(terms):
            return terms[:size].astype(F32) + terms[size:].astype(F32)

        terms = [both_terms(t) for t in [stat_terms] + [got[out_half:] for got in out_got]]
        while len(terms) > 1:
            terms = [terms[i] + terms[i + 1] for i in range(0, len(terms), 2)]
        stats = terms[0] + over_core(terms[0])

        grad_blocks = [from_tensor(tie(grads[0], out_got, up_got, down_got))]
        qkv_recv = over_core(qkv_send)
        def tail(s, *after):
            before = [Free(input_grads[-1])] if s > 0 else []
            (input_part,) = call(
                functools.partial(tail_kernel, parts, s),
                [Far(SDS((rows_here, feat), F32), (shard, feat), s)],
                [*map(Free, tie(grad_blocks[s], *after)), Free(w_rows)]
                + [Free(in_hbm(w)) for w in (*w_mine, w_theirs)]
                + [Free(flat_tokens), gain1]
                + [Free(grad_hidden), *before],
                2 * shard * feat * 3 * channels * parts,
                [
                    VMEM((parts * 3 * channels, shard), BF16),
                    VMEM((parts * 3 * channels, feat), BF16),
                    VMEM((shard, feat), BF16),
                    VMEM((shard, feat), F32),
                    pltpu.SemaphoreType.DMA((3 * parts + 1,)),
                ],
                scalar=core,
                aliases={2 * parts + 5: 0} if s > 0 else None,
            )
            return input_part

        qkv_keep = qkv_keep + qkv_recv[:split].astype(F32)
        norm1_grad = norm1_grad + jnp.sum(qkv_recv[split : split + 3].astype(F32), axis=0, keepdims=True)
        stats = stats + jnp.pad(norm1_grad, ((router + 2, size - router - 3), (0, 0)))
        values = jnp.concatenate([qkv_keep, out_part, stats], axis=0)
        values = jnp.pad(values, ((0, -values.shape[0] % (8 << bits)), (0, 0)))
        input_grads = []
        up_last = down_last = ()
        for level, mask in enumerate(masks):
            keep, send = halves(values, chip_bit(level))
            send = send.astype(BF16)
            came = over_chip(send, mask)
            if level == 0:
                (result,) = call(
                    functools.partial(out_kernel, experts, cap),
                    [Far(SDS((rows_here, feat), F32))],
                    [Far(b) for b in tie(back, send)]
                    + [Far(hidden), Far(gate), Far(placing)],
                    2 * rows_here * rows_here * feat,
                    cover=0,
                )
                came = tie(came, result)
            if level == 1:
                grad_blocks.append(from_tensor(tie(grads[1], grad_blocks[0], send)))
                input_grads.append(tail(0, send))
                came = tie(came, input_grads[0])
            values = keep + came.astype(F32)
        summed = values.astype(BF16)
        if parts == 4:
            held = tie((up_got, down_got), summed)
            up_held = second(up_own, up_recv, held[0], 2)
            down_held = second(down_own, down_recv, held[1], 1)
            up_last = over_tensor(up_held, 2)
            down_last = over_tensor(down_held, 1)
            input_grads.append(tail(1, up_held, down_held, summed))
            up_last, down_last = tie((up_last, down_last), input_grads[1])
        else:
            input_grads.append(tail(1, summed))
        for level in reversed(range(bits)):
            summed = joined(summed, over_chip(summed, masks[level]), chip_bit(level))
        other_half = over_core(summed[: split + out_half])
        stats = summed[split + out_half :].astype(F32)
        query_key_value_gradient = (
            joined(summed[:split], other_half[:split], core)
            .reshape(3, channels, feat)
            .transpose(0, 2, 1)
            .astype(F32)
        )
        ends = slice(split, split + out_half)
        out_proj_grad = joined(summed[ends], other_half[ends], core).astype(F32)
        if parts == 4:
            up_weight_grad = final(up_own, up_recv, up_got, up_last)
            down_weight_grad = final(down_own, down_recv, down_got, down_last)
        else:
            up_weight_grad = slow_scatter(up_own, up_recv)
            down_weight_grad = slow_scatter(down_own, down_recv)

        beside = [(up_weight_grad, down_weight_grad), (query_key_value_gradient, out_proj_grad)]
        norm1_grad = stats[router + 2 : router + 3]
        mask = 1
        while mask < tensor_size:
            came = over_tensor(norm1_grad, mask)
            if beside:
                came = tie(came, beside.pop(0))
            norm1_grad = norm1_grad + came
            mask *= 2
        route_grad = stats[:router].T
        norm2_grad = stats[router]
        norm1_grad = norm1_grad[0] / norm1_gain
        width, digits, stride = count_digits(rows_here, 2 * parts * experts)
        loads = sum(
            stats[router + 1, stride * i : stride * i + experts] * float(1 << (width * i))
            for i in range(digits)
        )
        embed_grad = stats[router + 8 : router + 8 + experts, :router]

        return (
            result.reshape(seqs, shard, feat),
            input_grads[-1].reshape(seqs, shard, feat),
            loads,
            norm1_grad,
            query_key_value_gradient,
            out_proj_grad,
            norm2_grad,
            route_grad,
            embed_grad,
            up_weight_grad,
            down_weight_grad,
        )

    return body


def solution(mesh):
    return jax.shard_map(
        program(mesh.shape["tensor"], mesh.shape["expert"]),
        mesh=mesh,
        in_specs=(
            P("expert", "tensor", None),
            P("expert", "tensor", None),
            P("expert", "tensor"),
            P("expert", "tensor", None),
            P(),
            P(None, None, "tensor"),
            P("tensor", None),
            P(),
            P(),
            P(),
            P("expert", None, None),
            P("expert", None, None),
        ),
        out_specs=(
            P("expert", "tensor", None),
            P("expert", "tensor", None),
            P(),
            P(),
            P(None, None, "tensor"),
            P("tensor", None),
            P(),
            P(),
            P(),
            P("expert", None, "tensor"),
            P("expert", None, "tensor"),
        ),
        check_vma=False,
    )
```

```python
import functools

import jax
import jax.numpy as jnp
from jax import lax
from jax.experimental import pallas as pl
from jax.experimental.pallas import tpu as pltpu
from jax.sharding import PartitionSpec as P

HEAD = 64
F32 = jnp.float32
BF16 = jnp.bfloat16
LOG2E = 1.4426950408889634
SCALE = HEAD**-0.5
EXACT = lax.Precision.HIGHEST
SDS = jax.ShapeDtypeStruct
VMEM = pltpu.VMEM
COVER = 4
LAST_COVER = 0

ERFC_SLOPE = 0.44
ERFC = (
    0.248227568,
    0.248777028,
    0.217859919,
    0.214130365,
    -0.0172025688,
    0.293641958,
    -0.276276279,
    0.0708421859,
)


def dot_nn(left, right, precision=None):
    return jnp.dot(left, right, preferred_element_type=F32, precision=precision)


def dot_nt(left, right, precision=None):
    return lax.dot_general(
        left, right, (((1,), (1,)), ((), ())), preferred_element_type=F32, precision=precision
    )


def dot_tn(left, right, precision=None):
    return lax.dot_general(
        left, right, (((0,), (0,)), ((), ())), preferred_element_type=F32, precision=precision
    )


class Far:
    def __init__(self, value, block=None, at=0):
        self.value = value
        self.block = value.shape if block is None else block
        self.at = at


class Here(Far):
    pass


class Loose(Far):
    pass


class Free(Far):
    pass


def start_all(pairs, sems):
    copies = [pltpu.make_async_copy(a, b, sems.at[i]) for i, (a, b) in enumerate(pairs)]
    for copy in copies:
        copy.start()

    def wait():
        for copy in copies:
            copy.wait()

    return wait


def plain(value):
    return value.value if isinstance(value, Far) else value


def in_hbm(value):
    return pltpu.with_memory_space_constraint(value, pltpu.HBM)


def cost(flops, size, transcendentals=0, cover=COVER):
    return pl.CostEstimate(
        flops=flops * cover, bytes_accessed=size * cover, transcendentals=transcendentals * cover
    )


def call(kernel, outs, args, flops, scratch=(), limit=24, transcendentals=0, scalar=None, cover=COVER, aliases=None):
    whole = pl.BlockSpec(memory_space=VMEM)

    def spec(arg):
        if isinstance(arg, Loose):
            return pl.BlockSpec(memory_space=pl.ANY)
        if not isinstance(arg, Far):
            return whole
        if isinstance(arg, (Loose, Free)):
            return pl.BlockSpec(memory_space=pl.ANY)
        where = arg.at if isinstance(arg.at, tuple) else (arg.at,)
        where += (0,) * (arg.value.ndim - len(where))
        return pl.BlockSpec(
            arg.block, lambda i: where, pipeline_mode=pl.Buffered(buffer_count=1)
        )

    specs = [spec(a) for a in args]
    out_specs = [spec(o) for o in outs]
    size = sum(a.size * a.dtype.itemsize for a in map(plain, args))
    size += sum(o.size * o.dtype.itemsize for o in map(plain, outs))
    args = [
        a.value if isinstance(a, (Free, Here)) else in_hbm(a.value) if isinstance(a, Far) else a for a in args
    ]
    outs = [pltpu.HBM(o.value.shape, o.value.dtype) if isinstance(o, Far) else o for o in outs]
    if scalar is not None:
        specs = [pl.BlockSpec(memory_space=pltpu.SMEM)] + specs
        args = [scalar.reshape(1)] + args
    return pl.pallas_call(
        kernel,
        grid=(1,),
        out_shape=list(outs),
        in_specs=specs,
        out_specs=out_specs,
        scratch_shapes=list(scratch),
        input_output_aliases=aliases or {},
        compiler_params=pltpu.CompilerParams(vmem_limit_bytes=limit << 20),
        cost_estimate=cost(flops, size, transcendentals, cover),
    )(*args)


def centred(x):
    cen = x - jnp.mean(x, axis=1, keepdims=True)
    return cen, lax.rsqrt(jnp.mean(cen * cen, axis=1, keepdims=True) + 1e-05)


def tie(values, *after):
    return lax.optimization_barrier((values, after))[0]


def attend_kernel(parts, pieces, channels, riding, *refs):
    tok = refs[: sum(pieces)]
    refs = refs[sum(pieces) :]
    gain_ref, w_ref = refs[:2]
    rider = refs[2 : 2 + riding]
    refs = refs[2 + riding :]
    normed_out, qkv_out, lse_ref = refs[:3]
    mixed = refs[3 : 3 + parts]
    normed_ref, qkv_ref, sems = refs[3 + parts :]
    shard = tok[0].shape[0]
    for ref in rider:
        for b in range(parts):
            mixed[b][:, pl.ds(shard, ref.shape[1])] = ref[...]
    at = 0
    for ref in tok:
        size = ref.shape[0]
        cen, inv = centred(ref[...].astype(F32))
        rows = (cen * inv * gain_ref[...]).astype(BF16)
        normed_ref[pl.ds(at, size), :] = rows
        qkv_ref[:, pl.ds(at, size)] = dot_nt(w_ref[...], rows).astype(BF16)
        at += size
    copies = [
        pltpu.make_async_copy(normed_ref, normed_out, sems.at[0]),
        pltpu.make_async_copy(qkv_ref, qkv_out, sems.at[1]),
    ]
    for copy in copies:
        copy.start()
    size = 128
    chunks = parts * shard // size

    def head(h, carry):
        off = pl.multiple_of(h * HEAD, HEAD)
        key = qkv_ref[pl.ds(channels + off, HEAD), :].T
        value_t = qkv_ref[pl.ds(2 * channels + off, HEAD), :]
        for b in range(parts):
            query_t = qkv_ref[pl.ds(off, HEAD), pl.ds(b * shard, shard)]
            scores = [dot_nn(key[i * size : (i + 1) * size], query_t) for i in range(chunks)]
            top = None
            for score in scores:
                part = jnp.max(score.reshape(size // 8, 8, shard), axis=0)
                top = part if top is None else jnp.maximum(top, part)
            top = jnp.max(top, axis=0, keepdims=True) * (SCALE * LOG2E)
            total, out = None, None
            for i, score in enumerate(scores):
                expos = jnp.exp2(score * (SCALE * LOG2E) - top)
                part = jnp.sum(expos.reshape(size // 8, 8, shard), axis=0)
                term = dot_nn(value_t[:, i * size : (i + 1) * size], expos.astype(BF16))
                total = part if i == 0 else total + part
                out = term if i == 0 else out + term
            total = jnp.sum(total, axis=0, keepdims=True)
            mixed[b][pl.ds(off, HEAD), pl.ds(0, shard)] = (out * (1.0 / total)).astype(BF16)
            lse_ref[pl.ds(h, 1), pl.ds(b * shard, shard)] = top + jnp.log2(total)
        return carry

    lax.fori_loop(0, channels // HEAD, head, 0)
    for copy in copies:
        copy.wait()


def attend(tok, gain, w_rows, *rider):
    parts = len(tok)
    shard, feat = tok[0].shape
    length = parts * shard
    channels = w_rows.shape[0] // 3
    pieces = [len(block) if isinstance(block, tuple) else 1 for block in tok]
    tok = jax.tree.leaves(tok)
    outs = call(
        functools.partial(attend_kernel, parts, pieces, channels, len(rider)),
        [
            Loose(SDS((length, feat), BF16)),
            Loose(SDS((3 * channels, length), BF16)),
            Far(SDS((8, length), F32)),
        ]
        + [SDS((channels, shard + sum(r.shape[1] for r in rider)), BF16)] * parts,
        [*tok, gain, Far(w_rows), *[Far(r) for r in rider]],
        2 * length * feat * 3 * channels + 4 * length * length * channels,
        scratch=[
            VMEM((length, feat), BF16),
            VMEM((3 * channels, length), BF16),
            pltpu.SemaphoreType.DMA((2,)),
        ],
        transcendentals=length * length * channels // HEAD,
    )
    return outs[0], outs[1], outs[2], outs[3:]


def attend_back_kernel(parts, channels, at, *refs):
    qkv_ref, lse_ref = refs[:2]
    shard = qkv_ref.shape[1] // parts
    grad = [ref.at[:, pl.ds(at * shard, shard)] for ref in refs[2 : 2 + parts]]
    refs = refs[2 + parts :]
    outs = refs[:parts]
    key_acc, value_acc = refs[parts:]

    def head(h, carry):
        off = pl.multiple_of(h * HEAD, HEAD)
        key_t = qkv_ref[pl.ds(channels + off, HEAD), :]
        key = key_t.T
        value = qkv_ref[pl.ds(2 * channels + off, HEAD), :].T
        for b in range(parts):
            query_t = qkv_ref[pl.ds(off, HEAD), pl.ds(b * shard, shard)]
            grad_t = grad[b][pl.ds(off, HEAD), :]
            scores = dot_nn(key, query_t)
            probs = jnp.exp2(
                scores * (SCALE * LOG2E) - lse_ref[pl.ds(h, 1), pl.ds(b * shard, shard)]
            )
            grad_probs = dot_nn(value, grad_t)
            inner = jnp.sum(probs * grad_probs, axis=0, keepdims=True)
            grad_scores = (probs * (grad_probs - inner)).astype(BF16)
            value_part = dot_nt(grad_t, probs.astype(BF16))
            key_part = dot_nt(query_t, grad_scores)
            outs[b][pl.ds(off, HEAD), :] = (dot_nn(key_t, grad_scores) * SCALE).astype(BF16)
            if b == 0:
                key_acc[...] = key_part
                value_acc[...] = value_part
            else:
                key_acc[...] += key_part
                value_acc[...] += value_part
        for b in range(parts):
            cols = pl.ds(b * shard, shard)
            outs[b][pl.ds(channels + off, HEAD), :] = (key_acc[:, cols] * SCALE).astype(BF16)
            outs[b][pl.ds(2 * channels + off, HEAD), :] = value_acc[:, cols].astype(BF16)
        return carry

    lax.fori_loop(0, channels // HEAD, head, 0)


def attend_back(qkv, lse, grad, at, cover):
    parts = len(grad)
    channels = grad[0].shape[0]
    length = qkv.shape[1]
    shard = length // parts
    return call(
        functools.partial(attend_back_kernel, parts, channels, at),
        [SDS((3 * channels, shard), BF16)] * parts,
        [Far(qkv), Far(lse), *[Far(g) for g in grad]],
        10 * length * length * channels,
        scratch=[VMEM((HEAD, length), F32)] * 2,
        transcendentals=length * length * channels // HEAD,
        cover=cover,
    )


def gate_parts(raw, embed, member):
    inv = lax.rsqrt(jnp.sum(raw * raw, axis=0, keepdims=True) + 1e-06)
    rows = raw * inv
    embed_inv = lax.rsqrt(jnp.sum(embed * embed, axis=1, keepdims=True) + 1e-06)
    centers = embed * embed_inv
    logits = 3.0 * dot_nn(centers, rows, EXACT)
    expos = jnp.exp(logits - jnp.max(logits, axis=0, keepdims=True))
    probs = expos / jnp.sum(expos, axis=0, keepdims=True)
    gate = jnp.sum(probs * member, axis=0, keepdims=True)
    return inv, rows, embed_inv, centers, probs, gate


def split_rows(row):
    first = row.astype(BF16).astype(F32)
    second = (row - first).astype(BF16).astype(F32)
    third = (row - first) - second
    shape = (8, row.shape[1])
    at = lax.broadcasted_iota(jnp.int32, shape, 0)
    parts = jnp.where(at == 0, first, jnp.where(at == 1, second, jnp.where(at == 2, third, 0.0)))
    return parts.astype(BF16)


def middle_kernel(seqs, parts, groups, *refs):
    refs = list(refs)
    take = lambda n: [refs.pop(0) for _ in range(n)]
    (tok_in,) = take(1)
    mixed = [take(parts) for _ in range(seqs)]
    gain_ref, route_ref, embed_ref, member_ref, place_in = take(5)
    hidden_ref, gate_ref, raw_ref, mixed_out, weight_out = take(5)
    packed = take(groups)
    mixed_ref, weight_ref, tok_ref, place_ref, in_sems, out_sems, late_sems = take(7)
    rows, feat = tok_ref.shape
    shard = rows // seqs
    channels = mixed[1][0].shape[0]
    cap = rows // groups
    pairs = []
    for m in range(parts):
        at = pl.ds(m * channels, channels)
        pairs.append((mixed[0][m].at[:, pl.ds(shard, feat)], weight_ref.at[at, :]))
        for s in range(seqs):
            pairs.append(
                (mixed[s][m].at[:, pl.ds(0, shard)], mixed_ref.at[at, pl.ds(s * shard, shard)])
            )
    first = start_all(pairs, in_sems)
    late = start_all([(tok_in, tok_ref), (place_in, place_ref)], late_sems)
    first()
    wait = start_all([(mixed_ref, mixed_out), (weight_ref, weight_out)], out_sems)
    attn = dot_tn(mixed_ref[...], weight_ref[...])
    late()
    hidden = tok_ref[...].astype(F32) + attn
    hidden_ref[...] = hidden
    cen, inv = centred(hidden)
    normed = cen * inv * gain_ref[...]
    raw = dot_nt(route_ref[...], normed, EXACT)
    raw_ref[...] = raw
    gate = gate_parts(raw, embed_ref[...], member_ref[...])[-1]
    gate_ref[...] = jnp.broadcast_to(gate, gate_ref.shape)
    low = normed.astype(BF16)
    scalars = split_rows(gate)
    for g in range(groups):
        place = place_ref[pl.ds(g * cap, cap), :]
        packed[g][pl.ds(0, cap), :] = dot_nn(place, low).astype(BF16)
        packed[g][pl.ds(cap, 8), :] = jnp.zeros((8, feat), BF16)
        packed[g][pl.ds(cap, 8), pl.ds(0, cap)] = dot_nt(scalars, place).astype(BF16)
    wait()


def count_digits(rows, devices):
    width = max(1, (256 // devices + 1).bit_length() - 1)
    digits = -(-rows.bit_length() // width)
    return width, digits, 128 if digits <= 6 else 64


def back_kernel(seqs, parts, groups, *refs):
    refs = list(refs)
    take = lambda n: [refs.pop(0) for _ in range(n)]
    packed = take(groups)
    cot_ref, hidden_ref, raw_ref, weight_ref = take(4)
    gain_ref, route_ref, embed_ref, member_ref, place_ref = take(5)
    grad_ref, low_ref, stats_ref = take(3)
    mixed_grad = take(parts)
    (slot_ref,) = take(1)
    rows = hidden_ref.shape[0]
    shard = rows // seqs
    cap = rows // groups
    channels = mixed_grad[0].shape[0]
    scalars = None
    for g in range(groups):
        slot_ref[pl.ds(g * cap, cap), :] = packed[g][pl.ds(0, cap), :]
        scalar = dot_nn(packed[g][pl.ds(cap, 8), pl.ds(0, cap)], place_ref[pl.ds(g * cap, cap), :])
        scalars = scalar if g == 0 else scalars + scalar
    at = lax.broadcasted_iota(jnp.int32, scalars.shape, 0)
    grad_gate = jnp.sum(jnp.where(at < 3, scalars, 0.0), axis=0, keepdims=True)
    cen, inv = centred(hidden_ref[...])
    unit = cen * inv
    gain = gain_ref[...]
    raw_inv, dirs, embed_inv, centers, probs, gate = gate_parts(
        raw_ref[...], embed_ref[...], member_ref[...]
    )
    grad_logits = (3.0 * grad_gate * gate) * (member_ref[...] - probs)
    grad_dirs = dot_tn(centers, grad_logits, EXACT)
    grad_centers = dot_nt(grad_logits, dirs, EXACT)
    grad_raw = raw_inv * (
        grad_dirs - dirs * jnp.sum(dirs * grad_dirs, axis=0, keepdims=True)
    )
    router = route_ref.shape[0]
    experts = embed_ref.shape[0]
    stats_ref[...] = jnp.zeros(stats_ref.shape, F32)
    stats_ref[pl.ds(router + 8, experts), pl.ds(0, router)] = embed_inv * (
        grad_centers - centers * jnp.sum(centers * grad_centers, axis=1, keepdims=True)
    )
    stats_ref[pl.ds(0, router), :] = dot_nn(grad_raw, unit * gain, EXACT)
    count = dot_nt(jnp.ones((8, rows), F32), member_ref[...], EXACT)[:1].astype(jnp.int32)
    width, digits, stride = count_digits(rows, 2 * parts * groups)
    for digit in range(digits):
        part = (count >> (width * digit)) & ((1 << width) - 1)
        stats_ref[pl.ds(router + 1, 1), pl.ds(stride * digit, experts)] = part.astype(F32)
    grad_normed = dot_tn(place_ref[...], slot_ref[...]) + dot_tn(grad_raw, route_ref[...], EXACT)
    stats_ref[pl.ds(router, 1), :] = jnp.sum(grad_normed * unit, axis=0, keepdims=True)
    grad_unit = grad_normed * gain
    grad_hidden = inv * (
        grad_unit
        - jnp.mean(grad_unit, axis=1, keepdims=True)
        - unit * jnp.mean(grad_unit * unit, axis=1, keepdims=True)
    )
    grad_hidden = cot_ref[...].astype(F32) + grad_hidden
    grad_ref[...] = grad_hidden
    low = grad_hidden.astype(BF16)
    low_ref[...] = low
    grad_mixed = dot_nt(weight_ref[...], low).astype(BF16)
    for m in range(parts):
        mixed_grad[m][...] = grad_mixed[m * channels : (m + 1) * channels]


def out_kernel(groups, cap, *refs):
    back = refs[:groups]
    hidden_ref, gate_ref, place_ref, out_ref = refs[groups:]
    mixture = None
    for g in range(groups):
        rows = back[g][pl.ds(back[g].shape[0] - cap, cap), :]
        part = dot_tn(place_ref[pl.ds(g * cap, cap), :], rows)
        mixture = part if g == 0 else mixture + part
    out_ref[...] = hidden_ref[...] + gate_ref[...].T[:, :1] * mixture


def tail_kernel(parts, s, core_ref, *refs):
    refs = list(refs)
    take = lambda n: [refs.pop(0) for _ in range(n)]
    grads = take(parts)
    (weight,) = take(1)
    mine = take(parts - 1)
    theirs, tok_in, gain_ref, hidden_in = take(4)
    out_ref, grad_ref, weight_ref, tok_ref, hidden_grad_ref, sems = refs[-6:]
    shard = tok_ref.shape[0]
    core = core_ref[0]
    rows = weight.shape[0]
    half = rows // 2
    pairs = [(grads[m], grad_ref.at[pl.ds(m * rows, rows), :]) for m in range(parts)]
    pairs.append((weight, weight_ref.at[pl.ds(0, rows), :]))
    for m in range(1, parts):
        near = pl.multiple_of(m * rows + core * half, 16)
        away = pl.multiple_of(m * rows + (1 - core) * half, 16)
        pairs.append((mine[m - 1], weight_ref.at[pl.ds(near, half), :]))
        pairs.append((theirs.at[pl.ds((m - 1) * half, half), :], weight_ref.at[pl.ds(away, half), :]))
    near_tok = start_all([(tok_in.at[pl.ds(s * shard, shard), :], tok_ref)], sems.at[pl.ds(0, 1)])
    pairs.append((hidden_in.at[pl.ds(s * shard, shard), :], hidden_grad_ref))
    wait = start_all(pairs, sems.at[pl.ds(1, len(pairs))])
    near_tok()
    cen, inv = centred(tok_ref[...].astype(F32))
    unit = cen * inv
    wait()
    grad_normed = dot_tn(grad_ref[...], weight_ref[...])
    grad_unit = grad_normed * gain_ref[...]
    out_ref[...] = hidden_grad_ref[...] + inv * (
        grad_unit
        - jnp.mean(grad_unit, axis=1, keepdims=True)
        - unit * jnp.mean(grad_unit * unit, axis=1, keepdims=True)
    )


def gelu_pair(x):
    z = jnp.abs(x) * (0.5**0.5)
    t = 1.0 / (1.0 + ERFC_SLOPE * z)
    poly = jnp.full_like(t, ERFC[-1])
    for value in ERFC[-2::-1]:
        poly = poly * t + value
    bell = jnp.exp2(x * x * (-0.5 * LOG2E))
    tail = (0.5 * bell) * (t * poly)
    cdf = jnp.where(x < 0.0, tail, 1.0 - tail)
    return x * cdf, cdf + x * (bell * 0.3989422804014327)


def expert_kernel(count, steps, *refs):
    refs = list(refs)
    take = lambda n: [refs.pop(0) for _ in range(n)]
    packed, cot = take(count), take(count)
    ups, downs = take(2), take(2)
    cap = cot[0].shape[0]
    returned, grads = [], []
    for i in range(count):
        (ref,) = take(1)
        if ref.shape[0] == cap:
            returned.append(ref)
            grads += take(1)
        else:
            grads.append(ref.at[pl.ds(0, cap + 8), :])
            returned.append(ref.at[pl.ds(cap + 8, cap), :])
    rows_ref, gr_ref = take(2)
    acts, gups = take(2), take(2)
    ret_acc, grad_acc = take(2)
    step = pl.program_id(0)

    def eye():
        shape = (cap, cap)
        return lax.broadcasted_iota(jnp.int32, shape, 0) == lax.broadcasted_iota(jnp.int32, shape, 1)

    @pl.when(step == 0)
    def _():
        for i in range(count):
            part = pl.ds(i * cap, cap)
            rows_ref[part, :] = packed[i][pl.ds(0, cap), :]
            scalars = packed[i][pl.ds(cap, 8), pl.ds(0, cap)].astype(F32)
            at = lax.broadcasted_iota(jnp.int32, scalars.shape, 0)
            row = jnp.sum(jnp.where(at < 3, scalars, 0.0), axis=0, keepdims=True)
            gate = jnp.sum(jnp.where(eye(), row, 0.0), axis=1, keepdims=True)
            gr_ref[part, :] = (gate * cot[i][...].astype(F32)).astype(BF16)

    rows, grad_rows = rows_ref[...], gr_ref[...]
    ret = None
    for h in range(2):
        up_w, down_w = ups[h][...], downs[h][...]
        act, slope = gelu_pair(dot_nn(rows, up_w))
        act = act.astype(BF16)
        gup = (dot_nn(grad_rows, down_w) * slope).astype(BF16)
        acts[h][...] = act
        gups[h][...] = gup
        ret_part = dot_nt(act, down_w)
        grad_part = dot_nt(gup, up_w)
        ret = ret_part if h == 0 else ret + ret_part
        grad = grad_part if h == 0 else grad + grad_part

    @pl.when(step == 0)
    def _():
        ret_acc[...] = ret
        grad_acc[...] = grad

    @pl.when(step > 0)
    def _():
        ret_acc[...] += ret
        grad_acc[...] += grad

    @pl.when(step == steps - 1)
    def _():
        for i in range(count):
            part = pl.ds(i * cap, cap)
            low = ret_acc[part, :].astype(BF16)
            returned[i][...] = low
            product = jnp.sum(low.astype(F32) * cot[i][...].astype(F32), axis=1, keepdims=True)
            row = jnp.sum(jnp.where(eye(), product, 0.0), axis=0, keepdims=True)
            grads[i][pl.ds(0, cap), :] = grad_acc[part, :].astype(BF16)
            grads[i][pl.ds(cap, 8), :] = jnp.zeros((8, grads[i].shape[1]), BF16)
            grads[i][pl.ds(cap, 8), pl.ds(0, cap)] = split_rows(row)


def expert(packed, cot, cap, up_own, up_other, down_own, down_other, joined=()):
    count = len(cot)
    feat, units = up_own.shape
    width = 512 if units % 512 == 0 else units
    steps = units // width
    rows = count * cap

    def same(size, at=0):
        return pl.BlockSpec((size, feat), lambda j: (at, 0))

    weight = pl.BlockSpec((feat, width), lambda j: (0, j))
    wide = pl.BlockSpec((rows, width), lambda j: (0, j))
    sizes = []
    for i in range(count):
        sizes += [2 * cap + 8] if i in joined else [cap, cap + 8]
    outs = pl.pallas_call(
        functools.partial(expert_kernel, count, steps),
        grid=(steps,),
        in_specs=[same(cap + 8, at) for _, at in packed]
        + [same(cap, at) for _, at in cot]
        + [weight] * 4,
        out_specs=[same(size) for size in sizes] + [same(rows)] * 2 + [wide] * 4,
        out_shape=[SDS((size, feat), BF16) for size in sizes]
        + [pltpu.HBM((rows, feat), BF16)] * 2
        + [pltpu.HBM((rows, units), BF16)] * 4,
        scratch_shapes=[VMEM((rows, feat), F32)] * 2,
        compiler_params=pltpu.CompilerParams(
            vmem_limit_bytes=24 << 20, dimension_semantics=("arbitrary",)
        ),
        cost_estimate=cost(
            16 * rows * feat * units, 8 * feat * units + 16 * rows * units, 4 * rows * units
        ),
    )(
        *[a for a, _ in packed],
        *[in_hbm(a) for a, _ in cot],
        *[in_hbm(w) for w in (up_own, up_other, down_own, down_other)],
    )
    back, grads = [], []
    at = 0
    for i in range(count):
        back.append(outs[at])
        if i not in joined:
            at += 1
        grads.append(outs[at])
        at += 1
    return back, grads, outs[at], outs[at + 1], outs[at + 2 : at + 4], outs[at + 4 :]


def expert_grad_kernel(halves, me_ref, *refs):
    refs = list(refs)
    take = lambda n: [refs.pop(0) for _ in range(n)]
    lefts = [take(halves) for _ in range(2)]
    wides = [[take(2) for _ in range(halves)] for _ in range(2)]
    own_ref, other_ref = take(2)
    turned = take(2)
    size = lefts[0][0].shape[0]

    @pl.when(pl.program_id(0) == 0)
    def _():
        for which in range(2):
            for i in range(halves):
                turned[which][:, pl.ds(i * size, size)] = lefts[which][i][...].T

    for which in range(2):
        for h, ref in enumerate((own_ref, other_ref)):
            full = jnp.concatenate([wides[which][i][h][...] for i in range(halves)], axis=0)
            ref[which, 0] = dot_nn(turned[which][...], full).astype(ref.dtype)


def expert_grad(me, rows, grad_rows, gups, acts, tensor_size):
    halves = len(rows)
    size, feat = rows[0].shape
    units = gups[0][0].shape[1]
    width = units // tensor_size
    same = pl.BlockSpec((size, feat), lambda j, me: (0, 0))
    part = pl.BlockSpec((size, width), lambda j, me: (0, me[0] ^ j))
    block = pl.BlockSpec((2, 1, feat, width), lambda j, me: (0, j, 0, 0))
    shape = (2, tensor_size, feat, width)
    wides = [a for pairs in (gups, acts) for pair in pairs for a in pair]
    return pl.pallas_call(
        functools.partial(expert_grad_kernel, halves),
        grid_spec=pltpu.PrefetchScalarGridSpec(
            num_scalar_prefetch=1,
            grid=(tensor_size,),
            in_specs=[same] * (2 * halves) + [part] * (4 * halves),
            out_specs=[block, block],
            scratch_shapes=[VMEM((feat, halves * size), BF16)] * 2,
        ),
        out_shape=[pltpu.HBM(shape, BF16), pltpu.HBM(shape, BF16)],
        compiler_params=pltpu.CompilerParams(
            vmem_limit_bytes=24 << 20, dimension_semantics=("arbitrary",)
        ),
        cost_estimate=cost(8 * halves * size * feat * units, 24 << 20),
    )(me.reshape(1), *[in_hbm(a) for a in (*rows, *grad_rows, *wides)])


def pair_kernel(*refs):
    for i in range(2):
        for j in range(2):
            own, recv = refs[4 * i + 2 * j : 4 * i + 2 * j + 2]
            refs[8 + i][j] = (own[0, 0].astype(F32) + recv[0, 0].astype(F32)).astype(BF16)


def first_pairs(own, recv, picks):
    feat, width = own.shape[2:]
    block = (1, 1, feat, width)
    args = []
    for which in range(2):
        for m in picks[which]:
            args += [Far(own, block, (which, m)), Here(recv, block, (which, m))]
    return call(pair_kernel, [SDS((2, feat, width), BF16)] * 2, args, 4 * feat * width)


def out_grad_kernel(core_ref, mixed_ref, low_ref, keep_ref, send_ref, full_ref):
    core = core_ref[0]
    parts, half, _ = keep_ref.shape
    full_ref[...] = dot_nn(mixed_ref[...], low_ref[...])
    for m in range(parts):
        near = pl.multiple_of((2 * m + core) * half, half)
        away = pl.multiple_of((2 * m + 1 - core) * half, half)
        keep_ref[m] = full_ref[pl.ds(near, half), :]
        send_ref[m] = full_ref[pl.ds(away, half), :].astype(BF16)


def qkv_grad_kernel(seqs, parts, core_ref, *refs):
    grads = [refs[s * parts : (s + 1) * parts] for s in range(seqs)]
    normed = refs[seqs * parts : seqs * parts + seqs]
    w_in, keep_ref, send_ref, norm1_ref = refs[seqs * parts + seqs :][:4]
    full_ref, grad_ref, normed_ref, w_ref, sems = refs[seqs * parts + seqs + 4 :]
    send_ref, extra_ref = send_ref.at[pl.ds(0, keep_ref.shape[0]), :], send_ref
    core = core_ref[0]
    shard = grads[0][0].shape[1]
    half = keep_ref.shape[0]
    pairs = []
    for s in range(seqs):
        for b in range(parts):
            pairs.append((grads[s][b], grad_ref.at[s, :, pl.ds(b * shard, shard)]))
        pairs.append((normed[s], normed_ref.at[s]))
    pairs.append((w_in, w_ref))
    start_all(pairs, sems)()
    total = dot_nn(grad_ref[0], normed_ref[0])
    for s in range(1, seqs):
        total += dot_nn(grad_ref[s], normed_ref[s])
    full_ref[...] = total
    norm1 = jnp.sum(total * w_ref[...].astype(F32), axis=0, keepdims=True)
    norm1_ref[...] = norm1
    terms = jnp.concatenate([split_rows(norm1), split_rows(jnp.zeros_like(norm1))], axis=0)
    extra_ref[pl.ds(keep_ref.shape[0], 16), :] = terms
    keep_ref[...] = full_ref[pl.ds(pl.multiple_of(core * half, half), half), :]
    send_ref[...] = full_ref[pl.ds(pl.multiple_of((1 - core) * half, half), half), :].astype(BF16)


def program(tensor_size, expert_size):
    chips = expert_size // 2
    bits = chips.bit_length() - 1

    def over_tensor(values, mask):
        return lax.ppermute(values, "tensor", [(i, i ^ mask) for i in range(tensor_size)])

    def over_core(values):
        return lax.ppermute(values, "expert", [(i, i ^ 1) for i in range(expert_size)])

    def over_chip(values, mask):
        return lax.ppermute(values, "expert", [(i, i ^ (2 * mask)) for i in range(expert_size)])

    def from_tensor(blocks):
        return [blocks[0]] + [over_tensor(blocks[m], m) for m in range(1, tensor_size)]

    def gather_first(block):
        if tensor_size != 4:
            return from_tensor([block] * tensor_size)
        half = block.shape[0] // 2
        one, two = over_tensor(block, 1), over_tensor(block, 2)
        low, high = over_tensor(one[:half], 2), over_tensor(two[half:], 1)
        return [block, one, two, (low, high)]

    def swap_chips(blocks):
        if chips <= 4:
            return [blocks[0]] + [over_chip(blocks[m], m) for m in range(1, chips)]
        chip = lax.axis_index("expert") // 2
        order = chip ^ jnp.arange(chips)
        groups = [[2 * i + core for i in range(chips)] for core in range(2)]
        moved = lax.all_to_all(
            jnp.stack(blocks)[order],
            "expert",
            split_axis=0,
            concat_axis=0,
            tiled=True,
            axis_index_groups=groups,
        )[order]
        return [moved[m] for m in range(chips)]

    if chips == 4:
        masks = (1, 3)
    else:
        masks = tuple(1 << bit for bit in range(bits))

    def chip_bit(level):
        chip = lax.axis_index("expert") // 2
        if chips == 4:
            return ((chip ^ (chip >> 1)) & 1) if level == 0 else (chip >> 1) & 1
        return (chip >> level) & 1

    def halves(values, bit):
        half = values.shape[0] // 2
        low, high = values[:half], values[half:]
        return jnp.where(bit == 0, low, high), jnp.where(bit == 0, high, low)

    def joined(mine, theirs, bit):
        return jnp.concatenate(
            [jnp.where(bit == 0, mine, theirs), jnp.where(bit == 0, theirs, mine)], axis=0
        )

    def body(
        tokens,
        out_grad,
        masked,
        route,
        norm1_gain,
        query_key_value_weight,
        output_weight,
        norm2_gain,
        route_weight,
        expert_embed,
        up_weight,
        down_weight,
    ):
        seqs, shard, feat = tokens.shape
        rows_here = seqs * shard
        experts, router = expert_embed.shape
        cap = rows_here // experts
        channels = query_key_value_weight.shape[2]
        units = up_weight.shape[2]
        parts = tensor_size
        me = lax.axis_index("tensor")
        place_index = lax.axis_index("expert")
        chip, core = place_index // 2, place_index % 2
        gain1 = norm1_gain.reshape(1, feat)
        gain2 = norm2_gain.reshape(1, feat)

        w_rows = query_key_value_weight.transpose(0, 2, 1).reshape(3 * channels, feat)
        half_rows = 3 * channels // 2
        w_half = lax.dynamic_slice_in_dim(w_rows, core * half_rows, half_rows, axis=0)
        gathered = [gather_first(tokens[0])]
        for s in range(1, seqs):
            gathered.append(from_tensor([tie(tokens[s], gathered[-1])] * parts))

        picks = route.reshape(rows_here)
        expert_ids = jnp.arange(experts, dtype=jnp.int32)
        member = (picks[:, None] == expert_ids[None, :]).astype(jnp.int32)
        earlier = jnp.cumsum(member, axis=0) - member
        slot_ids = jnp.sum(earlier * member, axis=1)
        target = (picks ^ chip) * cap + slot_ids
        target = jnp.where(slot_ids < cap, target, -1)
        slot_range = jnp.arange(experts * cap, dtype=jnp.int32)
        placing = (slot_range[:, None] == target[None, :]).astype(BF16)
        member_t = (expert_ids[:, None] == picks[None, :]).astype(F32)
        cotangent = out_grad.reshape(rows_here, feat) * masked.reshape(rows_here, 1).astype(BF16)
        sent_cotangent = dot_nn(placing, cotangent).astype(BF16)
        if experts == 4:
            cot_one = over_chip(sent_cotangent[cap : 3 * cap], 1)
            cot_held = jnp.concatenate([sent_cotangent[3 * cap :], cot_one[cap:]], axis=0)
            slot_cotangent = [(sent_cotangent, 0), (cot_one, 0)]
        else:
            slot_cotangent = [
                (block, 0)
                for block in swap_chips(
                    [sent_cotangent[g * cap : (g + 1) * cap] for g in range(experts)]
                )
            ]

        normed, qkv, lse, mixed = [], [], [], []
        up_other, down_other = over_core(up_weight[0]), over_core(down_weight[0])
        for s in range(seqs):
            if s == 0:
                gathered[0] = tie(
                    gathered[0], sent_cotangent, member_t, w_half, up_other, down_other
                )
            if s == 1:
                if experts == 4:
                    cot_two = over_chip(cot_held, 3)
                    slot_cotangent += [(cot_two, 0), (cot_two, 1)]
                gathered[s] = tie(gathered[s], [block for block, _ in slot_cotangent[1:]], lse[0])
            rider = (output_weight,) if s == 0 else ()
            n, q, l, blocks = attend(gathered[s], gain1, w_rows, *rider)
            normed.append(n)
            qkv.append(q)
            lse.append(l)
            mixed.append(from_tensor(blocks if s == 0 else tie(blocks, mixed[0][1:])))

        flat_tokens = tokens.reshape(rows_here, feat)
        route_t = route_weight.T
        ready = tie(mixed, [block for block, _ in slot_cotangent[1:]])
        copies = parts * (seqs + 1)
        hidden, gate, raw, mixed_all, out_weight_all, *packed = call(
            functools.partial(middle_kernel, seqs, parts, experts),
            [
                Far(SDS((rows_here, feat), F32)),
                Far(SDS((8, rows_here), F32)),
                Far(SDS((router, rows_here), F32)),
                Loose(SDS((feat, rows_here), BF16)),
                Loose(SDS((feat, feat), BF16)),
            ]
            + [SDS((cap + 8, feat), BF16)] * experts,
            [Free(flat_tokens), *[Free(b) for blocks in ready for b in blocks]]
            + [gain2, route_t, expert_embed, member_t, Free(in_hbm(placing))],
            4 * rows_here * feat * feat,
            scratch=[
                VMEM((feat, rows_here), BF16),
                VMEM((feat, feat), BF16),
                VMEM((rows_here, feat), BF16),
                VMEM((rows_here, rows_here), BF16),
                pltpu.SemaphoreType.DMA((copies,)),
                pltpu.SemaphoreType.DMA((2,)),
                pltpu.SemaphoreType.DMA((2,)),
            ],
        )

        half = experts // 2
        expert_weights = (up_weight[0], up_other, down_weight[0], down_other)
        w_held = tie(w_half, packed)
        w_near = [over_tensor(w_held, m) for m in range(1, parts - 1)]
        if experts == 4:
            one = over_chip(packed[1], 1)
            held = tie(packed[2:], one)
            two, three = over_chip(held[0], 2), over_chip(held[1], 3)
            slot_rows = [(packed[0], 0), (one, 0)]
            low_half = expert(slot_rows[:2], slot_cotangent[:2], cap, *expert_weights, joined=(1,))
            near = over_chip(low_half[1][1], 1)
            three, two, w_near = tie((three, two, w_near), low_half[1])
            w_far = over_tensor(tie(w_half, w_near), parts - 1)
            high_half = expert([(three, 0), (two, 0)], slot_cotangent[2:], cap, *expert_weights)
        else:
            slot_rows = [(block, 0) for block in swap_chips(packed)]
            low_half = expert(slot_rows[:half], slot_cotangent[:half], cap, *expert_weights)
            high_half = expert(slot_rows[half:], slot_cotangent[half:], cap, *expert_weights)
            w_far = over_tensor(tie(w_half, w_near), parts - 1)
            near = ()
        results = [low_half, high_half]
        rows = [r[2] for r in results]
        grad_rows = [r[3] for r in results]
        acts = [r[4] for r in results]
        gups = [r[5] for r in results]
        w_mine = [*w_near, w_far]
        rows, near = tie((rows, near), w_far)
        grad_own, grad_send = expert_grad(me, rows, grad_rows, gups, acts, parts)
        if experts == 4:
            back_grad = [
                low_half[1][0],
                near,
                over_chip(high_half[1][1], 2),
                over_chip(high_half[1][0], 3),
            ]
        else:
            back_grad = swap_chips(low_half[1] + high_half[1])
        back_grad, grad_send, w_mine = tie((back_grad, grad_send, w_mine), grad_send)
        grad_recv = over_core(grad_send)
        w_theirs = over_core(jnp.concatenate(w_mine, axis=0))

        outs = call(
            functools.partial(back_kernel, seqs, parts, experts),
            [
                Far(SDS((rows_here, feat), F32)),
                Far(SDS((rows_here, feat), BF16)),
                SDS((router + 8 + -(-experts // 8) * 8, feat), F32),
            ]
            + [SDS((channels, rows_here), BF16)] * parts,
            [*back_grad, Far(cotangent), Far(hidden), Far(raw), Far(out_weight_all)]
            + [gain2, route_t, expert_embed, member_t, Far(placing)],
            4 * rows_here * feat * feat,
            scratch=[VMEM((rows_here, feat), BF16)],
        )
        grad_hidden, grad_low, stats = outs[:3]
        grad_mixed = from_tensor(outs[3:])
        up_own, down_own = grad_own[0], grad_own[1]
        up_recv, down_recv = grad_recv[0], grad_recv[1]
        up_pair, down_pair = first_pairs(grad_own, grad_recv, ((1, parts - 1), (2, parts - 1)))

        out_half = channels // 2
        out_keep, out_send = call(
            out_grad_kernel,
            [SDS((parts, out_half, feat), F32), SDS((parts, out_half, feat), BF16)],
            [Far(mixed_all), Far(tie(grad_low, up_pair, down_pair))],
            2 * rows_here * feat * feat,
            [VMEM((feat, feat), F32)],
            scalar=core,
        )
        out_keep = out_keep + over_core(out_send).astype(F32)
        stat_high = lax.reduce_precision(stats, 8, 7)
        stat_low = lax.reduce_precision(stats - stat_high, 8, 7)
        stat_terms = jnp.concatenate([stat_high, stat_low], axis=0).astype(BF16)
        out_ride = [
            jnp.concatenate([out_keep[m].astype(BF16), stat_terms], axis=0) for m in range(1, parts)
        ]

        if experts == 4:
            two, three = tie((high_half[0][1], high_half[0][0]), out_send)
            back = [low_half[0][0], near, over_chip(two, 2), over_chip(three, 3)]
        else:
            back = swap_chips(low_half[0] + high_half[0])

        if parts == 4:
            up_got = over_tensor(tie(up_pair, grad_mixed), 1)
            down_got = over_tensor(tie(down_pair, grad_mixed), 2)
        else:
            up_got, down_got = (), ()

        def second(own, recv, got, mask):
            return (own[mask].astype(F32) + recv[mask].astype(F32) + got[1].astype(F32)).astype(BF16)

        def final(own, recv, got, last):
            total = own[0].astype(F32) + recv[0].astype(F32)
            return (total + got[0].astype(F32) + last.astype(F32))[None]

        def slow_scatter(own, recv):
            total = own[0].astype(F32) + recv[0].astype(F32)
            for m in range(1, parts):
                part = own[m].astype(F32) + recv[m].astype(F32)
                total = total + over_tensor(part.astype(BF16), m).astype(F32)
            return total[None]

        grads = []
        came = tie(grad_mixed, out_send, w_theirs)
        for s in range(seqs):
            if s == 1:
                came = tie(came, grads[0])
            grads.append(
                attend_back(qkv[s], lse[s], came, s, cover=COVER if s == 0 else LAST_COVER)
            )
            if s == 0:
                out_held = tie(out_ride, grads[0], back)
                out_got = [over_tensor(out_held[m - 1], m) for m in range(1, parts)]
        split = 3 * channels // 2
        qkv_keep, qkv_send, norm1_grad = call(
            functools.partial(qkv_grad_kernel, seqs, parts),
            [SDS((split, feat), F32), SDS((split + 16, feat), BF16), SDS((1, feat), F32)],
            [Free(b) for blocks in tie(grads, up_got, down_got) for b in blocks]
            + [Free(in_hbm(n)) for n in normed]
            + [Free(w_rows)],
            2 * seqs * parts * shard * 3 * channels * feat,
            [
                VMEM((3 * channels, feat), F32),
                VMEM((seqs, 3 * channels, parts * shard), BF16),
                VMEM((seqs, parts * shard, feat), BF16),
                VMEM((3 * channels, feat), BF16),
                pltpu.SemaphoreType.DMA((seqs * parts + seqs + 1,)),
            ],
            scalar=core,
            cover=0,
        )
        out_half = out_keep.shape[1]
        out_part = sum((got[:out_half].astype(F32) for got in out_got), out_keep[0])
        size = stats.shape[0]

        def both_terms(terms):
            return terms[:size].astype(F32) + terms[size:].astype(F32)

        terms = [both_terms(t) for t in [stat_terms] + [got[out_half:] for got in out_got]]
        while len(terms) > 1:
            terms = [terms[i] + terms[i + 1] for i in range(0, len(terms), 2)]
        stats = terms[0] + over_core(terms[0])

        grad_blocks = [from_tensor(tie(grads[0], out_got, up_got, down_got))]
        qkv_recv = over_core(qkv_send)
        def tail(s, *after):
            before = [Free(input_grads[-1])] if s > 0 else []
            (input_part,) = call(
                functools.partial(tail_kernel, parts, s),
                [Far(SDS((rows_here, feat), F32), (shard, feat), s)],
                [*map(Free, tie(grad_blocks[s], *after)), Free(w_rows)]
                + [Free(in_hbm(w)) for w in (*w_mine, w_theirs)]
                + [Free(flat_tokens), gain1]
                + [Free(grad_hidden), *before],
                2 * shard * feat * 3 * channels * parts,
                [
                    VMEM((parts * 3 * channels, shard), BF16),
                    VMEM((parts * 3 * channels, feat), BF16),
                    VMEM((shard, feat), BF16),
                    VMEM((shard, feat), F32),
                    pltpu.SemaphoreType.DMA((3 * parts + 1,)),
                ],
                scalar=core,
                aliases={2 * parts + 5: 0} if s > 0 else None,
            )
            return input_part

        qkv_keep = qkv_keep + qkv_recv[:split].astype(F32)
        norm1_grad = norm1_grad + jnp.sum(qkv_recv[split : split + 3].astype(F32), axis=0, keepdims=True)
        stats = stats + jnp.pad(norm1_grad, ((router + 2, size - router - 3), (0, 0)))
        values = jnp.concatenate([qkv_keep, out_part, stats], axis=0)
        values = jnp.pad(values, ((0, -values.shape[0] % (8 << bits)), (0, 0)))
        input_grads = []
        up_last = down_last = ()
        for level, mask in enumerate(masks):
            keep, send = halves(values, chip_bit(level))
            send = send.astype(BF16)
            came = over_chip(send, mask)
            if level == 0:
                (result,) = call(
                    functools.partial(out_kernel, experts, cap),
                    [Far(SDS((rows_here, feat), F32))],
                    [Far(b) for b in tie(back, send)]
                    + [Far(hidden), Far(gate), Far(placing)],
                    2 * rows_here * rows_here * feat,
                    cover=0,
                )
                came = tie(came, result)
            if level == 1:
                grad_blocks.append(from_tensor(tie(grads[1], grad_blocks[0], send)))
                input_grads.append(tail(0, send))
                came = tie(came, input_grads[0])
            values = keep + came.astype(F32)
        summed = values.astype(BF16)
        if parts == 4:
            held = tie((up_got, down_got), summed)
            up_held = second(up_own, up_recv, held[0], 2)
            down_held = second(down_own, down_recv, held[1], 1)
            up_last = over_tensor(up_held, 2)
            down_last = over_tensor(down_held, 1)
            input_grads.append(tail(1, up_held, down_held, summed))
            up_last, down_last = tie((up_last, down_last), input_grads[1])
        else:
            input_grads.append(tail(1, summed))
        for level in reversed(range(bits)):
            summed = joined(summed, over_chip(summed, masks[level]), chip_bit(level))
        other_half = over_core(summed[: split + out_half])
        stats = summed[split + out_half :].astype(F32)
        query_key_value_gradient = (
            joined(summed[:split], other_half[:split], core)
            .reshape(3, channels, feat)
            .transpose(0, 2, 1)
            .astype(F32)
        )
        ends = slice(split, split + out_half)
        out_proj_grad = joined(summed[ends], other_half[ends], core).astype(F32)
        if parts == 4:
            up_weight_grad = final(up_own, up_recv, up_got, up_last)
            down_weight_grad = final(down_own, down_recv, down_got, down_last)
        else:
            up_weight_grad = slow_scatter(up_own, up_recv)
            down_weight_grad = slow_scatter(down_own, down_recv)

        beside = [(up_weight_grad, down_weight_grad), (query_key_value_gradient, out_proj_grad)]
        norm1_grad = stats[router + 2 : router + 3]
        mask = 1
        while mask < tensor_size:
            came = over_tensor(norm1_grad, mask)
            if beside:
                came = tie(came, beside.pop(0))
            norm1_grad = norm1_grad + came
            mask *= 2
        route_grad = stats[:router].T
        norm2_grad = stats[router]
        norm1_grad = norm1_grad[0] / norm1_gain
        width, digits, stride = count_digits(rows_here, 2 * parts * experts)
        loads = sum(
            stats[router + 1, stride * i : stride * i + experts] * float(1 << (width * i))
            for i in range(digits)
        )
        embed_grad = stats[router + 8 : router + 8 + experts, :router]

        return (
            result.reshape(seqs, shard, feat),
            input_grads[-1].reshape(seqs, shard, feat),
            loads,
            norm1_grad,
            query_key_value_gradient,
            out_proj_grad,
            norm2_grad,
            route_grad,
            embed_grad,
            up_weight_grad,
            down_weight_grad,
        )

    return body


def solution(mesh):
    return jax.shard_map(
        program(mesh.shape["tensor"], mesh.shape["expert"]),
        mesh=mesh,
        in_specs=(
            P("expert", "tensor", None),
            P("expert", "tensor", None),
            P("expert", "tensor"),
            P("expert", "tensor", None),
            P(),
            P(None, None, "tensor"),
            P("tensor", None),
            P(),
            P(),
            P(),
            P("expert", None, None),
            P("expert", None, None),
        ),
        out_specs=(
            P("expert", "tensor", None),
            P("expert", "tensor", None),
            P(),
            P(),
            P(None, None, "tensor"),
            P("tensor", None),
            P(),
            P(),
            P(),
            P("expert", None, "tensor"),
            P("expert", None, "tensor"),
        ),
        check_vma=False,
    )
```
